32 devices in a mesh: fsdp: 2 (over x), ctx: 4 (over y, core), tp: 4 (over z).
Axes of the slice: x: 2, y: 2, z: 4, core: 2. Of those that a mesh axis runs over, the one named last changes fastest.
Arguments:
- inputs: bfloat16 [16, 680, 1024], P('fsdp', 'ctx', 'tp'), may hold values from -6 to 6
- cotangent: bfloat16 [16, 680, 1024], P('fsdp', 'ctx', 'tp'), may hold values from -6 to 6
- labels: int32 [16], replicated, may hold values from 0 to 1000
- scale_ids: int32 [680], replicated, may hold values from 0 to 9, never falling along the last dimension, each value on 1 to 256 neighbouring positions
- head_flags: int32 [16], P('tp'), may hold values 0 or 1
- class_table: bfloat16 [1001, 1024], P(None, ('fsdp', 'ctx', 'tp')), may hold values from -6 to 6
- modulate_weight: bfloat16 [1024, 6, 1024], P(('fsdp', 'ctx'), None, 'tp'), may hold values from -0.1875 to 0.1875
- modulate_bias: bfloat16 [6, 16, 64], P(None, 'tp', ('fsdp', 'ctx')), may hold values from -3 to 3
- query_weight: bfloat16 [1024, 1024], P(('fsdp', 'ctx'), 'tp'), may hold values from -0.1875 to 0.1875
- key_weight: bfloat16 [1024, 1024], P(('fsdp', 'ctx'), 'tp'), may hold values from -0.1875 to 0.1875
- value_weight: bfloat16 [1024, 1024], P(('fsdp', 'ctx'), 'tp'), may hold values from -0.1875 to 0.1875
- query_bias: bfloat16 [16, 64], P('tp', ('fsdp', 'ctx')), may hold values from -3 to 3
- value_bias: bfloat16 [16, 64], P('tp', ('fsdp', 'ctx')), may hold values from -3 to 3
- query_gain: bfloat16 [16, 64], P('tp', ('fsdp', 'ctx')), may hold values from 0.69 to 2.27
- key_gain: bfloat16 [16, 64], P('tp', ('fsdp', 'ctx')), may hold values from 0.69 to 2.27
- output_weight: bfloat16 [1024, 1024], P('tp', ('fsdp', 'ctx')), may hold values from -1 to 1
- output_bias: bfloat16 [16, 64], P('tp', ('fsdp', 'ctx')), may hold values from -2 to 2
- up_weight: bfloat16 [1024, 4096], P(('fsdp', 'ctx'), 'tp'), may hold values from -0.1875 to 0.1875
- up_bias: bfloat16 [64, 64], P('tp', ('fsdp', 'ctx')), may hold values from -3 to 3
- down_weight: bfloat16 [4096, 1024], P('tp', ('fsdp', 'ctx')), may hold values from -0.09375 to 0.09375
- down_bias: bfloat16 [16, 64], P('tp', ('fsdp', 'ctx')), may hold values from -2 to 2
Outputs:
- block_out: bfloat16 [16, 680, 1024], P('fsdp', 'ctx', 'tp')
- inputs_grad: float32 [16, 680, 1024], P('fsdp', 'ctx', 'tp')
- class_table_grad: float32 [1001, 1024], P(None, ('fsdp', 'ctx', 'tp'))
- modulate_weight_grad: float32 [1024, 6, 1024], P(('fsdp', 'ctx'), None, 'tp')
- modulate_bias_grad: float32 [6, 16, 64], P(None, 'tp', ('fsdp', 'ctx'))
- query_weight_grad: float32 [1024, 1024], P(('fsdp', 'ctx'), 'tp')
- key_weight_grad: float32 [1024, 1024], P(('fsdp', 'ctx'), 'tp')
- value_weight_grad: float32 [1024, 1024], P(('fsdp', 'ctx'), 'tp')
- query_bias_grad: float32 [16, 64], P('tp', ('fsdp', 'ctx'))
- value_bias_grad: float32 [16, 64], P('tp', ('fsdp', 'ctx'))
- query_gain_grad: float32 [16, 64], P('tp', ('fsdp', 'ctx'))
- key_gain_grad: float32 [16, 64], P('tp', ('fsdp', 'ctx'))
- output_weight_grad: float32 [1024, 1024], P('tp', ('fsdp', 'ctx'))
- output_bias_grad: float32 [16, 64], P('tp', ('fsdp', 'ctx'))
- up_weight_grad: float32 [1024, 4096], P(('fsdp', 'ctx'), 'tp')
- up_bias_grad: float32 [64, 64], P('tp', ('fsdp', 'ctx'))
- down_weight_grad: float32 [4096, 1024], P('tp', ('fsdp', 'ctx'))
- down_bias_grad: float32 [16, 64], P('tp', ('fsdp', 'ctx'))
- clipped_query: float32 [1024, 1024], P(('fsdp', 'ctx'), 'tp')
- clipped_key: float32 [1024, 1024], P(('fsdp', 'ctx'), 'tp')
- clipped_query_bias: float32 [16, 64], P('tp', ('fsdp', 'ctx'))
The draws below stay inside these ranges and needn't reach their ends.
Inputs may be any that keep to these rules, and one draw needn't show every extreme that they name: scale_ids never fall along a pyramid; each of the 10 scales holds 1 to 256 consecutive tokens and one holds exactly 256.
All inputs are finite; a program needn't handle non-finite values. No bound on the sum of `head_flags` on one device may be relied on, other than what follows from the above.
Results may differ from the reference program's by a relative error of at most 0.019.
Values may be sent and summed in bfloat16 or wider, within the bound.
A program may use at most 192 MiB of HBM per device.

```python
import math
import jax
import jax.numpy as jnp
import numpy as np
from jax import lax

D = 1024
H = 16
HD = 64
FF = 4096
CLASSES = 1001
SEQ = 680
SCALES = 10
MOST = 256
IMAGES = 16


def head_levels(key):
    ranking = jax.random.permutation(jax.random.fold_in(key, 11), H)
    lowered = jax.random.randint(jax.random.fold_in(key, 12), (), 1, H)
    return jnp.where(ranking < lowered, 1.0, 1.73).astype(jnp.float32)


def gain_field(key, extra_seed):
    levels = head_levels(key)
    noise_key = jax.random.fold_in(key, extra_seed)
    spread = jnp.clip(0.12 * jax.random.normal(noise_key, (H, HD), jnp.float32), -0.3, 0.3)
    return (levels[:, None] * (1.0 + spread)).astype(jnp.bfloat16)


def draw_query_gain(key, part):
    return gain_field(key, 21)


def draw_key_gain(key, part):
    return gain_field(key, 22)


def set_ends(result, key, smallest, largest):
    longest = result.shape.index(max(result.shape))
    spots = []
    for shift in (0, 1):
        where = [jax.random.randint(jax.random.fold_in(key, axis), (), 0, length) for axis, length in enumerate(result.shape)]
        where[longest] = (where[longest] + shift) % result.shape[longest]
        spots.append(tuple(where))
    return result.at[spots[0]].set(smallest).at[spots[1]].set(largest)


def block_scale(rng, dims, cuts, low, top_value):
    loudness = 1.0
    for axis_at, blocks in cuts:
        heights = jax.random.uniform(jax.random.fold_in(jax.random.fold_in(rng, 6), axis_at), (blocks,), jnp.float32, low / len(cuts), top_value / len(cuts))
        loudness = loudness * jnp.repeat(jnp.exp(heights), dims[axis_at] // blocks).reshape((-1,) + (1,) * (len(dims) - 1 - axis_at))
    return loudness


def profile(count, total, bound, slope):
    portions = [(1 << 20) // math.isqrt(grade ** slope) + 1 for grade in range(2, count + 1)]
    spare, holding = total - bound - (count - 1), [1] * (count - 1)
    while spare > 0:
        candidates = [i for i in range(count - 1) if holding[i] < bound]
        pool, left = sum([portions[i] for i in candidates]), spare
        for i in candidates:
            more = min(bound - holding[i], max(1, left * portions[i] // pool), spare)
            holding[i] = holding[i] + more
            spare = spare - more
    return np.array([bound] + holding)


def uneven_parts(rng, count, total, limit, lean):
    if count == 2:
        one = jax.random.randint(rng, (), max(1, total - limit), min(limit, total - 1) + 1)
        return jnp.stack([one, total - one])
    lengths = jnp.asarray(profile(count, total, limit, lean), jnp.int32)
    couples = (count - 1) // 2
    source_of, receiver = lengths[1:1 + 2 * couples:2], lengths[2:2 + 2 * couples:2]
    slack = jnp.minimum(source_of - 1, limit - receiver)
    passed = jax.random.randint(jax.random.fold_in(rng, 1), (couples,), 0, 1 << 20) % (slack + 1)
    lengths = lengths.at[1:1 + 2 * couples:2].set(source_of - passed).at[2:2 + 2 * couples:2].set(receiver + passed)
    return lengths[jax.random.permutation(jax.random.fold_in(rng, 2), count)]


def bell_draw(own_key, dims, deviation, limit, split=(), held_as=jnp.bfloat16):
    result = jax.random.normal(own_key, dims, jnp.float32) * deviation
    if len(split) > 0:
        result = block_scale(own_key, dims, split, -0.22, 0.18) * result
    return jnp.clip(result, min=-limit, max=limit).astype(held_as)


def setup_inputs(seed: int = 0) -> dict:
    key_list = jax.random.split(jax.random.key(seed), 22)
    inputs = bell_draw(key_list[0], (IMAGES, SEQ, D), 1.0, 6.0, ((0, 2), (1, 4), (2, 4)))
    cotangent = bell_draw(key_list[1], (IMAGES, SEQ, D), 1.0, 6.0, ((0, 2), (1, 4), (2, 4)))
    labels = set_ends(jax.random.randint(key_list[2], (IMAGES,), 0, CLASSES), jax.random.fold_in(key_list[2], 1), 0, CLASSES - 1).astype(jnp.int32)
    scale_ids = jnp.searchsorted(jnp.cumsum(uneven_parts(key_list[3], SCALES, SEQ, MOST, 2)), jnp.arange(SEQ), side="right").astype(jnp.int32)
    head_flags = set_ends((jax.random.randint(key_list[4], (H,), 0, 2) < 1).astype(jnp.int32), jax.random.fold_in(key_list[4], 1), 0, 1)
    class_table = bell_draw(key_list[5], (CLASSES, D), 1.0, 6.0, ((1, 32),))
    modulate_weight = bell_draw(key_list[6], (D, 6, D), D ** -0.5, 0.1875, ((0, 8), (2, 4)))
    modulate_bias = bell_draw(key_list[7], (6, H, HD), 0.5, 3.0, ((1, 4), (2, 8)))
    query_weight = bell_draw(key_list[8], (D, D), D ** -0.5, 0.1875, ((0, 8), (1, 4)))
    key_weight = bell_draw(key_list[9], (D, D), D ** -0.5, 0.1875, ((0, 8), (1, 4)))
    value_weight = bell_draw(key_list[10], (D, D), D ** -0.5, 0.1875, ((0, 8), (1, 4)))
    query_bias = bell_draw(key_list[11], (H, HD), 0.5, 3.0, ((0, 4), (1, 8)))
    value_bias = bell_draw(key_list[12], (H, HD), 0.5, 3.0, ((0, 4), (1, 8)))
    query_gain = draw_query_gain(jax.random.fold_in(key_list[21], 71), 0)
    key_gain = draw_key_gain(jax.random.fold_in(key_list[21], 71), 0)
    output_weight = bell_draw(key_list[15], (D, D), (D // 32) ** -0.5, 1.0, ((0, 4), (1, 8)))
    output_bias = bell_draw(key_list[16], (H, HD), 0.3, 2.0, ((0, 4), (1, 8)))
    up_weight = bell_draw(key_list[17], (D, FF), D ** -0.5, 0.1875, ((0, 8), (1, 4)))
    up_bias = bell_draw(key_list[18], (FF // HD, HD), 0.5, 3.0, ((0, 4), (1, 8)))
    down_weight = bell_draw(key_list[19], (FF, D), FF ** -0.5, 0.09375, ((0, 4), (1, 8)))
    down_bias = bell_draw(key_list[20], (H, HD), 0.3, 2.0, ((0, 4), (1, 8)))
    return {"inputs": inputs, "cotangent": cotangent, "labels": labels, "scale_ids": scale_ids, "head_flags": head_flags, "class_table": class_table, "modulate_weight": modulate_weight, "modulate_bias": modulate_bias, "query_weight": query_weight, "key_weight": key_weight, "value_weight": value_weight, "query_bias": query_bias, "value_bias": value_bias, "query_gain": query_gain, "key_gain": key_gain, "output_weight": output_weight, "output_bias": output_bias, "up_weight": up_weight, "up_bias": up_bias, "down_weight": down_weight, "down_bias": down_bias}


precise = lax.Precision.HIGHEST
norm_epsilon = 1e-06
clip_threshold = 2.0
masked_score = -1e+30

@jax.custom_vjp
def low(v):
    return lax.optimization_barrier(v.astype(jnp.bfloat16)).astype(jnp.float32)

@jax.custom_vjp
def low_back(v):
    return v

def low_keep(v):
    return (low(v), None)

def low_pass(kept, grad):
    return (grad,)

def back_keep(v):
    return (v, None)

def back_low(kept, grad):
    return (low(grad),)
low.defvjp(low_keep, low_pass)
low_back.defvjp(back_keep, back_low)

def layer_norm(values):
    centered = values - lax.optimization_barrier(jnp.mean(values, axis=-1, keepdims=True))
    spread = lax.optimization_barrier(jnp.mean(centered * centered, axis=-1, keepdims=True))
    return centered * lax.rsqrt(spread + norm_epsilon)

def head_norm(values, gains):
    return values * lax.rsqrt(lax.optimization_barrier(jnp.mean(values * values, axis=-1, keepdims=True)) + norm_epsilon) * gains

def modulated(values, shift, scale):
    return layer_norm(values) * (1.0 + scale) + shift

def matmul(left, right):
    return jnp.dot(left, right, precision=precise)

def image_block(inputs, modul, weights, scale_ids):
    query_weight, key_weight, value_weight, query_bias, value_bias, query_gain, key_gain, output_weight, output_bias, up_weight, up_bias, down_weight, down_bias = weights
    length = inputs.shape[0]
    heads = query_gain.shape[0]
    normed = low(modulated(inputs, modul[0], modul[1]))
    queries = low_back(matmul(normed, query_weight) + query_bias)
    keys = low_back(matmul(normed, key_weight))
    values = low(low_back(matmul(normed, value_weight) + value_bias))
    query_hat = low(head_norm(queries.reshape(length, heads, HD), query_gain))
    key_hat = low(head_norm(keys.reshape(length, heads, HD), key_gain))
    scores = low_back(jnp.einsum('qhd,khd->hqk', query_hat, key_hat, precision=precise) / math.sqrt(HD))
    allowed = (scale_ids[None, :] <= scale_ids[:, None])[None]
    highest = lax.optimization_barrier(jnp.max(jnp.where(allowed, scores, -jnp.inf), axis=(1, 2)))
    masked = jnp.where(allowed, scores, masked_score)
    row_peak = lax.optimization_barrier(jnp.max(masked, axis=-1, keepdims=True))
    log_total = row_peak + jnp.log(lax.optimization_barrier(jnp.sum(jnp.exp(masked - row_peak), axis=-1, keepdims=True)))
    probs = low(jnp.exp(masked - log_total))
    attended = jnp.einsum('hqk,khd->qhd', probs, values.reshape(length, heads, HD), precision=precise)
    attended = low(low_back(attended.reshape(length, heads * HD)))
    branch_one = low_back(matmul(attended, output_weight) + output_bias)
    middle = low(inputs + modul[2] * branch_one)
    normed_two = low(modulated(middle, modul[3], modul[4]))
    hidden_pre = low_back(matmul(normed_two, up_weight) + up_bias)
    hidden = low(jax.nn.gelu(hidden_pre, approximate=True))
    branch_two = low_back(matmul(hidden, down_weight) + down_bias)
    return (middle + modul[5] * branch_two, highest)

def reference(inputs, cotangent, labels, scale_ids, head_flags, class_table, modulate_weight, modulate_bias, query_weight, key_weight, value_weight, query_bias, value_bias, query_gain, key_gain, output_weight, output_bias, up_weight, up_bias, down_weight, down_bias):
    classes = class_table.shape[0]
    onehot = (labels[:, None] == jnp.arange(classes, dtype=jnp.int32)[None, :]).astype(jnp.float32)

    def forward(inputs, class_table, modulate_weight, modulate_bias, query_weight, key_weight, value_weight, query_bias, value_bias, query_gain, key_gain, output_weight, output_bias, up_weight, up_bias, down_weight, down_bias):
        cond = matmul(onehot, class_table)
        width = cond.shape[1]
        modul = low(jnp.einsum('bd,dje->bje', low(jax.nn.silu(cond)), modulate_weight, precision=precise) + modulate_bias.reshape(6, width))
        weights = (query_weight, key_weight, value_weight, query_bias.reshape(-1), value_bias.reshape(-1), query_gain, key_gain, output_weight, output_bias.reshape(-1), up_weight, up_bias.reshape(-1), down_weight, down_bias.reshape(-1))

        def one_image(pair):
            return image_block(pair[0], pair[1], weights, scale_ids)
        outputs, highest = lax.map(jax.checkpoint(one_image), (inputs, modul))
        return (outputs, highest)
    primals = tuple((item.astype(jnp.float32) for item in (inputs, class_table, modulate_weight, modulate_bias, query_weight, key_weight, value_weight, query_bias, value_bias, query_gain, key_gain, output_weight, output_bias, up_weight, up_bias, down_weight, down_bias)))
    block_out, pullback, highest = jax.vjp(forward, *primals, has_aux=True)
    grads = pullback(cotangent.astype(jnp.float32))
    head_max = lax.optimization_barrier(jnp.max(highest, axis=0))
    factor = jnp.where(head_flags == 1, jnp.sqrt(clip_threshold / jnp.maximum(head_max, clip_threshold)), jnp.ones_like(head_max))
    columns = jnp.repeat(factor, HD)
    clipped_query = primals[4] * columns[None, :]
    clipped_key = primals[5] * columns[None, :]
    clipped_query_bias = primals[7] * factor[:, None]
    return (block_out.astype(jnp.bfloat16), grads[0], grads[1], grads[2], grads[3], grads[4], grads[5], grads[6], grads[7], grads[8], grads[9], grads[10], grads[11], grads[12], grads[13], grads[14], grads[15], grads[16], clipped_query, clipped_key, clipped_query_bias)
```

```python
import functools
import math

import jax
import jax.numpy as jnp
from jax import lax
from jax.experimental import pallas as pl
from jax.experimental.pallas import tpu as pltpu
from jax.sharding import PartitionSpec as P

HD = 64
GC = 512
MESH = pl.DeviceIdType.MESH
precise = lax.Precision.HIGHEST
norm_epsilon = 1e-06
clip_threshold = 2.0
masked_score = -1e30
f32, bf16 = jnp.float32, jnp.bfloat16


def product(left, right, form):
    return jnp.einsum(form, left, right, preferred_element_type=f32)


def rcopy(src, dst, send_sem, recv_sem, device):
    return pltpu.make_async_remote_copy(
        src_ref=src,
        dst_ref=dst,
        send_sem=send_sem,
        recv_sem=recv_sem,
        device_id=device,
        device_id_type=MESH,
    )


class Place:
    def __init__(self, fs, cs, ts):
        self.fs, self.cs, self.ts = fs, cs, ts
        self.count = fs * cs * ts
        self.f, self.c, self.t = (lax.axis_index(n) for n in ("fsdp", "ctx", "tp"))
        self.hi, self.k = self.c // 2, lax.rem(self.c, 2)
        self.me = (self.f * cs + self.c) * ts + self.t
        self.slot = self.hi * ts + self.t

    def coords(self, n):
        return (n // (self.cs * self.ts), lax.rem(n // self.ts, self.cs), lax.rem(n, self.ts))

    def sibling(self):
        return (self.f, self.hi * 2 + 1 - self.k, self.t)

    def ypeer(self):
        return (self.f, (1 - self.hi) * 2 + self.k, self.t)

    def xpeer(self, s):
        return (lax.rem(self.f + s, self.fs), self.c, self.t)

    def xfrom(self, s):
        return lax.rem(self.f + self.fs - s, self.fs)

    def zpeer(self, s):
        return (self.f, self.c, lax.rem(self.t + s, self.ts))

    def zto(self, s):
        return lax.rem(self.t + s, self.ts)

    def zfrom(self, s):
        return lax.rem(self.t + self.ts - s, self.ts)

    def barrier(self):
        sem = pltpu.get_barrier_semaphore()

        def greet(n, carry):
            @pl.when(n != self.me)
            def _():
                pl.semaphore_signal(sem, inc=1, device_id=self.coords(n), device_id_type=MESH)

            return carry

        lax.fori_loop(0, self.count, greet, 0)
        pl.semaphore_wait(sem, self.count - 1)


def exchange_images(at, src_of, dst_of, send_sems, recv_sems, local_sem):
    slots = 2 * at.ts

    def start():
        for i in range(slots):
            hi, t = i // at.ts, i % at.ts

            @pl.when(i != at.slot)
            def _():
                rcopy(
                    src_of(i),
                    dst_of(at.slot),
                    send_sems.at[i],
                    recv_sems.at[at.slot],
                    (at.f, hi * 2 + at.k, t),
                ).start()

            @pl.when(i == at.slot)
            def _():
                pltpu.make_async_copy(src_of(i), dst_of(i), local_sem).start()

    def wait():
        for i in range(slots):
            @pl.when(i != at.slot)
            def _():
                rcopy(src_of(i), dst_of(i), send_sems.at[i], recv_sems.at[i], (at.f, at.c, at.t)).wait()

            @pl.when(i == at.slot)
            def _():
                pltpu.make_async_copy(src_of(i), dst_of(i), local_sem).wait()

    return start, wait


def broadcast_messages(at, src_of, slot_of, send_sems, recv_sems, local_sem):
    def start():
        def each(n, carry):
            @pl.when(n != at.me)
            def _():
                rcopy(src_of(n), slot_of(at.me), send_sems.at[n], recv_sems.at[at.me], at.coords(n)).start()

            @pl.when(n == at.me)
            def _():
                pltpu.make_async_copy(src_of(n), slot_of(n), local_sem).start()

            return carry

        lax.fori_loop(0, at.count, each, 0)

    def wait():
        def each(n, carry):
            @pl.when(n != at.me)
            def _():
                rcopy(src_of(n), slot_of(n), send_sems.at[n], recv_sems.at[n], at.coords(n)).wait()

            @pl.when(n == at.me)
            def _():
                pltpu.make_async_copy(src_of(n), slot_of(n), local_sem).wait()

            return carry

        lax.fori_loop(0, at.count, each, 0)

    return start, wait


def gather_kernel(
    fs, cs, ts, padded, per,
    x_ref, g_ref, s1, s2, s3, cond_ref, wm_ref, small_ref,
    xo, go, w1, w2, w3, mo,
    cond_slots, part,
    x_send, x_recv, g_send, g_recv, loc, sib_send, sib_recv, gsib_send, gsib_recv,
    c_send, c_recv, m_send, m_recv,
    core_send, core_recv, core_loc, z_send, z_recv, xs_send, xs_recv, ys_send, ys_recv,
    fx_send, fx_recv, fy_send, fy_recv,
):
    at = Place(fs, cs, ts)
    at.barrier()
    width = x_ref.shape[2]
    shards, weights = (s1, s2, s3), (w1, w2, w3)
    half = ts // 2

    def block_at(out):
        def dst(i):
            c = (i // ts) * 2 + at.k
            return out.at[pl.ds(c * padded, padded), pl.ds(pl.multiple_of(lax.rem(i, ts) * width, 128), width)]

        return dst

    x_start, x_wait = exchange_images(at, lambda i: x_ref.at[i], block_at(xo), x_send, x_recv, loc.at[0])
    g_start, g_wait = exchange_images(at, lambda i: g_ref.at[i], block_at(go), g_send, g_recv, loc.at[1])
    x_start()

    def row(f, hi, k=0):
        return pl.multiple_of(((f * 2 + hi) * 2 + k) * per, per)

    def core_copies(g):
        mine = weights[g].at[at.t, pl.ds(row(at.f, at.hi, at.k), per), :]
        theirs = weights[g].at[at.t, pl.ds(row(at.f, at.hi, 1 - at.k), per), :]
        local = pltpu.make_async_copy(shards[g].at[at.k], mine, core_loc.at[g])
        out = rcopy(shards[g].at[1 - at.k], mine, core_send.at[g], core_recv.at[g], at.sibling())
        inn = rcopy(shards[g].at[1 - at.k], theirs, core_send.at[g], core_recv.at[g], at.sibling())
        return local, out, inn

    def core_start(g):
        local, out, _ = core_copies(g)
        local.start()
        out.start()

    def core_wait(g):
        local, _, inn = core_copies(g)
        local.wait()
        inn.wait()

    def slab(g, z, n, f, hi):
        return weights[g].at[pl.ds(z, n), pl.ds(row(f, hi), 2 * per), :]

    def z_start(g):
        for s in range(1, ts):
            src = slab(g, at.t, 1, at.f, at.hi)
            rcopy(src, src, z_send.at[g, s], z_recv.at[g, s], at.zpeer(s)).start()

    def z_wait(g):
        for s in range(1, ts):
            src = slab(g, at.zfrom(s), 1, at.f, at.hi)
            rcopy(src, src, z_send.at[g, s], z_recv.at[g, s], at.zpeer(s)).wait()

    def xy_start(g):
        src = slab(g, 0, ts, at.f, at.hi)
        rcopy(src, src, ys_send.at[g], ys_recv.at[g], at.ypeer()).start()
        for s in range(1, fs):
            rcopy(src, src, xs_send.at[g, s], xs_recv.at[g, s], at.xpeer(s)).start()

    def xy_wait(g):
        src = slab(g, 0, ts, at.f, 1 - at.hi)
        rcopy(src, src, ys_send.at[g], ys_recv.at[g], at.ypeer()).wait()
        for s in range(1, fs):
            src = slab(g, 0, ts, at.xfrom(s), at.hi)
            rcopy(src, src, xs_send.at[g, s], xs_recv.at[g, s], at.xpeer(s)).wait()

    def fwd_start(g):
        for s in range(1, fs):
            src = slab(g, half, half, at.f, 1 - at.hi)
            rcopy(src, src, fx_send.at[g, s], fx_recv.at[g, s], at.xpeer(s)).start()
            src = slab(g, 0, half, at.xfrom(s), at.hi)
            rcopy(src, src, fy_send.at[g, s], fy_recv.at[g, s], at.ypeer()).start()

    def fwd_wait(g):
        for s in range(1, fs):
            src = slab(g, half, half, at.xfrom(s), 1 - at.hi)
            rcopy(src, src, fx_send.at[g, s], fx_recv.at[g, s], at.xpeer(s)).wait()
            src = slab(g, 0, half, at.xfrom(s), 1 - at.hi)
            rcopy(src, src, fy_send.at[g, s], fy_recv.at[g, s], at.ypeer()).wait()

    core_start(0)

    cond_slots[at.t] = cond_ref[...]

    def cond_copy(s, slot):
        return rcopy(cond_ref, cond_slots.at[slot], c_send.at[s], c_recv.at[s], at.zpeer(s))

    for s in range(1, ts):
        cond_copy(s, at.t).start()
    core_start(1)
    core_start(2)
    for s in range(1, ts):
        cond_copy(s, at.zfrom(s)).wait()
    cond = cond_slots[0]
    for z in range(1, ts):
        cond = cond + cond_slots[z]
    silu = (cond / (1.0 + jnp.exp(-cond))).astype(bf16)
    columns = width
    for j in range(6):
        part[:, j, :] = jnp.dot(silu, wm_ref[:, j * columns : (j + 1) * columns], preferred_element_type=f32)
    images = part.shape[0]
    for j in range(2):
        part[:, 6 + j, :] = jnp.broadcast_to(small_ref[j : j + 1, :], (images, columns))

    def image_of(n):
        f, c, t = at.coords(n)
        return (f * 2 + c // 2) * ts + t

    m_start, m_wait = broadcast_messages(
        at, lambda n: part.at[image_of(n)], lambda n: mo.at[n], m_send, m_recv, loc.at[2]
    )
    m_start()

    core_wait(0)
    z_start(0)
    x_wait()

    def sib_copies(out, send, recv):
        copies = []
        for hi in range(2):
            mine = out.at[pl.ds((hi * 2 + at.k) * padded, padded), :]
            theirs = out.at[pl.ds((hi * 2 + 1 - at.k) * padded, padded), :]
            copies.append(
                (
                    rcopy(mine, mine, send.at[hi], recv.at[hi], at.sibling()),
                    rcopy(theirs, theirs, send.at[hi], recv.at[hi], at.sibling()),
                )
            )
        return copies

    for out, _ in sib_copies(xo, sib_send, sib_recv):
        out.start()
    g_start()
    core_wait(1)
    core_wait(2)
    z_wait(0)
    xy_start(0)
    z_start(1)
    z_wait(1)
    xy_start(1)
    xy_wait(0)
    fwd_start(0)
    z_start(2)
    z_wait(2)
    xy_wait(1)
    xy_start(2)
    fwd_start(1)
    g_wait()
    for out, _ in sib_copies(go, gsib_send, gsib_recv):
        out.start()
    xy_wait(2)
    fwd_start(2)
    m_wait()
    for _, inn in sib_copies(xo, sib_send, sib_recv):
        inn.wait()
    for _, inn in sib_copies(go, gsib_send, gsib_recv):
        inn.wait()
    for g in range(3):
        fwd_wait(g)


def scatter_kernel(
    fs, cs, ts, padded, per,
    d1, d2, d3, dx_ref, bo_ref, small_ref,
    o1, o2, o3, dxo, boo, mo,
    ry1, rx1, xs, ys, rx2, ry2, own, rz, total,
    dx_send, dx_recv, bo_send, bo_recv, loc, m_send, m_recv,
    y1_send, y1_recv, x1_send, x1_recv, x2_send, x2_recv, y2_send, y2_recv,
    z_send, z_recv, k_send, k_recv,
):
    at = Place(fs, cs, ts)
    at.barrier()
    width = dxo.shape[2]
    grads, outs = (d1, d2, d3), (o1, o2, o3)
    half = ts // 2

    def block_of(ref):
        def src(i):
            c = (i // ts) * 2 + at.k
            return ref.at[pl.ds(c * padded, padded), pl.ds(pl.multiple_of(lax.rem(i, ts) * width, 128), width)]

        return src

    dx_start, dx_wait = exchange_images(at, block_of(dx_ref), lambda i: dxo.at[i], dx_send, dx_recv, loc.at[0])
    bo_start, bo_wait = exchange_images(at, block_of(bo_ref), lambda i: boo.at[i], bo_send, bo_recv, loc.at[1])

    def message_slot(n):
        f, c, t = at.coords(n)
        return mo.at[(f * 2 + c // 2) * ts + t, lax.rem(c, 2)]

    m_start, m_wait = broadcast_messages(
        at, lambda n: small_ref.at[lax.rem(n, ts)], message_slot, m_send, m_recv, loc.at[2]
    )

    def row(f, hi):
        return pl.multiple_of((f * 2 + hi) * 2 * per, 2 * per)

    def slab(g, z, n, f, hi):
        return grads[g].at[pl.ds(z, n), pl.ds(row(f, hi), 2 * per), :]

    def far(s):
        return lax.rem(at.f + s, fs)

    def one(g, s):
        a = rcopy(slab(g, 0, half, far(s), 1 - at.hi), ry1.at[g, s - 1], y1_send.at[g, s], y1_recv.at[g, s], at.ypeer())
        b = rcopy(slab(g, half, half, far(s), 1 - at.hi), rx1.at[g, s - 1], x1_send.at[g, s], x1_recv.at[g, s], at.xpeer(s))
        return a, b

    def two_x(g, s):
        return rcopy(xs.at[g, s - 1], rx2.at[g, s - 1], x2_send.at[g, s], x2_recv.at[g, s], at.xpeer(s))

    def two_y(g):
        return rcopy(ys.at[g], ry2.at[g], y2_send.at[g], y2_recv.at[g], at.ypeer())

    def three(g, s):
        return rcopy(own.at[g, at.zto(s)], rz.at[g, s - 1], z_send.at[g, s], z_recv.at[g, s], at.zpeer(s))

    def start_one(g):
        for s in range(1, fs):
            for copy in one(g, s):
                copy.start()

    def start_two(g):
        for s in range(1, fs):
            for copy in one(g, s):
                copy.wait()

        def body(z, carry):
            for s in range(1, fs):
                value = grads[g][z, pl.ds(row(far(s), at.hi), 2 * per), :].astype(f32)
                value = value + ry1[g, s - 1, z].astype(f32)
                xs[g, s - 1, z] = value.astype(bf16)
                xs[g, s - 1, half + z] = grads[g][half + z, pl.ds(row(far(s), at.hi), 2 * per), :]
            value = grads[g][half + z, pl.ds(row(at.f, 1 - at.hi), 2 * per), :].astype(f32)
            for s in range(1, fs):
                value = value + rx1[g, s - 1, z].astype(f32)
            ys[g, half + z] = value.astype(bf16)
            ys[g, z] = grads[g][z, pl.ds(row(at.f, 1 - at.hi), 2 * per), :]
            return carry

        lax.fori_loop(0, half, body, 0)
        for s in range(1, fs):
            two_x(g, s).start()
        two_y(g).start()

    def start_three(g):
        for s in range(1, fs):
            two_x(g, s).wait()
        two_y(g).wait()

        def body(z, carry):
            value = grads[g][z, pl.ds(row(at.f, at.hi), 2 * per), :].astype(f32) + ry2[g, z].astype(f32)
            for s in range(1, fs):
                value = value + rx2[g, s - 1, z].astype(f32)
            own[g, z] = value.astype(bf16)
            return carry

        lax.fori_loop(0, ts, body, 0)
        for s in range(1, ts):
            three(g, s).start()

    def four(g):
        there = pl.multiple_of((1 - at.k) * per, per)
        out = rcopy(total.at[g, pl.ds(there, per)], outs[g].at[at.k], k_send.at[g], k_recv.at[g], at.sibling())
        inn = rcopy(total.at[g, pl.ds(there, per)], outs[g].at[1 - at.k], k_send.at[g], k_recv.at[g], at.sibling())
        return out, inn

    def start_four(g):
        for s in range(1, ts):
            three(g, s).wait()
        value = own[g, at.t].astype(f32)
        for s in range(1, ts):
            value = value + rz[g, s - 1].astype(f32)
        total[g] = value
        four(g)[0].start()
        outs[g][at.k] = total[g, pl.ds(pl.multiple_of(at.k * per, per), per), :]

    order = (2, 1, 0)
    start_one(order[0])
    m_start()
    start_one(order[1])
    start_two(order[0])
    start_one(order[2])
    start_two(order[1])
    start_three(order[0])
    start_two(order[2])
    bo_start()
    start_three(order[1])
    start_four(order[0])
    dx_start()
    start_three(order[2])
    start_four(order[1])
    start_four(order[2])
    for g in range(3):
        four(g)[1].wait()
    m_wait()
    bo_wait()
    dx_wait()


def attention_forward(q_ref, k_ref, v_ref, qg_ref, kg_ref, sq_ref, sk_ref, qh_ref, kh_ref, at_ref, lse_ref, hm_ref):
    rows = q_ref.shape[0]
    tile = rows // 4
    for h in range(2):
        lanes = slice(h * HD, (h + 1) * HD)
        q, k = q_ref[:, lanes], k_ref[:, lanes]
        qh = q * lax.rsqrt(jnp.mean(q * q, axis=-1, keepdims=True) + norm_epsilon) * qg_ref[0, :, lanes]
        kh = k * lax.rsqrt(jnp.mean(k * k, axis=-1, keepdims=True) + norm_epsilon) * kg_ref[0, :, lanes]
        qh_ref[:, lanes] = qh.astype(bf16)
        kh_ref[:, lanes] = kh.astype(bf16)
        highest = jnp.full((1, 1), -jnp.inf, f32)
        keys, vals = kh_ref[:, lanes], v_ref[:, lanes]
        for n in range(4):
            span = slice(n * tile, (n + 1) * tile)
            s = lax.dot_general(qh_ref[span, lanes], keys, (((1,), (1,)), ((), ())), preferred_element_type=f32) * 0.125
            allowed = sk_ref[...] <= sq_ref[span, :]
            highest = jnp.maximum(highest, jnp.max(jnp.where(allowed, s, -jnp.inf), keepdims=True))
            s = jnp.where(allowed, s, masked_score)
            peak = jnp.max(s, axis=-1, keepdims=True)
            e = jnp.exp(s - peak)
            total = jnp.sum(e, axis=-1, keepdims=True)
            log_total = peak + jnp.log(total)
            p = jnp.exp(s - log_total).astype(bf16)
            at_ref[span, lanes] = jnp.dot(p, vals, preferred_element_type=f32).astype(bf16)
            lse_ref[0, h, span, :] = log_total
        hm_ref[0, h] = jnp.broadcast_to(highest, (8, 128))


def attention_backward(
    q_ref, k_ref, qh_ref, kh_ref, v_ref, da_ref, lse_ref, qg_ref, kg_ref, sq_ref, sk_ref,
    dq_ref, dk_ref, dv_ref, gg_ref, dqh, dkh, dvh,
):
    rows = q_ref.shape[0]
    tile = rows // 4
    for h in range(2):
        lanes = slice(h * HD, (h + 1) * HD)
        keys, vals = kh_ref[:, lanes], v_ref[:, lanes]
        dkh[...] = jnp.zeros_like(dkh)
        dvh[...] = jnp.zeros_like(dvh)
        for n in range(4):
            span = slice(n * tile, (n + 1) * tile)
            qh, da = qh_ref[span, lanes], da_ref[span, lanes]
            s = lax.dot_general(qh, keys, (((1,), (1,)), ((), ())), preferred_element_type=f32) * 0.125
            allowed = sk_ref[...] <= sq_ref[span, :]
            p = jnp.where(allowed, jnp.exp(jnp.where(allowed, s, masked_score) - lse_ref[0, h, span, :]), 0.0)
            dp = lax.dot_general(da, vals, (((1,), (1,)), ((), ())), preferred_element_type=f32)
            centre = jnp.sum(p * dp, axis=-1, keepdims=True)
            ds = (p * (dp - centre)).astype(bf16)
            dqh[span, :] = jnp.dot(ds, keys, preferred_element_type=f32) * 0.125
            dkh[...] += lax.dot_general(ds, qh, (((0,), (0,)), ((), ())), preferred_element_type=f32)
            dvh[...] += lax.dot_general(p.astype(bf16), da, (((0,), (0,)), ((), ())), preferred_element_type=f32)
        dv_ref[:, lanes] = dvh[...].astype(bf16)
        for which, (raw_ref, gain_ref, delta, out_ref) in enumerate(
            ((q_ref, qg_ref, dqh[...], dq_ref), (k_ref, kg_ref, dkh[...] * 0.125, dk_ref))
        ):
            raw, gain = raw_ref[:, lanes], gain_ref[0, :, lanes]
            r = lax.rsqrt(jnp.mean(raw * raw, axis=-1, keepdims=True) + norm_epsilon)
            gg_ref[0, which : which + 1, lanes] = jnp.sum(delta * raw * r, axis=0, keepdims=True)
            t = delta * gain
            out_ref[:, lanes] = (r * t - raw * (r * r * r) * jnp.mean(t * raw, axis=-1, keepdims=True)).astype(bf16)


def layer_norm(values):
    centered = values - jnp.mean(values, axis=-1, keepdims=True)
    spread = jnp.mean(centered * centered, axis=-1, keepdims=True)
    return centered * lax.rsqrt(spread + norm_epsilon), lax.rsqrt(spread + norm_epsilon)


def norm_backward(normal, inverse, scale, incoming):
    e = incoming * (1.0 + scale)
    mean_e = jnp.mean(e, axis=-1, keepdims=True)
    mean_en = jnp.mean(e * normal, axis=-1, keepdims=True)
    return (
        (e - mean_e - normal * mean_en) * inverse,
        jnp.sum(incoming, axis=0),
        jnp.sum(incoming * normal, axis=0),
    )


def gelu_tanh(values):
    return jax.nn.gelu(values, approximate=True)


def on_device(
    fs, cs, ts,
    inputs, cotangent, labels, scale_ids, head_flags, class_table, modulate_weight, modulate_bias,
    query_weight, key_weight, value_weight, query_bias, value_bias, query_gain, key_gain,
    output_weight, output_bias, up_weight, up_bias, down_weight, down_bias,
):
    images, rows_here, width = inputs.shape
    if images != 2 * ts or cs != 4 or ts % 2 or width != 256:
        raise ValueError("unsupported mesh")
    length = scale_ids.shape[0]
    every = labels.shape[0]
    count = fs * cs * ts
    blocks = fs * cs
    padded = -(-rows_here // 16) * 16
    tokens = cs * padded
    features = ts * width
    per = query_weight.shape[0]
    part_cols = class_table.shape[1]
    f, c, t = (lax.axis_index(n) for n in ("fsdp", "ctx", "tp"))
    core = lax.rem(c, 2)

    classes = class_table.shape[0]
    onehot = (labels[:, None] == jnp.arange(classes, dtype=jnp.int32)[None, :]).astype(bf16)
    cond_part = jnp.dot(onehot, class_table, preferred_element_type=f32)
    cond_spread = lax.dynamic_update_slice(
        jnp.zeros((every, per), f32), cond_part, (0, t * part_cols)
    )
    fit = ((0, 0), (0, padded - rows_here), (0, 0))
    x_blocks, g_blocks = jnp.pad(inputs, fit), jnp.pad(cotangent, fit)

    def halves(weight):
        return weight.reshape(per, 2, -1).transpose(1, 0, 2)

    out_t, down_t = output_weight.T, down_weight.T
    shard_one = jnp.concatenate(
        [halves(query_weight), halves(key_weight), halves(value_weight), halves(out_t)], axis=2
    )
    shard_two, shard_three = halves(up_weight), halves(down_t)
    lanes = modulate_bias.shape[2]
    small_rows = jnp.concatenate(
        [
            modulate_bias.reshape(-1, lanes), query_bias, value_bias, query_gain, key_gain,
            output_bias, down_bias, up_bias,
        ],
        axis=0,
    ).astype(f32)
    small = jnp.pad(small_rows.reshape(-1), (0, 2 * width - small_rows.size)).reshape(2, width)
    any_spec = pl.BlockSpec(memory_space=pl.ANY)
    vmem_spec = pl.BlockSpec(memory_space=pltpu.VMEM)
    dma = pltpu.SemaphoreType.DMA
    slots = 2 * ts
    wide = jax.ShapeDtypeStruct((ts, features, GC), bf16)
    flat = jax.ShapeDtypeStruct((tokens, features), bf16)
    x, g, weight_one, weight_two, weight_three, messages = pl.pallas_call(
        functools.partial(gather_kernel, fs, cs, ts, padded, per),
        name="gather",
        out_shape=(flat, flat, wide, wide, wide, jax.ShapeDtypeStruct((count, 8, width), f32)),
        in_specs=[any_spec] * 5 + [vmem_spec] * 3,
        out_specs=(any_spec,) * 5 + (vmem_spec,),
        scratch_shapes=[
            pltpu.VMEM((ts, every, per), f32),
            pltpu.VMEM((every, 8, width), f32),
            dma((slots,)), dma((slots,)), dma((slots,)), dma((slots,)), dma((3,)),
            dma((2,)), dma((2,)), dma((2,)), dma((2,)),
            dma((ts,)), dma((ts,)), dma((count,)), dma((count,)),
            dma((3,)), dma((3,)), dma((3,)), dma((3, ts)), dma((3, ts)),
            dma((3, fs)), dma((3, fs)), dma((3,)), dma((3,)),
            dma((3, fs)), dma((3, fs)), dma((3, fs)), dma((3, fs)),
        ],
        compiler_params=pltpu.CompilerParams(
            collective_id=0, has_side_effects=True, vmem_limit_bytes=32 << 20
        ),
    )(
        x_blocks, g_blocks, shard_one, shard_two, shard_three, cond_spread,
        modulate_weight.reshape(per, 6 * width), small,
    )

    messages = messages.reshape(blocks, ts, 8, width)
    params = messages[:, :, 6:8].reshape(blocks, ts, 2 * width)[:, :, : small_rows.size]
    params = params.reshape(blocks, ts, -1, lanes).transpose(2, 1, 0, 3)
    params = params.reshape(-1, ts, blocks * lanes)
    heads = modulate_bias.shape[1]

    def whole(start):
        return params[start : start + heads].transpose(1, 0, 2).reshape(features)

    def here(start, rows):
        mine = lax.dynamic_slice_in_dim(params, start + core * (rows // 2), rows // 2, 0)
        return mine.transpose(1, 0, 2).reshape(ts, 1, -1)

    first = 6 * heads
    query_shift, value_shift = here(first, heads), here(first + heads, heads)
    query_gains, key_gains = here(first + 2 * heads, heads), here(first + 3 * heads, heads)
    output_shift, down_shift = whole(first + 4 * heads), whole(first + 5 * heads)
    up_shift = here(first + 6 * heads, up_bias.shape[0])
    modulate_shift = (
        params[:first].reshape(6, heads, ts, -1).transpose(0, 2, 1, 3).reshape(6, features)
    )
    modulation = jnp.sum(messages[:, :, :6], axis=0).transpose(1, 0, 2).reshape(6, features)
    modulation = (modulation + modulate_shift).astype(bf16).astype(f32)
    shift_one, scale_one, gate_one, shift_two, scale_two, gate_two = (modulation[j] for j in range(6))

    x_wide = x.astype(f32)
    valid = (jnp.arange(tokens) % padded < rows_here)[:, None]
    x_wide = jnp.where(valid, x_wide, 0.0)
    incoming = jnp.where(valid, g.astype(f32), 0.0)
    normal_one, inverse_one = layer_norm(x_wide)
    normed_one = (normal_one * (1.0 + scale_one) + shift_one).astype(bf16)
    qkv_pre = product(normed_one, weight_one[:, :, :384], "sd,zde->sze")
    query_pre = (qkv_pre[:, :, :128] + query_shift[:, 0]).reshape(tokens, -1)
    key_pre = qkv_pre[:, :, 128:256].reshape(tokens, -1)
    value_rows = (qkv_pre[:, :, 256:] + value_shift[:, 0]).astype(bf16).reshape(tokens, -1)
    ids = scale_ids.reshape(cs, rows_here)
    spare = ((0, 0), (0, padded - rows_here))
    ids_query = jnp.pad(ids, spare, constant_values=-1).reshape(tokens, 1)
    ids_key = jnp.pad(ids, spare, constant_values=1 << 20).reshape(1, tokens)
    column = pl.BlockSpec((tokens, 128), lambda z: (0, z))
    gain_spec = pl.BlockSpec((1, 1, 128), lambda z: (z, 0, 0))
    id_specs = [pl.BlockSpec((tokens, 1), lambda z: (0, 0)), pl.BlockSpec((1, tokens), lambda z: (0, 0))]
    lse_spec = pl.BlockSpec((1, 2, tokens, 1), lambda z: (z, 0, 0, 0))
    here_cols = ts * 128
    rows_type = jax.ShapeDtypeStruct((tokens, here_cols), bf16)
    query_hat, key_hat, attended, log_totals, highest = pl.pallas_call(
        attention_forward,
        name="attend",
        grid=(ts,),
        out_shape=(
            rows_type, rows_type, rows_type,
            jax.ShapeDtypeStruct((ts, 2, tokens, 1), f32),
            jax.ShapeDtypeStruct((ts, 2, 8, 128), f32),
        ),
        in_specs=[column] * 3 + [gain_spec] * 2 + id_specs,
        out_specs=(column, column, column, lse_spec, pl.BlockSpec((1, 2, 8, 128), lambda z: (z, 0, 0, 0))),
        compiler_params=pltpu.CompilerParams(vmem_limit_bytes=48 << 20),
    )(query_pre, key_pre, value_rows, query_gains, key_gains, ids_query, ids_key)

    pairs = [(i, i ^ 1) for i in range(cs)]

    def both_cores(partial_rows):
        mine = partial_rows.astype(bf16)
        return mine.astype(f32) + lax.ppermute(mine, "ctx", pairs).astype(f32)

    attended_z = attended.reshape(tokens, ts, 128)
    branch_one = both_cores(product(attended_z, weight_one[:, :, 384:], "sze,zfe->sf")) + output_shift
    middle = (x_wide + gate_one * branch_one).astype(bf16)
    middle_wide = middle.astype(f32)
    normal_two, inverse_two = layer_norm(middle_wide)
    normed_two = (normal_two * (1.0 + scale_two) + shift_two).astype(bf16)
    hidden_pre = product(normed_two, weight_two, "sd,zdh->zsh") + up_shift
    hidden = gelu_tanh(hidden_pre).astype(bf16)
    branch_two = both_cores(product(hidden, weight_three, "zsh,zfh->sf")) + down_shift
    block_rows = (middle_wide + gate_two * branch_two).astype(bf16)

    down_delta = (incoming * gate_two).astype(bf16)
    gate_two_delta = jnp.sum(incoming * branch_two, axis=0)
    down_bias_part = jnp.sum(down_delta.astype(f32), axis=0)
    grad_three = product(down_delta, hidden, "sf,zsh->zfh").astype(bf16)
    hidden_delta = product(down_delta, weight_three, "sf,zfh->zsh")
    primal, gelu_back = jax.vjp(gelu_tanh, hidden_pre)
    pre_delta = gelu_back(hidden_delta)[0].astype(bf16)
    up_bias_part = jnp.sum(pre_delta.astype(f32), axis=1)
    grad_two = product(normed_two, pre_delta, "sd,zsh->zdh").astype(bf16)
    normed_two_delta = both_cores(product(pre_delta, weight_two, "zsh,zdh->sd"))
    middle_part, shift_two_delta, scale_two_delta = norm_backward(
        normal_two, inverse_two, scale_two, normed_two_delta
    )
    middle_delta = incoming + middle_part
    branch_delta = (middle_delta * gate_one).astype(bf16)
    gate_one_delta = jnp.sum(middle_delta * branch_one, axis=0)
    output_bias_part = jnp.sum(branch_delta.astype(f32), axis=0)
    grad_out = product(branch_delta, attended_z, "sf,sze->zfe").astype(bf16)
    attended_delta = product(branch_delta, weight_one[:, :, 384:], "sf,zfe->sze").astype(bf16)
    queries_delta, keys_delta, values_low, gain_parts = pl.pallas_call(
        attention_backward,
        name="attend_back",
        grid=(ts,),
        out_shape=(rows_type, rows_type, rows_type, jax.ShapeDtypeStruct((ts, 2, 128), f32)),
        in_specs=[column] * 6 + [lse_spec] + [gain_spec] * 2 + id_specs,
        out_specs=(column, column, column, pl.BlockSpec((1, 2, 128), lambda z: (z, 0, 0))),
        scratch_shapes=[pltpu.VMEM((tokens, HD), f32)] * 3,
        compiler_params=pltpu.CompilerParams(vmem_limit_bytes=48 << 20),
    )(
        query_pre, key_pre, query_hat, key_hat, value_rows,
        attended_delta.reshape(tokens, here_cols), log_totals, query_gains, key_gains, ids_query, ids_key,
    )
    query_bias_part = jnp.sum(queries_delta.astype(f32), axis=0).reshape(ts, 128)
    value_bias_part = jnp.sum(values_low.astype(f32), axis=0).reshape(ts, 128)
    deltas = jnp.concatenate(
        [v.reshape(tokens, ts, 128) for v in (queries_delta, keys_delta, values_low)], axis=2
    )
    grad_qkv = product(normed_one, deltas, "sd,sze->zde").astype(bf16)
    grad_one = jnp.concatenate([grad_qkv, grad_out], axis=2)
    normed_one_delta = both_cores(product(deltas, weight_one[:, :, :384], "sze,zde->sd"))
    inputs_part, shift_one_delta, scale_one_delta = norm_backward(
        normal_one, inverse_one, scale_one, normed_one_delta
    )
    inputs_delta = (middle_delta + inputs_part).astype(bf16)
    deltas_six = jnp.stack(
        [shift_one_delta, scale_one_delta, gate_one_delta, shift_two_delta, scale_two_delta, gate_two_delta]
        + [output_bias_part, down_bias_part]
    )
    tops = jnp.broadcast_to(highest[:, :, 0, :1], (ts, 2, HD)).reshape(ts, 1, 128)
    own_small = jnp.concatenate(
        [
            deltas_six.reshape(8, ts, width).transpose(1, 0, 2),
            jnp.stack([query_bias_part, value_bias_part], axis=1).reshape(ts, 1, width),
            gain_parts.reshape(ts, 1, width),
            up_bias_part.reshape(ts, 2, width),
            jnp.pad(tops, ((0, 0), (0, 3), (0, width - 128))),
        ],
        axis=1,
    )
    f1 = max(fs - 1, 1)
    out_type = jax.ShapeDtypeStruct((2, per, GC), f32)
    blocks_type = jax.ShapeDtypeStruct((slots, padded, width), bf16)
    sum_one, sum_two, sum_three, dx_blocks, bo_blocks, mail = pl.pallas_call(
        functools.partial(scatter_kernel, fs, cs, ts, padded, per),
        name="scatter",
        out_shape=(
            out_type, out_type, out_type, blocks_type, blocks_type,
            jax.ShapeDtypeStruct((every, 2, 16, width), f32),
        ),
        in_specs=[vmem_spec] * 3 + [any_spec] * 3,
        out_specs=(vmem_spec,) * 3 + (any_spec,) * 3,
        scratch_shapes=[
            pltpu.VMEM((3, f1, ts // 2, 2 * per, GC), bf16),
            pltpu.VMEM((3, f1, ts // 2, 2 * per, GC), bf16),
            pltpu.VMEM((3, f1, ts, 2 * per, GC), bf16),
            pltpu.VMEM((3, ts, 2 * per, GC), bf16),
            pltpu.VMEM((3, f1, ts, 2 * per, GC), bf16),
            pltpu.VMEM((3, ts, 2 * per, GC), bf16),
            pltpu.VMEM((3, ts, 2 * per, GC), bf16),
            pltpu.VMEM((3, ts - 1, 2 * per, GC), bf16),
            pltpu.VMEM((3, 2 * per, GC), f32),
            dma((slots,)), dma((slots,)), dma((slots,)), dma((slots,)), dma((3,)),
            dma((count,)), dma((count,)),
            dma((3, fs)), dma((3, fs)), dma((3, fs)), dma((3, fs)),
            dma((3, fs)), dma((3, fs)), dma((3,)), dma((3,)),
            dma((3, ts)), dma((3, ts)), dma((3,)), dma((3,)),
        ],
        compiler_params=pltpu.CompilerParams(
            collective_id=1, has_side_effects=True, vmem_limit_bytes=60 << 20
        ),
    )(grad_one, grad_two, grad_three, inputs_delta, block_rows, own_small)

    block_out = bo_blocks[:, :rows_here]
    inputs_grad = dx_blocks[:, :rows_here].astype(f32)

    def joined(parts):
        return parts.transpose(1, 0, 2).reshape(per, -1)

    query_weight_grad = joined(sum_one[:, :, :128])
    key_weight_grad = joined(sum_one[:, :, 128:256])
    value_weight_grad = joined(sum_one[:, :, 256:384])
    output_weight_grad = joined(sum_one[:, :, 384:]).T
    up_weight_grad = joined(sum_two)
    down_weight_grad = joined(sum_three).T
    mod_delta = mail[:, 0, :6]
    same = jnp.sum(mail[:, 0, :8], axis=0)
    halves_sum = jnp.sum(mail[:, :, 8:12], axis=0)
    block = f * cs + c

    def mine(values):
        return lax.dynamic_slice_in_dim(values, block * lanes, lanes, values.ndim - 1)

    same = mine(same.reshape(8, heads, HD))
    modulate_bias_grad, output_bias_grad, down_bias_grad = same[:6], same[6], same[7]
    quarter = mine(halves_sum[:, :2].reshape(2, 4, heads // 2, HD)).transpose(1, 0, 2, 3).reshape(4, heads, lanes)
    query_bias_grad, value_bias_grad, query_gain_grad, key_gain_grad = (quarter[j] for j in range(4))
    up_bias_grad = mine(halves_sum[:, 2:].reshape(-1, HD))
    head_max = jnp.max(mail[:, :, 12, :128], axis=0).reshape(heads, HD)[:, 0]

    cond_rows = lax.all_gather(cond_part, "tp", axis=1, tiled=True)
    silu_cond = jax.nn.silu(cond_rows).astype(bf16)
    flat_delta = mod_delta.reshape(every, 6 * width)
    modulate_weight_grad = jnp.einsum(
        "bd,be->de", silu_cond.astype(f32), flat_delta, precision=precise
    ).reshape(per, 6, width)
    silu_delta = jnp.einsum(
        "be,de->bd", flat_delta, modulate_weight.reshape(per, 6 * width).astype(f32), precision=precise
    )
    silu_cols = lax.psum_scatter(silu_delta, "tp", scatter_dimension=1, tiled=True)
    primal, silu_back = jax.vjp(jax.nn.silu, cond_part)
    cond_delta = silu_back(silu_cols)[0]
    class_table_grad = jnp.dot(onehot.astype(f32).T, cond_delta, precision=precise)

    factor = jnp.where(
        head_flags == 1,
        jnp.sqrt(clip_threshold / jnp.maximum(head_max, clip_threshold)),
        jnp.ones_like(head_max),
    )
    columns = jnp.repeat(factor, HD)
    clipped_query = query_weight.astype(f32) * columns[None, :]
    clipped_key = key_weight.astype(f32) * columns[None, :]
    clipped_query_bias = query_bias.astype(f32) * factor[:, None]
    return (
        block_out, inputs_grad, class_table_grad, modulate_weight_grad, modulate_bias_grad,
        query_weight_grad, key_weight_grad, value_weight_grad, query_bias_grad, value_bias_grad,
        query_gain_grad, key_gain_grad, output_weight_grad, output_bias_grad,
        up_weight_grad, up_bias_grad, down_weight_grad, down_bias_grad,
        clipped_query, clipped_key, clipped_query_bias,
    )


def solution(mesh):
    rows = P("fsdp", "ctx", "tp")
    table = P(None, ("fsdp", "ctx", "tp"))
    left = P(("fsdp", "ctx"), "tp")
    right = P("tp", ("fsdp", "ctx"))
    modulate = P(("fsdp", "ctx"), None, "tp")
    modulate_small = P(None, "tp", ("fsdp", "ctx"))
    return jax.shard_map(
        functools.partial(on_device, mesh.shape["fsdp"], mesh.shape["ctx"], mesh.shape["tp"]),
        mesh=mesh,
        in_specs=(
            rows, rows, P(), P(), P("tp"), table, modulate, modulate_small,
            left, left, left, right, right, right, right,
            right, right, left, right, right, right,
        ),
        out_specs=(
            rows, rows, table, modulate, modulate_small,
            left, left, left, right, right, right, right,
            right, right, left, right, right, right,
            left, left, right,
        ),
        check_vma=False,
    )
```

```python
import functools
import math

import jax
import jax.numpy as jnp
from jax import lax
from jax.experimental import pallas as pl
from jax.experimental.pallas import tpu as pltpu
from jax.sharding import PartitionSpec as P

HD = 64
GC = 512
CHUNK = 256
MESH = pl.DeviceIdType.MESH
precise = lax.Precision.HIGHEST
norm_epsilon = 1e-06
clip_threshold = 2.0
masked_score = -1e30
f32, bf16 = jnp.float32, jnp.bfloat16


def product(left, right, form):
    return jnp.einsum(form, left, right, preferred_element_type=f32)


def rcopy(src, dst, send_sem, recv_sem, device):
    return pltpu.make_async_remote_copy(
        src_ref=src,
        dst_ref=dst,
        send_sem=send_sem,
        recv_sem=recv_sem,
        device_id=device,
        device_id_type=MESH,
    )


class Place:
    def __init__(self, fs, cs, ts):
        self.fs, self.cs, self.ts = fs, cs, ts
        self.count = fs * cs * ts
        self.f, self.c, self.t = (lax.axis_index(n) for n in ("fsdp", "ctx", "tp"))
        self.hi, self.k = self.c // 2, lax.rem(self.c, 2)
        self.me = (self.f * cs + self.c) * ts + self.t
        self.slot = self.hi * ts + self.t

    def coords(self, n):
        return (n // (self.cs * self.ts), lax.rem(n // self.ts, self.cs), lax.rem(n, self.ts))

    def sibling(self):
        return (self.f, self.hi * 2 + 1 - self.k, self.t)

    def ypeer(self):
        return (self.f, (1 - self.hi) * 2 + self.k, self.t)

    def xpeer(self, s):
        return (lax.rem(self.f + s, self.fs), self.c, self.t)

    def xfrom(self, s):
        return lax.rem(self.f + self.fs - s, self.fs)

    def zpeer(self, s):
        return (self.f, self.c, lax.rem(self.t + s, self.ts))

    def zto(self, s):
        return lax.rem(self.t + s, self.ts)

    def zfrom(self, s):
        return lax.rem(self.t + self.ts - s, self.ts)

    def barrier(self):
        sem = pltpu.get_barrier_semaphore()

        def greet(n, carry):
            @pl.when(n != self.me)
            def _():
                pl.semaphore_signal(sem, inc=1, device_id=self.coords(n), device_id_type=MESH)

            return carry

        lax.fori_loop(0, self.count, greet, 0)
        pl.semaphore_wait(sem, self.count - 1)


def exchange_images(at, src_of, dst_of, send_sems, recv_sems, local_sem):
    slots = 2 * at.ts

    def start():
        for i in range(slots):
            hi, t = i // at.ts, i % at.ts

            @pl.when(i != at.slot)
            def _():
                rcopy(
                    src_of(i),
                    dst_of(at.slot),
                    send_sems.at[i],
                    recv_sems.at[at.slot],
                    (at.f, hi * 2 + at.k, t),
                ).start()

            @pl.when(i == at.slot)
            def _():
                pltpu.make_async_copy(src_of(i), dst_of(i), local_sem).start()

    def wait():
        for i in range(slots):
            @pl.when(i != at.slot)
            def _():
                rcopy(src_of(i), dst_of(i), send_sems.at[i], recv_sems.at[i], (at.f, at.c, at.t)).wait()

            @pl.when(i == at.slot)
            def _():
                pltpu.make_async_copy(src_of(i), dst_of(i), local_sem).wait()

    return start, wait


def broadcast_messages(at, src_of, slot_of, send_sems, recv_sems, local_sem):
    def start():
        def each(n, carry):
            @pl.when(n != at.me)
            def _():
                rcopy(src_of(n), slot_of(at.me), send_sems.at[n], recv_sems.at[at.me], at.coords(n)).start()

            @pl.when(n == at.me)
            def _():
                pltpu.make_async_copy(src_of(n), slot_of(n), local_sem).start()

            return carry

        lax.fori_loop(0, at.count, each, 0)

    def wait():
        def each(n, carry):
            @pl.when(n != at.me)
            def _():
                rcopy(src_of(n), slot_of(n), send_sems.at[n], recv_sems.at[n], at.coords(n)).wait()

            @pl.when(n == at.me)
            def _():
                pltpu.make_async_copy(src_of(n), slot_of(n), local_sem).wait()

            return carry

        lax.fori_loop(0, at.count, each, 0)

    return start, wait


FORWARD_IN = ("xb", "gb", "s1", "s2", "s3", "sp", "cond", "wm", "idq", "idk")
FORWARD_OUT = (
    "w1", "w2", "w3", "x", "g", "normed1", "qpre", "kpre", "v", "qh", "kh", "att", "branch1",
    "middle", "normed2", "hpre", "hid", "bo", "lse", "top", "mod", "par", "gate2",
)


class Refs:
    pass


def bundle(keys, values):
    refs = Refs()
    for key, value in zip(keys, values, strict=True):
        setattr(refs, key, value)
    return refs


def normalize(values):
    centered = values - jnp.mean(values, axis=-1, keepdims=True)
    inverse = lax.rsqrt(jnp.mean(centered * centered, axis=-1, keepdims=True) + norm_epsilon)
    return centered * inverse, inverse


def nt(left, right):
    return lax.dot_general(left, right, (((1,), (1,)), ((), ())), preferred_element_type=f32)


def nn(left, right):
    return lax.dot_general(left, right, (((1,), (0,)), ((), ())), preferred_element_type=f32)


def head_inverse(values):
    squares = values * values
    rows = values.shape[0]
    first = lax.rsqrt(jnp.mean(squares[:, :HD], axis=-1, keepdims=True) + norm_epsilon)
    second = lax.rsqrt(jnp.mean(squares[:, HD:], axis=-1, keepdims=True) + norm_epsilon)
    lane = lax.broadcasted_iota(jnp.int32, (rows, 2 * HD), 1)
    return jnp.where(lane < HD, first, second)


gelu_a = math.sqrt(2.0 / math.pi)
gelu_b = 0.044715


def forward_kernel(fs, cs, ts, sent, padded, per, keys, *values):
    r = bundle(keys, values)
    at = Place(fs, cs, ts)
    width = 256
    tokens, features = r.xs.shape
    half = tokens // 2
    quarter = features // ts
    zero = jnp.zeros((padded - sent, features), bf16)
    for c in range(cs):
        r.xs[c * padded + sent : (c + 1) * padded, :] = zero
        r.gs[c * padded + sent : (c + 1) * padded, :] = zero
    at.barrier()

    def block_at(out):
        def dst(i):
            c = (i // ts) * 2 + at.k
            return out.at[
                pl.ds(pl.multiple_of(c * padded, padded), sent),
                pl.ds(pl.multiple_of(lax.rem(i, ts) * width, width), width),
            ]

        return dst

    x_start, x_wait = exchange_images(at, lambda i: r.xb.at[i], block_at(r.xs), r.x_send, r.x_recv, r.loc.at[0])
    g_start, g_wait = exchange_images(at, lambda i: r.gb.at[i], block_at(r.gs), r.g_send, r.g_recv, r.loc.at[1])

    items = [(r.parts, r.sp, None, r.sp.shape[0])]
    for full, shard in ((r.w1s, r.s1), (r.w2s, r.s2), (r.w3s, r.s3)):
        for col in range(0, GC, CHUNK):
            items.append((full, shard, slice(col, col + CHUNK), per))

    def slab(n, z, nz, f, hi, k=0, blocks=2):
        full, _, cols, size = items[n]
        row = pl.multiple_of(((f * 2 + hi) * 2 + k) * size, size)
        span = pl.ds(row, blocks * size)
        return full.at[pl.ds(z, nz), span, :] if cols is None else full.at[pl.ds(z, nz), span, cols]

    def shard_of(n, k):
        _, shard, cols, _ = items[n]
        return shard if cols is None else shard.at[k, :, cols]

    def core_pair(n):
        mine = slab(n, at.t, 1, at.f, at.hi, at.k, 1).at[0]
        theirs = slab(n, at.t, 1, at.f, at.hi, 1 - at.k, 1).at[0]
        keep = pltpu.make_async_copy(shard_of(n, at.k), mine, r.core_loc.at[n])
        out = functools.partial(rcopy, shard_of(n, 1 - at.k), mine, r.core_send.at[n], r.core_recv.at[n], at.sibling())
        inn = functools.partial(rcopy, shard_of(n, 1 - at.k), theirs, r.core_send.at[n], r.core_recv.at[n], at.sibling())
        return keep, out, inn

    def core_start(n):
        keep, out, _ = core_pair(n)
        keep.start()
        out().start()

    def core_wait(n):
        keep, _, inn = core_pair(n)
        keep.wait()
        inn().wait()

    def z_start(n):
        for s in range(1, ts):
            src = slab(n, at.t, 1, at.f, at.hi)
            rcopy(src, src, r.z_send.at[n, s], r.z_recv.at[n, s], at.zpeer(s)).start()

    def z_wait(n):
        for s in range(1, ts):
            src = slab(n, at.zfrom(s), 1, at.f, at.hi)
            rcopy(src, src, r.z_send.at[n, s], r.z_recv.at[n, s], at.zpeer(s)).wait()

    def xy_start(n):
        src = slab(n, 0, ts, at.f, at.hi)
        rcopy(src, src, r.ys_send.at[n], r.ys_recv.at[n], at.ypeer()).start()
        for s in range(1, fs):
            rcopy(src, src, r.xs_send.at[n, s], r.xs_recv.at[n, s], at.xpeer(s)).start()

    def xy_wait(n):
        src = slab(n, 0, ts, at.f, 1 - at.hi)
        rcopy(src, src, r.ys_send.at[n], r.ys_recv.at[n], at.ypeer()).wait()
        for s in range(1, fs):
            src = slab(n, 0, ts, at.xfrom(s), at.hi)
            rcopy(src, src, r.xs_send.at[n, s], r.xs_recv.at[n, s], at.xpeer(s)).wait()

    zh = ts // 2

    def fwd_start(n):
        for s in range(1, fs):
            src = slab(n, zh, zh, at.f, 1 - at.hi)
            rcopy(src, src, r.fx_send.at[n, s], r.fx_recv.at[n, s], at.xpeer(s)).start()
            src = slab(n, 0, zh, at.xfrom(s), at.hi)
            rcopy(src, src, r.fy_send.at[n, s], r.fy_recv.at[n, s], at.ypeer()).start()

    def fwd_wait(n):
        for s in range(1, fs):
            src = slab(n, zh, zh, at.xfrom(s), 1 - at.hi)
            rcopy(src, src, r.fx_send.at[n, s], r.fx_recv.at[n, s], at.xpeer(s)).wait()
            src = slab(n, 0, zh, at.xfrom(s), 1 - at.hi)
            rcopy(src, src, r.fy_send.at[n, s], r.fy_recv.at[n, s], at.ypeer()).wait()

    saved = []

    def save(src, out):
        copy = pltpu.make_async_copy(src, out, r.out_sem.at[len(saved)])
        copy.start()
        saved.append((src, out, len(saved)))

    last = len(items) - 1
    core_start(0)
    core_start(1)
    r.cond_slots[at.t] = r.cond[...]

    def cond_copy(s, slot):
        return rcopy(r.cond, r.cond_slots.at[slot], r.c_send.at[s], r.c_recv.at[s], at.zpeer(s))

    for s in range(1, ts):
        cond_copy(s, at.t).start()
    core_wait(0)
    core_wait(1)
    z_start(0)
    z_start(1)
    for n in range(2, last + 1):
        core_start(n)

    for s in range(1, ts):
        cond_copy(s, at.zfrom(s)).wait()
    cond = r.cond_slots[0]
    for z in range(1, ts):
        cond = cond + r.cond_slots[z]
    silu = (cond / (1.0 + jnp.exp(-cond))).astype(bf16)
    for j in range(6):
        r.part[:, j, :] = jnp.dot(silu, r.wm[:, j * width : (j + 1) * width], preferred_element_type=f32)

    def image_of(n):
        f, c, t = at.coords(n)
        return (f * 2 + c // 2) * ts + t

    m_start, m_wait = broadcast_messages(
        at, lambda n: r.part.at[image_of(n)], lambda n: r.msg.at[n], r.m_send, r.m_recv, r.loc.at[2]
    )
    m_start()
    for n in range(2, last + 1):
        core_wait(n)
    z_wait(0)
    xy_start(0)
    z_wait(1)
    xy_start(1)
    z_start(2)
    xy_wait(0)
    fwd_start(0)
    z_wait(2)
    x_start()
    xy_start(2)
    xy_wait(1)
    fwd_start(1)
    m_wait()
    fwd_wait(0)

    blocks = fs * cs
    rows_small = r.sp.shape[0]

    def small_sum(n, carry):
        return carry + r.parts[:, pl.ds(pl.multiple_of(n * rows_small, rows_small), rows_small), :].astype(f32)

    r.psum[...] = lax.fori_loop(0, blocks, small_sum, jnp.zeros(r.psum.shape, f32))
    for z in range(ts):

        def mod_sum(n, carry):
            return carry + r.msg[n * ts + z]

        total = lax.fori_loop(0, blocks, mod_sum, jnp.zeros((8, width), f32))
        for j in range(6):
            for h in range(2):
                value = total[j : j + 1, h * 128 : (h + 1) * 128] + r.psum[z, 2 * j + h : 2 * j + h + 1, :]
                r.mods[j : j + 1, z * width + h * 128 : z * width + (h + 1) * 128] = value.astype(bf16).astype(f32)
                if j < 2:
                    row = r.psum[z, 20 + 2 * j + h : 21 + 2 * j + h, :]
                    r.mods[6 + j : 7 + j, z * width + h * 128 : z * width + (h + 1) * 128] = row

    def mod(j):
        return r.mods[j : j + 1, :]

    def own_row(z, start):
        return r.psum[z, pl.ds(start + at.k, 1), :]

    x_wait()

    def sib_pair(buf, send, recv, hi):
        mine = buf.at[pl.ds(pl.multiple_of((hi * 2 + at.k) * padded, padded), sent), :]
        theirs = buf.at[pl.ds(pl.multiple_of((hi * 2 + 1 - at.k) * padded, padded), sent), :]
        return (
            functools.partial(rcopy, mine, mine, send.at[hi], recv.at[hi], at.sibling()),
            functools.partial(rcopy, theirs, theirs, send.at[hi], recv.at[hi], at.sibling()),
        )

    for hi in range(2):
        sib_pair(r.xs, r.sib_send, r.sib_recv, hi)[0]().start()
    z_start(3)
    xy_wait(2)
    fwd_start(2)
    for hi in range(2):
        sib_pair(r.xs, r.sib_send, r.sib_recv, hi)[1]().wait()
    save(r.xs, r.x)

    step = 64

    def norm_tile(src, dst, shift, scale):
        def tile(n, carry):
            span = pl.ds(pl.multiple_of(n * step, step), step)
            normal, _ = normalize(src[span, :].astype(f32))
            dst[span, :] = (normal * (1.0 + mod(scale)) + mod(shift)).astype(bf16)
            return carry

        lax.fori_loop(0, tokens // step, tile, 0)

    norm_tile(r.xs, r.n1, 0, 1)
    save(r.n1, r.normed1)
    z_wait(3)
    xy_start(3)
    z_start(4)
    fwd_wait(1)
    fwd_wait(2)
    save(r.w1s, r.w1)

    def qkv(i, carry):
        z = i // 2
        span = pl.ds(pl.multiple_of(lax.rem(i, 2) * half, half), half)
        raw = nn(r.n1[span, :], r.w1s[z, :, : 3 * 128])
        q = raw[:, :128] + own_row(z, 12)
        k = raw[:, 128:256]
        r.qp[z, span, :] = q
        r.kp[z, span, :] = k
        r.vs[z, span, :] = (raw[:, 256:] + own_row(z, 14)).astype(bf16)
        r.qhs[z, span, :] = (q * head_inverse(q) * own_row(z, 16)).astype(bf16)
        r.khs[z, span, :] = (k * head_inverse(k) * own_row(z, 18)).astype(bf16)
        return carry

    lax.fori_loop(0, 2 * ts, qkv, 0)
    for src, out in ((r.qp, r.qpre), (r.kp, r.kpre), (r.vs, r.v), (r.qhs, r.qh), (r.khs, r.kh)):
        save(src, out)
    z_wait(4)
    xy_start(4)
    z_start(5)
    xy_wait(3)
    fwd_start(3)

    qt = 256

    def attend(z):
        v_t = r.vs[z].T
        tops = [jnp.full((1, qt), masked_score, f32) for _ in range(2)]

        def tile(n, tops):
            span = pl.ds(pl.multiple_of(n * qt, qt), qt)
            allowed = r.idk[...] <= r.idq[:, span]
            outs, peaks = [], []
            for h in range(2):
                lanes = slice(h * HD, (h + 1) * HD)
                s = nt(r.khs[z, :, lanes], r.qhs[z, span, lanes] * 0.125)
                s = jnp.where(allowed, s, masked_score)
                peak = jnp.max(s, axis=0, keepdims=True)
                e = jnp.exp(s - peak)
                total = jnp.sum(e, axis=0, keepdims=True)
                r.lses[z, h : h + 1, span] = peak + jnp.log(total)
                p = (e * (1.0 / total)).astype(bf16)
                outs.append(nn(v_t[h * HD : (h + 1) * HD, :], p))
                peaks.append(jnp.maximum(tops[h], peak))
            r.atts[z, span, :] = jnp.concatenate(outs, axis=0).T.astype(bf16)
            return peaks

        tops = lax.fori_loop(0, tokens // qt, tile, tops)
        for h in range(2):
            r.tops[z, h : h + 1, :] = jnp.broadcast_to(jnp.max(tops[h], axis=1, keepdims=True), (1, 128))

    attend(0)
    z_wait(5)
    xy_start(5)
    z_start(6)
    xy_wait(4)
    fwd_start(4)
    attend(1)
    z_wait(6)
    xy_start(6)
    g_start()
    xy_wait(5)
    fwd_start(5)
    attend(2)
    fwd_wait(3)
    attend(3)
    for src, out in ((r.atts, r.att), (r.lses, r.lse), (r.tops, r.top)):
        save(src, out)

    def pair(e, n):
        span = pl.ds(n * half, half)
        return rcopy(
            r.sendbuf.at[span, :], r.recvs.at[e, span, :], r.e_send.at[e, n], r.e_recv.at[e, n], at.sibling()
        )

    for n in range(2):
        span = slice(n * half, (n + 1) * half)
        for c in range(2):
            cols = slice(c * 512, (c + 1) * 512)
            acc = nt(r.atts[0, span, :], r.w1s[0, cols, 384:])
            for z in range(1, ts):
                acc = acc + nt(r.atts[z, span, :], r.w1s[z, cols, 384:])
            r.sendbuf[span, cols] = acc.astype(bf16)
        pair(0, n).start()
    xy_wait(6)
    fwd_start(6)
    for n in range(2):
        pair(0, n).wait()

        def tile(i, carry):
            span = pl.ds(pl.multiple_of(n * half + i * step, step), step)
            branch = r.sendbuf[span, :].astype(f32) + r.recvs[0, span, :].astype(f32) + mod(6)
            r.b1[span, :] = branch.astype(bf16)
            middle = (r.xs[span, :].astype(f32) + mod(2) * branch).astype(bf16)
            r.mid[span, :] = middle
            normal, _ = normalize(middle.astype(f32))
            r.n2[span, :] = (normal * (1.0 + mod(4)) + mod(3)).astype(bf16)
            return carry

        lax.fori_loop(0, half // step, tile, 0)
    for src, out in ((r.b1, r.branch1), (r.mid, r.middle), (r.n2, r.normed2)):
        save(src, out)

    def up_part(c):
        cols = slice(c * CHUNK, (c + 1) * CHUNK)

        def body(i, carry):
            z = i // 2
            span = pl.ds(pl.multiple_of(lax.rem(i, 2) * half, half), half)
            pre = nn(r.n2[span, :], r.w2s[z, :, cols])
            bias = [r.psum[z, pl.ds(24 + 4 * at.k + 2 * c + j, 1), :] for j in range(2)]
            pre = pre + jnp.concatenate(bias, axis=1)
            r.hp[z, span, cols] = pre
            inner = jnp.tanh(gelu_a * (pre + gelu_b * pre * pre * pre))
            r.hs[z, span, cols] = (0.5 * pre * (1.0 + inner)).astype(bf16)
            return carry

        lax.fori_loop(0, 2 * ts, body, 0)

    up_part(0)
    fwd_wait(4)
    save(r.w2s, r.w2)
    up_part(1)
    save(r.hp, r.hpre)
    save(r.hs, r.hid)
    g_wait()
    for hi in range(2):
        sib_pair(r.gs, r.gsib_send, r.gsib_recv, hi)[0]().start()

    def down_part(c, first):
        cols = slice(c * CHUNK, (c + 1) * CHUNK)
        for n in range(2):
            span = slice(n * half, (n + 1) * half)
            for m in range(2):
                rows = slice(m * 512, (m + 1) * 512)
                acc = nt(r.hs[0, span, cols], r.w3s[0, rows, cols])
                for z in range(1, ts):
                    acc = acc + nt(r.hs[z, span, cols], r.w3s[z, rows, cols])
                if first:
                    r.acc[span, rows] = acc
                else:
                    r.sendbuf[span, rows] = (r.acc[span, rows] + acc).astype(bf16)
            if not first:
                pair(1, n).start()

    fwd_wait(5)
    down_part(0, True)
    fwd_wait(6)
    save(r.w3s, r.w3)
    down_part(1, False)
    for hi in range(2):
        sib_pair(r.gs, r.gsib_send, r.gsib_recv, hi)[1]().wait()
    save(r.gs, r.g)
    for n in range(2):
        pair(1, n).wait()

        def tile(i, carry):
            span = pl.ds(pl.multiple_of(n * half + i * step, step), step)
            branch = r.sendbuf[span, :].astype(f32) + r.recvs[1, span, :].astype(f32) + mod(7)
            r.bos[span, :] = (r.mid[span, :].astype(f32) + mod(5) * branch).astype(bf16)
            product = r.gs[span, :].astype(f32) * branch
            return carry + jnp.sum(product.reshape(step // 8, 8, features), axis=0)

        part = lax.fori_loop(0, half // step, tile, jnp.zeros((8, features), f32))
        if n == 0:
            r.gates[...] = part
        else:
            r.gates[...] += part
    for src, out in ((r.bos, r.bo), (r.gates, r.gate2), (r.mods, r.mod), (r.psum, r.par)):
        save(src, out)
    for src, out, n in saved:
        pltpu.make_async_copy(src, out, r.out_sem.at[n]).wait()


def run_forward(fs, cs, ts, sent, padded, per, every, args):
    tokens, features = cs * padded, ts * 256
    sds = jax.ShapeDtypeStruct
    big = (ts, features, GC)
    outs = {
        "w1": (big, bf16), "w2": (big, bf16), "w3": (big, bf16),
        "x": ((tokens, features), bf16), "g": ((tokens, features), bf16), "normed1": ((tokens, features), bf16),
        "qpre": ((ts, tokens, 128), f32), "kpre": ((ts, tokens, 128), f32),
        "v": ((ts, tokens, 128), bf16), "qh": ((ts, tokens, 128), bf16), "kh": ((ts, tokens, 128), bf16),
        "att": ((ts, tokens, 128), bf16), "branch1": ((tokens, features), bf16),
        "middle": ((tokens, features), bf16), "normed2": ((tokens, features), bf16),
        "hpre": ((ts, tokens, GC), f32), "hid": ((ts, tokens, GC), bf16), "bo": ((tokens, features), bf16),
        "lse": ((ts, 2, tokens), f32), "top": ((ts, 2, 128), f32), "mod": ((8, features), f32),
        "par": ((ts, 32, 128), f32), "gate2": ((8, features), f32),
    }
    vm, dma = pltpu.VMEM, pltpu.SemaphoreType.DMA
    local = dict(
        w1s="w1", w2s="w2", w3s="w3", xs="x", gs="g", n1="normed1", qp="qpre", kp="kpre", vs="v", qhs="qh",
        khs="kh", atts="att", b1="branch1", mid="middle", n2="normed2", hp="hpre", hs="hid", bos="bo",
        lses="lse", tops="top", mods="mod", psum="par", gates="gate2",
    )
    scratch = {k: vm(*outs[v]) for k, v in local.items()}
    items = 1 + 3 * (GC // CHUNK)
    scratch.update(
        sendbuf=vm((tokens, features), bf16), recvs=vm((2, tokens, features), bf16), acc=vm((tokens, features), f32),
        cond_slots=vm((ts, every, per), f32), part=vm((every, 8, 256), f32),
        msg=vm((fs * cs * ts, 8, 256), f32), parts=vm((ts, fs * cs * 32, 128), bf16),
        x_send=dma((2 * ts,)), x_recv=dma((2 * ts,)), g_send=dma((2 * ts,)), g_recv=dma((2 * ts,)), loc=dma((3,)),
        sib_send=dma((2,)), sib_recv=dma((2,)), gsib_send=dma((2,)), gsib_recv=dma((2,)),
        c_send=dma((ts,)), c_recv=dma((ts,)), m_send=dma((fs * cs * ts,)), m_recv=dma((fs * cs * ts,)),
        core_send=dma((items,)), core_recv=dma((items,)), core_loc=dma((items,)),
        z_send=dma((items, ts)), z_recv=dma((items, ts)),
        xs_send=dma((items, fs)), xs_recv=dma((items, fs)), ys_send=dma((items,)), ys_recv=dma((items,)),
        fx_send=dma((items, fs)), fx_recv=dma((items, fs)), fy_send=dma((items, fs)), fy_recv=dma((items, fs)),
        e_send=dma((2, 2)), e_recv=dma((2, 2)), out_sem=dma((len(outs),)),
    )
    anywhere, on_chip = pl.BlockSpec(memory_space=pl.ANY), pl.BlockSpec(memory_space=vm)
    results = pl.pallas_call(
        functools.partial(
            forward_kernel, fs, cs, ts, sent, padded, per, FORWARD_IN + FORWARD_OUT + tuple(scratch)
        ),
        name="forward",
        out_shape=tuple(sds(*outs[k]) for k in FORWARD_OUT),
        in_specs=[anywhere] * 6 + [on_chip] * 4,
        out_specs=(anywhere,) * len(FORWARD_OUT),
        scratch_shapes=list(scratch.values()),
        compiler_params=pltpu.CompilerParams(
            collective_id=0, has_side_effects=True, vmem_limit_bytes=62 << 20
        ),
    )(*[args[k] for k in FORWARD_IN])
    return bundle(FORWARD_OUT, results)


def segment_mean(values):
    first = jnp.mean(values[:, :HD], axis=-1, keepdims=True)
    second = jnp.mean(values[:, HD:], axis=-1, keepdims=True)
    lane = lax.broadcasted_iota(jnp.int32, values.shape, 1)
    return jnp.where(lane < HD, first, second)


def attend_back(z, r, query_gain, key_gain):
    tokens = r.vs.shape[1]
    qt = 256
    r.dka[...] = jnp.zeros_like(r.dka)
    r.dva[...] = jnp.zeros_like(r.dva)
    k_t = r.khs[z].T

    def tile(n, carry):
        span = pl.ds(pl.multiple_of(n * qt, qt), qt)
        allowed = r.idk[...] <= r.idq[:, span]
        outs = []
        for h in range(2):
            lanes = slice(h * HD, (h + 1) * HD)
            qh, da = r.qhs[z, span, lanes] * 0.125, r.das[z, span, lanes]
            s = jnp.where(allowed, nt(r.khs[z, :, lanes], qh), masked_score)
            p = jnp.exp(s - r.lses[z, h : h + 1, span])
            dp = nt(r.vs[z, :, lanes], da)
            centre = jnp.sum(p * dp, axis=0, keepdims=True)
            ds = (p * (dp - centre)).astype(bf16)
            r.dva[h] += nn(p.astype(bf16), da)
            r.dka[h] += nn(ds, qh)
            outs.append(nn(k_t[h * HD : (h + 1) * HD, :], ds))
        r.dqa[span, :] = jnp.concatenate(outs, axis=0).T * 0.125
        return carry

    lax.fori_loop(0, tokens // qt, tile, 0)

    def finish(n, sums):
        span = pl.ds(pl.multiple_of(n * qt, qt), qt)
        dk = jnp.concatenate([r.dka[0, span, :], r.dka[1, span, :]], axis=1)
        dv = jnp.concatenate([r.dva[0, span, :], r.dva[1, span, :]], axis=1).astype(bf16)
        r.dqkv[z, span, 256:] = dv
        results = [None, None, None, jnp.sum(dv.astype(f32), axis=0, keepdims=True)]
        for i, (raw_ref, gain, delta) in enumerate(((r.qp, query_gain, r.dqa[span, :]), (r.kp, key_gain, dk))):
            raw = raw_ref[z, span, :]
            inverse = head_inverse(raw)
            results[i] = jnp.sum(delta * raw * inverse, axis=0, keepdims=True)
            t = delta * gain
            out = (inverse * t - raw * (inverse * inverse * inverse) * segment_mean(t * raw)).astype(bf16)
            r.dqkv[z, span, i * 128 : (i + 1) * 128] = out
            if i == 0:
                results[2] = jnp.sum(out.astype(f32), axis=0, keepdims=True)
        return [a + b for a, b in zip(sums, results)]

    sums = lax.fori_loop(0, tokens // qt, finish, [jnp.zeros((1, 128), f32)] * 4)
    for row, value in enumerate((sums[2], sums[3], sums[0], sums[1])):
        r.vec[z, row : row + 1, :] = value


BACKWARD_IN = (
    "w1", "w2", "w3", "x", "g", "normed1", "qpre", "kpre", "v", "qh", "kh", "att", "branch1",
    "middle", "normed2", "hpre", "hid", "bo", "lse", "top", "mod", "par", "gate2", "idq", "idk",
)
BACKWARD_OUT = ("o1", "o2", "o3", "dxo", "boo", "mail")


def backward_kernel(fs, cs, ts, sent, padded, per, keys, *values):
    r = bundle(keys, values)
    at = Place(fs, cs, ts)
    width = 256
    tokens, features = r.gs.shape
    half = tokens // 2
    step = 64
    at.barrier()

    pending = {}
    order = []

    def load(name, src, dst):
        pltpu.make_async_copy(src, dst, r.in_sem.at[len(order)]).start()
        pending[name] = (src, dst, len(order))
        order.append(name)

    def need(*wanted):
        for name in wanted:
            src, dst, n = pending.pop(name)
            pltpu.make_async_copy(src, dst, r.in_sem.at[n]).wait()

    load("g", r.g, r.gs)
    load("mod", r.mod, r.mods)
    load("hid", r.hid, r.hs)
    load("w3", r.w3, r.wa)
    load("hp0", r.hpre.at[0], r.hp.at[0])
    load("n2", r.normed2, r.nn_)
    load("hp1", r.hpre.at[1], r.hp.at[1])
    load("w2", r.w2, r.wb)
    load("mid", r.middle, r.mid)
    load("b1", r.branch1, r.b1)
    load("att", r.att, r.atts)
    load("par", r.par, r.psum)
    for name, src, dst in (
        ("qh", r.qh, r.qhs), ("kh", r.kh, r.khs), ("v", r.v, r.vs), ("lse", r.lse, r.lses),
        ("qp", r.qpre, r.qp), ("kp", r.kpre, r.kp), ("top", r.top, r.tops), ("gate2", r.gate2, r.gates),
    ):
        load(name, src, dst)

    def block_of(ref):
        def src(i):
            c = (i // ts) * 2 + at.k
            return ref.at[
                pl.ds(pl.multiple_of(c * padded, padded), sent),
                pl.ds(pl.multiple_of(lax.rem(i, ts) * width, width), width),
            ]

        return src

    bo_start, bo_wait = exchange_images(
        at, block_of(r.bo), lambda i: r.boo.at[i], r.bo_send, r.bo_recv, r.loc.at[1]
    )
    dx_start, dx_wait = exchange_images(
        at, block_of(r.dd), lambda i: r.dxo.at[i], r.dx_send, r.dx_recv, r.loc.at[0]
    )
    bo_start()

    hc = GC // 2
    outs = (r.o1, r.o2, r.o3)
    x_part, y_part = slice(hc, GC), slice(0, hc)

    def slot(g, z):
        return z + (ts if g == 1 else 0)

    def rows(f, hi):
        return pl.ds(pl.multiple_of((f * 2 + hi) * 2 * per, 2 * per), 2 * per)

    def far(s):
        return lax.rem(at.f + s, fs)

    def stage_one(g, z, s):
        n, d = g * ts + z, slot(g, z)
        return (
            rcopy(
                r.d.at[d, rows(far(s), 1 - at.hi), y_part], r.ry1.at[n, s - 1],
                r.y1_send.at[n, s], r.y1_recv.at[n, s], at.ypeer(),
            ),
            rcopy(
                r.d.at[d, rows(far(s), 1 - at.hi), x_part], r.rx1.at[n, s - 1],
                r.x1_send.at[n, s], r.x1_recv.at[n, s], at.xpeer(s),
            ),
        )

    def stage_two(g, z):
        n, d = g * ts + z, slot(g, z)
        copies = [
            rcopy(
                r.d.at[d, rows(far(s), at.hi), :], r.rx2.at[n, s - 1],
                r.x2_send.at[n, s], r.x2_recv.at[n, s], at.xpeer(s),
            )
            for s in range(1, fs)
        ]
        copies.append(
            rcopy(r.d.at[d, rows(at.f, 1 - at.hi), :], r.ry2.at[n], r.y2_send.at[n], r.y2_recv.at[n], at.ypeer())
        )
        return copies

    def rs_a(g, z):
        for s in range(1, fs):
            for copy in stage_one(g, z, s):
                copy.start()

    def rs_b(g, z):
        n, d = g * ts + z, slot(g, z)
        for s in range(1, fs):
            for copy in stage_one(g, z, s):
                copy.wait()
        for s in range(1, fs):
            span = rows(far(s), at.hi)
            r.d[d, span, y_part] = (r.d[d, span, y_part].astype(f32) + r.ry1[n, s - 1].astype(f32)).astype(bf16)
        span = rows(at.f, 1 - at.hi)
        value = r.d[d, span, x_part].astype(f32)
        for s in range(1, fs):
            value = value + r.rx1[n, s - 1].astype(f32)
        r.d[d, span, x_part] = value.astype(bf16)
        for copy in stage_two(g, z):
            copy.start()

    def to_owner(g, z):
        s = lax.rem(at.t + ts - z, ts)
        index = jnp.maximum(s, 1)
        return rcopy(
            r.d.at[slot(g, z), rows(at.f, at.hi), :], r.rz.at[g, index - 1],
            r.z_send.at[g * ts + z], r.z_recv.at[g, index], (at.f, at.c, z),
        )

    def rs_c(g, z):
        n, d = g * ts + z, slot(g, z)
        for copy in stage_two(g, z):
            copy.wait()
        span = rows(at.f, at.hi)
        for part in (y_part, x_part):
            value = r.d[d, span, part].astype(f32) + r.ry2[n, :, part].astype(f32)
            for s in range(1, fs):
                value = value + r.rx2[n, s - 1, :, part].astype(f32)
            r.d[d, span, part] = value.astype(bf16)

        @pl.when(at.t != z)
        def _():
            to_owner(g, z).start()

    def pair_sum(g):
        src = r.total.at[pl.ds(pl.multiple_of((1 - at.k) * per, per), per)]
        own = r.total.at[pl.ds(pl.multiple_of(at.k * per, per), per)]
        keep = pltpu.make_async_copy(own, outs[g].at[at.k], r.k_loc.at[g])
        out = functools.partial(rcopy, src, outs[g].at[at.k], r.k_send.at[g], r.k_recv.at[g], at.sibling())
        inn = functools.partial(rcopy, src, outs[g].at[1 - at.k], r.k_send.at[g], r.k_recv.at[g], at.sibling())
        return keep, out, inn

    def pair_wait(g):
        keep, _, inn = pair_sum(g)
        keep.wait()
        inn().wait()

    def rs_e(g):
        for z in range(ts):

            @pl.when(at.t != z)
            def _():
                to_owner(g, z).wait_send()

        for s in range(1, ts):
            rcopy(
                r.rz.at[g, s - 1], r.rz.at[g, s - 1], r.z_send.at[g * ts], r.z_recv.at[g, s], at.zpeer(s)
            ).wait_recv()
        base = ts if g == 1 else 0
        for part in (y_part, x_part):
            value = r.d[base + at.t, rows(at.f, at.hi), part].astype(f32)
            for s in range(1, ts):
                value = value + r.rz[g, s - 1, :, part].astype(f32)
            r.total[:, part] = value
        keep, out, _ = pair_sum(g)
        keep.start()
        out().start()

    def mod(j):
        return r.mods[j : j + 1, :]

    def own_row(z, start):
        return r.psum[z, pl.ds(start + at.k, 1), :]

    def transpose(src):
        def tile(n, carry):
            span = pl.ds(pl.multiple_of(n * 128, 128), 128)
            r.xt[:, span] = src[span, :].T
            return carry

        lax.fori_loop(0, tokens // 128, tile, 0)

    def grad_into(d, cols, right):
        def tile(m, carry):
            span = pl.ds(pl.multiple_of(m * 256, 256), 256)
            r.d[d, span, cols] = nn(r.xt[span, :], right()).astype(bf16)
            return carry

        lax.fori_loop(0, features // 256, tile, 0)

    def eight(values):
        return jnp.sum(values.reshape(values.shape[0] // 8, 8, values.shape[1]), axis=0)

    def collapse(values):
        return jnp.sum(values, axis=0, keepdims=True)

    def pair(e, n):
        span = pl.ds(n * half, half)
        return rcopy(
            r.sendbuf.at[span, :], r.recvs.at[e, span, :], r.e_send.at[e, n], r.e_recv.at[e, n], at.sibling()
        )

    need("g", "mod")

    def delta_tile(n, carry):
        span = pl.ds(pl.multiple_of(n * step, step), step)
        delta = (r.gs[span, :].astype(f32) * mod(5)).astype(bf16)
        r.dd[span, :] = delta
        return carry + eight(delta.astype(f32))

    zeros = jnp.zeros((8, features), f32)
    down_bias = collapse(lax.fori_loop(0, tokens // step, delta_tile, zeros))
    transpose(r.dd)
    need("hid")

    def grad_down(z):
        grad_into(slot(2, z), slice(None), lambda: r.hs[z])

    def back_up(z):
        need("hp%d" % z)

        def tile(n, carry):
            span = pl.ds(pl.multiple_of(n * half, half), half)
            hidden_delta = nn(r.dd[span, :], r.wa[z])
            pre = r.hp[z % 2, span, :]
            inner = jnp.tanh(gelu_a * (pre + gelu_b * pre * pre * pre))
            slope = 0.5 * (1.0 + inner) + 0.5 * pre * (1.0 - inner * inner) * (
                gelu_a * (1.0 + 3.0 * gelu_b * pre * pre)
            )
            delta = (hidden_delta * slope).astype(bf16)
            r.hs[z, span, :] = delta
            return carry + eight(delta.astype(f32))

        r.ubs[z] = collapse(lax.fori_loop(0, 2, tile, jnp.zeros((8, GC), f32)))
        if z + 2 < ts:
            load("hp%d" % (z + 2), r.hpre.at[z + 2], r.hp.at[z % 2])

    def grad_up(z):
        grad_into(slot(1, z), slice(None), lambda: r.hs[z])

    grad_down(0)
    rs_a(2, 0)
    grad_down(1)
    rs_a(2, 1)
    grad_down(2)
    rs_a(2, 2)
    rs_b(2, 0)
    grad_down(3)
    rs_a(2, 3)
    need("n2", "w3")
    transpose(r.nn_)
    load("n1", r.normed1, r.nn_)
    rs_b(2, 1)
    back_up(0)
    rs_b(2, 2)
    grad_up(0)
    rs_a(1, 0)
    rs_c(2, 0)
    back_up(1)
    rs_b(2, 3)
    grad_up(1)
    rs_a(1, 1)
    rs_c(2, 1)
    back_up(2)
    rs_b(1, 0)
    grad_up(2)
    rs_a(1, 2)
    rs_c(2, 2)
    back_up(3)
    load("w1", r.w1, r.wa)
    rs_b(1, 1)
    grad_up(3)
    rs_a(1, 3)
    rs_c(2, 3)
    need("w2")
    for n in range(2):
        span = slice(n * half, (n + 1) * half)
        for m in range(2):
            cols = slice(m * 512, (m + 1) * 512)
            acc = nt(r.hs[0, span, :], r.wb[0, cols, :])
            for z in range(1, ts):
                acc = acc + nt(r.hs[z, span, :], r.wb[z, cols, :])
            r.sendbuf[span, cols] = acc.astype(bf16)
        pair(0, n).start()
        rs_b(1, 2 + n)
    rs_c(1, 0)
    need("mid", "b1")

    def norm_two(n):
        def tile(i, sums):
            span = pl.ds(pl.multiple_of(n * half + i * step, step), step)
            incoming = r.sendbuf[span, :].astype(f32) + r.recvs[0, span, :].astype(f32)
            normal, inverse = normalize(r.mid[span, :].astype(f32))
            e = incoming * (1.0 + mod(4))
            mean_e = jnp.mean(e, axis=-1, keepdims=True)
            mean_en = jnp.mean(e * normal, axis=-1, keepdims=True)
            delta = r.gs[span, :].astype(f32) + (e - mean_e - normal * mean_en) * inverse
            r.hp[0, span, :] = delta[:, :512]
            r.hp[1, span, :] = delta[:, 512:]
            low = (delta * mod(2)).astype(bf16)
            r.dd[span, :] = low
            parts = (incoming, incoming * normal, delta * r.b1[span, :].astype(f32), low.astype(f32))
            return [a + eight(b) for a, b in zip(sums, parts)]

        return tile

    sums = [zeros] * 4
    for n in range(2):
        pair(0, n).wait()
        sums = lax.fori_loop(0, half // step, norm_two(n), sums)
    shift_two, scale_two, gate_one, output_bias = (collapse(v) for v in sums)
    load("x", r.x, r.gs)
    rs_c(1, 1)

    transpose(r.dd)
    need("att", "w1")
    rs_e(2)
    for z in range(ts):
        grad_into(slot(0, z), slice(384, GC), lambda: r.atts[z])

        def tile(n, carry):
            span = pl.ds(pl.multiple_of(n * half, half), half)
            r.das[z, span, :] = nn(r.dd[span, :], r.wa[z, :, 384:]).astype(bf16)
            return carry

        lax.fori_loop(0, 2, tile, 0)
    rs_c(1, 2)
    need("n1")
    transpose(r.nn_)
    need("par", "qh", "kh", "v", "lse", "qp", "kp", "top", "gate2")
    for z in range(ts):
        attend_back(z, r, own_row(z, 16), own_row(z, 18))
        grad_into(slot(0, z), slice(0, 384), lambda: r.dqkv[z])
        rs_a(0, z)
        if z == 0:
            rs_c(1, 3)
        if z >= 1:
            rs_b(0, z - 1)
        if z == 2:
            pair_wait(2)
            rs_e(1)
        if z >= 2:
            rs_c(0, z - 2)
    for n in range(2):
        span = slice(n * half, (n + 1) * half)
        for m in range(2):
            cols = slice(m * 512, (m + 1) * 512)
            acc = nt(r.dqkv[0, span, :], r.wa[0, cols, :384])
            for z in range(1, ts):
                acc = acc + nt(r.dqkv[z, span, :], r.wa[z, cols, :384])
            r.sendbuf[span, cols] = acc.astype(bf16)
        pair(1, n).start()
    rs_b(0, ts - 1)
    need("x")

    def norm_one(n):
        def tile(i, sums):
            span = pl.ds(pl.multiple_of(n * half + i * step, step), step)
            incoming = r.sendbuf[span, :].astype(f32) + r.recvs[1, span, :].astype(f32)
            normal, inverse = normalize(r.gs[span, :].astype(f32))
            e = incoming * (1.0 + mod(1))
            mean_e = jnp.mean(e, axis=-1, keepdims=True)
            mean_en = jnp.mean(e * normal, axis=-1, keepdims=True)
            middle_delta = jnp.concatenate([r.hp[0, span, :], r.hp[1, span, :]], axis=1)
            r.dd[span, :] = (middle_delta + (e - mean_e - normal * mean_en) * inverse).astype(bf16)
            return [a + eight(b) for a, b in zip(sums, (incoming, incoming * normal))]

        return tile

    sums = [zeros] * 2
    for n in range(2):
        pair(1, n).wait()
        sums = lax.fori_loop(0, half // step, norm_one(n), sums)
    dx_start()
    shift_one, scale_one = (collapse(v) for v in sums)

    gate_two = collapse(r.gates[...])
    tops = (
        shift_one, scale_one, gate_one, shift_two, scale_two, gate_two, output_bias, down_bias,
    )
    for z in range(ts):
        lanes = slice(z * width, (z + 1) * width)
        for row, value in enumerate(tops):
            r.small[z, row : row + 1, :] = value[:, lanes]
        for row in range(2):
            r.small[z, 8 + row : 9 + row, :128] = r.vec[z, 2 * row : 2 * row + 1, :]
            r.small[z, 8 + row : 9 + row, 128:] = r.vec[z, 2 * row + 1 : 2 * row + 2, :]
            r.small[z, 10 + row : 11 + row, :] = r.ubs[z, :, row * width : (row + 1) * width]
            r.small[z, 12:13, row * 128 : (row + 1) * 128] = r.tops[z, row : row + 1, :]
        r.small[z, 13:16, :] = jnp.zeros((3, width), f32)

    def message_slot(n):
        f, c, t = at.coords(n)
        return r.mail.at[(f * 2 + c // 2) * ts + t, lax.rem(c, 2)]

    m_start, m_wait = broadcast_messages(
        at, lambda n: r.small.at[lax.rem(n, ts)], message_slot, r.m_send, r.m_recv, r.loc.at[2]
    )
    m_start()
    rs_c(0, ts - 2)
    rs_c(0, ts - 1)
    pair_wait(1)
    rs_e(0)
    pair_wait(0)
    m_wait()
    bo_wait()
    dx_wait()


def run_backward(fs, cs, ts, sent, padded, per, every, args):
    tokens, features = cs * padded, ts * 256
    f1 = max(fs - 1, 1)
    chunks = 3 * ts
    vm, dma, sds = pltpu.VMEM, pltpu.SemaphoreType.DMA, jax.ShapeDtypeStruct
    rows, cube = (tokens, features), (ts, tokens, 128)
    scratch = dict(
        gs=vm(rows, bf16), hs=vm((ts, tokens, GC), bf16), hp=vm((2, tokens, GC), f32),
        wa=vm((ts, features, GC), bf16), wb=vm((ts, features, GC), bf16),
        nn_=vm(rows, bf16), mid=vm(rows, bf16), b1=vm(rows, bf16), atts=vm(cube, bf16),
        qhs=vm(cube, bf16), khs=vm(cube, bf16), vs=vm(cube, bf16), lses=vm((ts, 2, tokens), f32),
        qp=vm(cube, f32), kp=vm(cube, f32), tops=vm((ts, 2, 128), f32), gates=vm((8, features), f32),
        mods=vm((8, features), f32), psum=vm((ts, 32, 128), f32),
        dd=vm(rows, bf16), xt=vm((features, tokens), bf16), sendbuf=vm(rows, bf16), recvs=vm((2, *rows), bf16),
        das=vm(cube, bf16), dqkv=vm((ts, tokens, 384), bf16), vec=vm((ts, 4, 128), f32), ubs=vm((ts, 1, GC), f32),
        dqa=vm((tokens, 128), f32), dka=vm((2, tokens, HD), f32), dva=vm((2, tokens, HD), f32),
        small=vm((ts, 16, 256), f32),
        d=vm((2 * ts, features, GC), bf16),
        ry1=vm((chunks, f1, 2 * per, GC // 2), bf16), rx1=vm((chunks, f1, 2 * per, GC // 2), bf16),
        rx2=vm((chunks, f1, 2 * per, GC), bf16), ry2=vm((chunks, 2 * per, GC), bf16),
        rz=vm((3, ts - 1, 2 * per, GC), bf16), total=vm((2 * per, GC), f32),
        in_sem=dma((32,)), loc=dma((3,)),
        bo_send=dma((2 * ts,)), bo_recv=dma((2 * ts,)), dx_send=dma((2 * ts,)), dx_recv=dma((2 * ts,)),
        y1_send=dma((chunks, fs)), y1_recv=dma((chunks, fs)), x1_send=dma((chunks, fs)), x1_recv=dma((chunks, fs)),
        x2_send=dma((chunks, fs)), x2_recv=dma((chunks, fs)), y2_send=dma((chunks,)), y2_recv=dma((chunks,)),
        z_send=dma((chunks,)), z_recv=dma((3, ts)), k_send=dma((3,)), k_recv=dma((3,)), k_loc=dma((3,)),
        e_send=dma((2, 2)), e_recv=dma((2, 2)), m_send=dma((fs * cs * ts,)), m_recv=dma((fs * cs * ts,)),
    )
    anywhere, on_chip = pl.BlockSpec(memory_space=pl.ANY), pl.BlockSpec(memory_space=vm)
    share = sds((2, per, GC), f32)
    blocks = sds((2 * ts, sent, 256), bf16)
    results = pl.pallas_call(
        functools.partial(
            backward_kernel, fs, cs, ts, sent, padded, per, BACKWARD_IN + BACKWARD_OUT + tuple(scratch)
        ),
        name="backward",
        out_shape=(share, share, share, blocks, blocks, sds((every, 2, 16, 256), f32)),
        in_specs=[anywhere] * (len(BACKWARD_IN) - 2) + [on_chip] * 2,
        out_specs=(anywhere,) * 6,
        scratch_shapes=list(scratch.values()),
        compiler_params=pltpu.CompilerParams(
            collective_id=1, has_side_effects=True, vmem_limit_bytes=63 << 20
        ),
    )(*[args[k] for k in BACKWARD_IN])
    return bundle(BACKWARD_OUT, results)


def on_device(
    fs, cs, ts,
    inputs, cotangent, labels, scale_ids, head_flags, class_table, modulate_weight, modulate_bias,
    query_weight, key_weight, value_weight, query_bias, value_bias, query_gain, key_gain,
    output_weight, output_bias, up_weight, up_bias, down_weight, down_bias,
):
    images, rows_here, width = inputs.shape
    if images != 2 * ts or cs != 4 or ts % 2 or width != 256:
        raise ValueError("unsupported mesh")
    length = scale_ids.shape[0]
    every = labels.shape[0]
    count = fs * cs * ts
    sent = -(-rows_here // 16) * 16
    padded = -(-rows_here // 64) * 64
    tokens = cs * padded
    features = ts * width
    per = query_weight.shape[0]
    part_cols = class_table.shape[1]
    f, c, t = (lax.axis_index(n) for n in ("fsdp", "ctx", "tp"))
    core = lax.rem(c, 2)
    block = f * cs + c

    classes = class_table.shape[0]
    onehot = (labels[:, None] == jnp.arange(classes, dtype=jnp.int32)[None, :]).astype(bf16)
    cond_part = jnp.dot(onehot, class_table, preferred_element_type=f32)
    cond_spread = lax.dynamic_update_slice(
        jnp.zeros((every, per), f32), cond_part, (0, t * part_cols)
    )
    fit = ((0, 0), (0, sent - rows_here), (0, 0))

    def halves(weight):
        return weight.reshape(per, 2, -1).transpose(1, 0, 2)

    out_t, down_t = output_weight.T, down_weight.T
    lanes = modulate_bias.shape[2]
    small_rows = jnp.concatenate(
        [
            modulate_bias.reshape(-1, lanes), query_bias, value_bias, query_gain, key_gain,
            output_bias, down_bias, up_bias,
        ],
        axis=0,
    )
    small = lax.dynamic_update_slice(
        jnp.zeros((small_rows.shape[0], HD), bf16), small_rows, (0, block * lanes)
    ).reshape(-1, 2 * HD)
    ids = scale_ids.reshape(cs, rows_here)
    spare = ((0, 0), (0, padded - rows_here))
    ids_query = jnp.pad(ids, spare, constant_values=-1).reshape(1, tokens)
    ids_key = jnp.pad(ids, spare, constant_values=1 << 20).reshape(tokens, 1)
    k = run_forward(
        fs, cs, ts, sent, padded, per, every,
        dict(
            xb=jnp.pad(inputs, fit), gb=jnp.pad(cotangent, fit),
            s1=jnp.concatenate(
                [halves(query_weight), halves(key_weight), halves(value_weight), halves(out_t)], axis=2
            ),
            s2=halves(up_weight), s3=halves(down_t), sp=small, cond=cond_spread,
            wm=modulate_weight.reshape(per, 6 * width), idq=ids_query, idk=ids_key,
        ),
    )
    m = run_backward(
        fs, cs, ts, sent, padded, per, every,
        {key: {"idq": ids_query, "idk": ids_key}.get(key, getattr(k, key, None)) for key in BACKWARD_IN},
    )
    heads = modulate_bias.shape[1]
    sum_one, sum_two, sum_three, dx_blocks, bo_blocks, mail = m.o1, m.o2, m.o3, m.dxo, m.boo, m.mail

    block_out = bo_blocks[:, :rows_here]
    inputs_grad = dx_blocks[:, :rows_here].astype(f32)

    def joined(parts):
        return parts.transpose(1, 0, 2).reshape(per, -1)

    query_weight_grad = joined(sum_one[:, :, :128])
    key_weight_grad = joined(sum_one[:, :, 128:256])
    value_weight_grad = joined(sum_one[:, :, 256:384])
    output_weight_grad = joined(sum_one[:, :, 384:]).T
    up_weight_grad = joined(sum_two)
    down_weight_grad = joined(sum_three).T
    mod_delta = mail[:, 0, :6]
    same = jnp.sum(mail[:, 0, :8], axis=0)
    halves_sum = jnp.sum(mail[:, :, 8:12], axis=0)

    def mine(values):
        return lax.dynamic_slice_in_dim(values, block * lanes, lanes, values.ndim - 1)

    same = mine(same.reshape(8, heads, HD))
    modulate_bias_grad, output_bias_grad, down_bias_grad = same[:6], same[6], same[7]
    quarter = mine(halves_sum[:, :2].reshape(2, 4, heads // 2, HD)).transpose(1, 0, 2, 3).reshape(4, heads, lanes)
    query_bias_grad, value_bias_grad, query_gain_grad, key_gain_grad = (quarter[j] for j in range(4))
    up_bias_grad = mine(halves_sum[:, 2:].reshape(-1, HD))
    head_max = jnp.max(mail[:, :, 12], axis=0).reshape(heads, 128)[:, 0]

    cond_rows = lax.all_gather(cond_part, "tp", axis=1, tiled=True)
    silu_cond = jax.nn.silu(cond_rows).astype(bf16)
    flat_delta = mod_delta.reshape(every, 6 * width)
    modulate_weight_grad = jnp.einsum(
        "bd,be->de", silu_cond.astype(f32), flat_delta, precision=precise
    ).reshape(per, 6, width)
    silu_delta = jnp.einsum(
        "be,de->bd", flat_delta, modulate_weight.reshape(per, 6 * width).astype(f32), precision=precise
    )
    silu_cols = lax.psum_scatter(silu_delta, "tp", scatter_dimension=1, tiled=True)
    primal, silu_back = jax.vjp(jax.nn.silu, cond_part)
    cond_delta = silu_back(silu_cols)[0]
    class_table_grad = jnp.dot(onehot.astype(f32).T, cond_delta, precision=precise)

    factor = jnp.where(
        head_flags == 1,
        jnp.sqrt(clip_threshold / jnp.maximum(head_max, clip_threshold)),
        jnp.ones_like(head_max),
    )
    columns = jnp.repeat(factor, HD)
    clipped_query = query_weight.astype(f32) * columns[None, :]
    clipped_key = key_weight.astype(f32) * columns[None, :]
    clipped_query_bias = query_bias.astype(f32) * factor[:, None]
    return (
        block_out, inputs_grad, class_table_grad, modulate_weight_grad, modulate_bias_grad,
        query_weight_grad, key_weight_grad, value_weight_grad, query_bias_grad, value_bias_grad,
        query_gain_grad, key_gain_grad, output_weight_grad, output_bias_grad,
        up_weight_grad, up_bias_grad, down_weight_grad, down_bias_grad,
        clipped_query, clipped_key, clipped_query_bias,
    )


def solution(mesh):
    rows = P("fsdp", "ctx", "tp")
    table = P(None, ("fsdp", "ctx", "tp"))
    left = P(("fsdp", "ctx"), "tp")
    right = P("tp", ("fsdp", "ctx"))
    modulate = P(("fsdp", "ctx"), None, "tp")
    modulate_small = P(None, "tp", ("fsdp", "ctx"))
    return jax.shard_map(
        functools.partial(on_device, mesh.shape["fsdp"], mesh.shape["ctx"], mesh.shape["tp"]),
        mesh=mesh,
        in_specs=(
            rows, rows, P(), P(), P("tp"), table, modulate, modulate_small,
            left, left, left, right, right, right, right,
            right, right, left, right, right, right,
        ),
        out_specs=(
            rows, rows, table, modulate, modulate_small,
            left, left, left, right, right, right, right,
            right, right, left, right, right, right,
            left, left, right,
        ),
        check_vma=False,
    )
```

```python
import functools
import math

import jax
import jax.numpy as jnp
from jax import lax
from jax.experimental import pallas as pl
from jax.experimental.pallas import tpu as pltpu
from jax.sharding import PartitionSpec as P

HD = 64
GC = 512
CHUNK = 256
MESH = pl.DeviceIdType.MESH
precise = lax.Precision.HIGHEST
norm_epsilon = 1e-06
clip_threshold = 2.0
masked_score = -1e30
f32, bf16 = jnp.float32, jnp.bfloat16


def product(left, right, form):
    return jnp.einsum(form, left, right, preferred_element_type=f32)


def rcopy(src, dst, send_sem, recv_sem, device):
    return pltpu.make_async_remote_copy(
        src_ref=src,
        dst_ref=dst,
        send_sem=send_sem,
        recv_sem=recv_sem,
        device_id=device,
        device_id_type=MESH,
    )


class Place:
    def __init__(self, fs, cs, ts):
        self.fs, self.cs, self.ts = fs, cs, ts
        self.count = fs * cs * ts
        self.f, self.c, self.t = (lax.axis_index(n) for n in ("fsdp", "ctx", "tp"))
        self.hi, self.k = self.c // 2, lax.rem(self.c, 2)
        self.me = (self.f * cs + self.c) * ts + self.t
        self.slot = self.hi * ts + self.t

    def coords(self, n):
        return (n // (self.cs * self.ts), lax.rem(n // self.ts, self.cs), lax.rem(n, self.ts))

    def sibling(self):
        return (self.f, self.hi * 2 + 1 - self.k, self.t)

    def ypeer(self):
        return (self.f, (1 - self.hi) * 2 + self.k, self.t)

    def xpeer(self, s):
        return (lax.rem(self.f + s, self.fs), self.c, self.t)

    def xfrom(self, s):
        return lax.rem(self.f + self.fs - s, self.fs)

    def zpeer(self, s):
        return (self.f, self.c, lax.rem(self.t + s, self.ts))

    def zto(self, s):
        return lax.rem(self.t + s, self.ts)

    def zfrom(self, s):
        return lax.rem(self.t + self.ts - s, self.ts)

    def barrier(self):
        sem = pltpu.get_barrier_semaphore()

        def greet(n, carry):
            @pl.when(n != self.me)
            def _():
                pl.semaphore_signal(sem, inc=1, device_id=self.coords(n), device_id_type=MESH)

            return carry

        lax.fori_loop(0, self.count, greet, 0)
        pl.semaphore_wait(sem, self.count - 1)


def exchange_images(at, src_of, dst_of, send_sems, recv_sems, local_sem):
    slots = 2 * at.ts

    def start():
        for i in range(slots):
            hi, t = i // at.ts, i % at.ts

            @pl.when(i != at.slot)
            def _():
                rcopy(
                    src_of(i),
                    dst_of(at.slot),
                    send_sems.at[i],
                    recv_sems.at[at.slot],
                    (at.f, hi * 2 + at.k, t),
                ).start()

            @pl.when(i == at.slot)
            def _():
                pltpu.make_async_copy(src_of(i), dst_of(i), local_sem).start()

    def wait():
        for i in range(slots):
            @pl.when(i != at.slot)
            def _():
                rcopy(src_of(i), dst_of(i), send_sems.at[i], recv_sems.at[i], (at.f, at.c, at.t)).wait()

            @pl.when(i == at.slot)
            def _():
                pltpu.make_async_copy(src_of(i), dst_of(i), local_sem).wait()

    return start, wait


def broadcast_messages(at, src_of, slot_of, send_sems, recv_sems, local_sem):
    def start():
        def each(n, carry):
            @pl.when(n != at.me)
            def _():
                rcopy(src_of(n), slot_of(at.me), send_sems.at[n], recv_sems.at[at.me], at.coords(n)).start()

            @pl.when(n == at.me)
            def _():
                pltpu.make_async_copy(src_of(n), slot_of(n), local_sem).start()

            return carry

        lax.fori_loop(0, at.count, each, 0)

    def wait():
        def each(n, carry):
            @pl.when(n != at.me)
            def _():
                rcopy(src_of(n), slot_of(n), send_sems.at[n], recv_sems.at[n], at.coords(n)).wait()

            @pl.when(n == at.me)
            def _():
                pltpu.make_async_copy(src_of(n), slot_of(n), local_sem).wait()

            return carry

        lax.fori_loop(0, at.count, each, 0)

    return start, wait


FORWARD_IN = ("xb", "gb", "wq", "wk", "wv", "wu", "wo", "wd", "sp", "cond", "wm", "idq", "idk")
FORWARD_OUT = (
    "w1", "w2", "w3", "x", "g", "normed1", "qpre", "kpre", "v", "qh", "kh", "att", "branch1",
    "middle", "normed2", "hpre", "hid", "bo", "lse", "top", "mod", "par", "gate2",
    "dd", "d3", "n1t", "n2t", "db", "condr",
)


class Refs:
    pass


def bundle(keys, values):
    refs = Refs()
    for key, value in zip(keys, values, strict=True):
        setattr(refs, key, value)
    return refs


def normalize(values):
    centered = values - jnp.mean(values, axis=-1, keepdims=True)
    inverse = lax.rsqrt(jnp.mean(centered * centered, axis=-1, keepdims=True) + norm_epsilon)
    return centered * inverse, inverse


def nt(left, right):
    return lax.dot_general(left, right, (((1,), (1,)), ((), ())), preferred_element_type=f32)


def nn(left, right):
    return lax.dot_general(left, right, (((1,), (0,)), ((), ())), preferred_element_type=f32)


def segment_mean(values):
    row = lax.broadcasted_iota(jnp.int32, (2 * HD, 2 * HD), 0) < HD
    col = lax.broadcasted_iota(jnp.int32, (2 * HD, 2 * HD), 1) < HD
    same = jnp.where(row == col, 1.0 / HD, 0.0).astype(bf16)
    high = values.astype(bf16)
    rest = values - high.astype(f32)
    middle = rest.astype(bf16)
    low = (rest - middle.astype(f32)).astype(bf16)
    return nn(high, same) + nn(middle, same) + nn(low, same)


def head_inverse(values):
    return lax.rsqrt(segment_mean(values * values) + norm_epsilon)


gelu_a = math.sqrt(2.0 / math.pi)
gelu_b = 0.044715


def forward_kernel(fs, cs, ts, sent, padded, per, keys, *values):
    r = bundle(keys, values)
    at = Place(fs, cs, ts)
    width = 256
    tokens, features = r.xs.shape
    half = tokens // 2
    quarter = features // ts
    zero = jnp.zeros((padded - sent, features), bf16)
    for c in range(cs):
        r.xs[c * padded + sent : (c + 1) * padded, :] = zero
        r.gs[c * padded + sent : (c + 1) * padded, :] = zero
    at.barrier()

    def block_at(out):
        def dst(i):
            c = (i // ts) * 2 + at.k
            return out.at[
                pl.ds(pl.multiple_of(c * padded, padded), sent),
                pl.ds(pl.multiple_of(lax.rem(i, ts) * width, width), width),
            ]

        return dst

    x_start, x_wait = exchange_images(at, lambda i: r.xb.at[i], block_at(r.xs), r.x_send, r.x_recv, r.loc.at[0])
    g_start, g_wait = exchange_images(at, lambda i: r.gb.at[i], block_at(r.gs), r.g_send, r.g_recv, r.loc.at[1])

    r.wot[...] = r.wo[...].T
    r.wdt[...] = r.wd[...].T
    pieces, items = [[(r.sp, None, None)]], [(r.parts, None, r.sp.shape[0])]
    for col, sources in ((0, (r.wq,)), (128, (r.wk,)), (256, (r.wv, r.wot))):
        pieces.append([(ref, 128, (0, 128, col + 128 * i)) for i, ref in enumerate(sources)])
        items.append((r.w1s, slice(col, col + 128 * len(sources)), per))
    for full, ref in ((r.w2s, r.wu), (r.w3s, r.wdt)):
        for col in range(0, GC, CHUNK):
            pieces.append([(ref, CHUNK, (col, GC, col))])
            items.append((full, slice(col, col + CHUNK), per))

    def slab(n, z, nz, f, hi, k=0, blocks=2):
        full, cols, size = items[n]
        row = pl.multiple_of(((f * 2 + hi) * 2 + k) * size, size)
        span = pl.ds(row, blocks * size)
        return full.at[pl.ds(z, nz), span, :] if cols is None else full.at[pl.ds(z, nz), span, cols]

    def core_pair(n):
        full, _, size = items[n]

        def place(z, k, cols):
            span = pl.ds(pl.multiple_of(((at.f * 2 + at.hi) * 2 + k) * size, size), size)
            return full.at[z, span, :] if cols is None else full.at[z, span, cols]

        copies = []
        for i, (ref, w, where) in enumerate(pieces[n]):
            if where is None:
                mine, theirs, cols = ref, ref, None
            else:
                start, stride, col = where
                mine, theirs = (
                    ref.at[:, pl.ds(pl.multiple_of(start + k * stride, 128), w)] for k in (at.k, 1 - at.k)
                )
                cols = slice(col, col + w)
            sems = (r.core_send.at[n, i], r.core_recv.at[n, i], at.sibling())
            copies.append(
                (
                    functools.partial(pltpu.make_async_copy, mine, place(at.t, at.k, cols), r.core_loc.at[n, i]),
                    functools.partial(rcopy, theirs, place(at.t, at.k, cols), *sems),
                    functools.partial(rcopy, theirs, place(at.t, 1 - at.k, cols), *sems),
                )
            )
        return copies

    def core_start(n):
        for keep, out, _ in core_pair(n):
            keep().start()
            out().start()

    def core_wait(n):
        for keep, _, inn in core_pair(n):
            keep().wait()
            inn().wait()

    def hop(n, d, up, action):
        block = at.t - d if up else at.t + d
        sends = ((block >= 0) & (at.t < ts - 1)) if up else ((block < ts) & (at.t > 0))

        @pl.when(sends)
        def _():
            src = slab(n, block, 1, at.f, at.hi)
            side = 0 if up else 1
            copy = rcopy(
                src, src, r.z_send.at[side, n, d], r.z_recv.at[side, n, d + 1],
                (at.f, at.c, at.t + 1 if up else at.t - 1),
            )
            copy.start() if action == "start" else copy.wait_send()

    def z_start(n):
        hop(n, 0, True, "start")
        hop(n, 0, False, "start")

    def z_step(n, d):
        for up in (True, False):
            block = at.t - d if up else at.t + d

            @pl.when((block >= 0) & (block < ts))
            def _():
                src = slab(n, block, 1, at.f, at.hi)
                side = 0 if up else 1
                rcopy(
                    src, src, r.z_send.at[side, n, d], r.z_recv.at[side, n, d], (at.f, at.c, at.t)
                ).wait_recv()

            if d < ts - 1:
                hop(n, d, up, "start")

    def z_wait(n):
        for d in range(1, ts):
            z_step(n, d)

    def direct_start(n):
        for s in range(1, ts):
            src = slab(n, at.t, 1, at.f, at.hi)
            rcopy(src, src, r.zd_send.at[n, s], r.zd_recv.at[n, s], at.zpeer(s)).start()

    def direct_wait(n):
        for s in range(1, ts):
            src = slab(n, at.zfrom(s), 1, at.f, at.hi)
            rcopy(src, src, r.zd_send.at[n, s], r.zd_recv.at[n, s], at.zpeer(s)).wait()

    def z_sent(n):
        for d in range(ts - 1):
            for up in (True, False):
                hop(n, d, up, "sent")

    def xy_start(n):
        src = slab(n, 0, ts, at.f, at.hi)
        rcopy(src, src, r.ys_send.at[n], r.ys_recv.at[n], at.ypeer()).start()
        for s in range(1, fs):
            rcopy(src, src, r.xs_send.at[n, s], r.xs_recv.at[n, s], at.xpeer(s)).start()

    def xy_wait(n):
        src = slab(n, 0, ts, at.f, 1 - at.hi)
        rcopy(src, src, r.ys_send.at[n], r.ys_recv.at[n], at.ypeer()).wait()
        for s in range(1, fs):
            src = slab(n, 0, ts, at.xfrom(s), at.hi)
            rcopy(src, src, r.xs_send.at[n, s], r.xs_recv.at[n, s], at.xpeer(s)).wait()

    def fwd_start(n):
        zh = ts // 2 - n % 2
        for s in range(1, fs):
            src = slab(n, zh, ts - zh, at.f, 1 - at.hi)
            rcopy(src, src, r.fx_send.at[n, s], r.fx_recv.at[n, s], at.xpeer(s)).start()
            src = slab(n, 0, zh, at.xfrom(s), at.hi)
            rcopy(src, src, r.fy_send.at[n, s], r.fy_recv.at[n, s], at.ypeer()).start()

    def fwd_wait(n):
        zh = ts // 2 - n % 2
        for s in range(1, fs):
            src = slab(n, zh, ts - zh, at.xfrom(s), 1 - at.hi)
            rcopy(src, src, r.fx_send.at[n, s], r.fx_recv.at[n, s], at.xpeer(s)).wait()
            src = slab(n, 0, zh, at.xfrom(s), 1 - at.hi)
            rcopy(src, src, r.fy_send.at[n, s], r.fy_recv.at[n, s], at.ypeer()).wait()

    saved = []

    def save(src, out):
        copy = pltpu.make_async_copy(src, out, r.out_sem.at[len(saved)])
        copy.start()
        saved.append([src, out, True])
        return len(saved) - 1

    def settle(n):
        src, out, waiting = saved[n]
        if waiting:
            pltpu.make_async_copy(src, out, r.out_sem.at[n]).wait()
            saved[n][2] = False

    def transpose(src):
        def tile(n, carry):
            span = pl.ds(pl.multiple_of(n * 128, 128), 128)
            r.xt[:, span] = src[span, :].T
            return carry

        lax.fori_loop(0, tokens // 128, tile, 0)

    last = len(items) - 1
    r.cond_slots[at.t] = r.cond[...]

    def cond_copy(s, slot):
        return rcopy(r.cond, r.cond_slots.at[slot], r.c_send.at[s], r.c_recv.at[s], at.zpeer(s))

    for s in range(1, ts):
        cond_copy(s, at.t).start()
    for n in range(4):
        core_start(n)
    core_wait(0)
    direct_start(0)
    core_wait(1)
    direct_start(1)
    for n in range(4, last + 1):
        core_start(n)
    core_wait(2)
    z_start(2)
    direct_wait(0)
    xy_start(0)

    for s in range(1, ts):
        cond_copy(s, at.zfrom(s)).wait()
    cond = r.cond_slots[0]
    for z in range(1, ts):
        cond = cond + r.cond_slots[z]
    r.crow[...] = cond
    save(r.crow, r.condr)
    silu = (cond / (1.0 + jnp.exp(-cond))).astype(bf16)
    for j in range(6):
        r.part[:, j, :] = jnp.dot(silu, r.wm[:, j * width : (j + 1) * width], preferred_element_type=f32)

    def image_of(n):
        f, c, t = at.coords(n)
        return (f * 2 + c // 2) * ts + t

    m_start, m_wait = broadcast_messages(
        at, lambda n: r.part.at[image_of(n)], lambda n: r.msg.at[n], r.m_send, r.m_recv, r.loc.at[2]
    )
    xy_wait(0)
    fwd_start(0)
    direct_wait(1)
    xy_start(1)
    z_step(2, 1)
    core_wait(3)
    z_start(3)
    z_step(2, 2)
    z_step(2, 3)
    xy_start(2)
    xy_wait(1)
    fwd_start(1)
    z_step(3, 1)
    m_start()
    z_step(3, 2)
    xy_wait(2)
    fwd_start(2)
    z_step(3, 3)
    xy_start(3)
    x_start()
    for n in range(4, last + 1):
        core_wait(n)
    fwd_wait(0)
    m_wait()
    z_start(4)

    blocks = fs * cs
    rows_small = r.sp.shape[0]

    def small_sum(n, carry):
        return carry + r.parts[:, pl.ds(pl.multiple_of(n * rows_small, rows_small), rows_small), :].astype(f32)

    r.psum[...] = lax.fori_loop(0, blocks, small_sum, jnp.zeros(r.psum.shape, f32))
    for z in range(ts):

        def mod_sum(n, carry):
            return carry + r.msg[n * ts + z]

        total = lax.fori_loop(0, blocks, mod_sum, jnp.zeros((8, width), f32))
        for j in range(6):
            for h in range(2):
                value = total[j : j + 1, h * 128 : (h + 1) * 128] + r.psum[z, 2 * j + h : 2 * j + h + 1, :]
                r.mods[j : j + 1, z * width + h * 128 : z * width + (h + 1) * 128] = value.astype(bf16).astype(f32)
                if j < 2:
                    row = r.psum[z, 20 + 2 * j + h : 21 + 2 * j + h, :]
                    r.mods[6 + j : 7 + j, z * width + h * 128 : z * width + (h + 1) * 128] = row

    def mod(j):
        return r.mods[j : j + 1, :]

    def own_row(z, start):
        return r.psum[z, pl.ds(start + at.k, 1), :]

    z_step(4, 1)
    xy_wait(3)
    fwd_start(3)
    z_step(4, 2)
    z_start(5)
    x_wait()

    def sib_pair(buf, send, recv, hi):
        mine = buf.at[pl.ds(pl.multiple_of((hi * 2 + at.k) * padded, padded), sent), :]
        theirs = buf.at[pl.ds(pl.multiple_of((hi * 2 + 1 - at.k) * padded, padded), sent), :]
        return (
            functools.partial(rcopy, mine, mine, send.at[hi], recv.at[hi], at.sibling()),
            functools.partial(rcopy, theirs, theirs, send.at[hi], recv.at[hi], at.sibling()),
        )

    for hi in range(2):
        sib_pair(r.xs, r.sib_send, r.sib_recv, hi)[0]().start()
    z_step(4, 3)
    xy_start(4)
    for hi in range(2):
        sib_pair(r.xs, r.sib_send, r.sib_recv, hi)[1]().wait()
    save(r.xs, r.x)

    step = 64

    def norm_tile(src, dst, shift, scale):
        def tile(n, carry):
            span = pl.ds(pl.multiple_of(n * step, step), step)
            normal, _ = normalize(src[span, :].astype(f32))
            dst[span, :] = (normal * (1.0 + mod(scale)) + mod(shift)).astype(bf16)
            return carry

        lax.fori_loop(0, tokens // step, tile, 0)

    norm_tile(r.xs, r.n1, 0, 1)
    save(r.n1, r.normed1)
    z_step(5, 1)
    z_step(5, 2)
    z_start(6)
    for n in range(1, 4):
        fwd_wait(n)
    save(r.w1s, r.w1)

    def qkv(i, carry):
        z = i // 2
        span = pl.ds(pl.multiple_of(lax.rem(i, 2) * half, half), half)
        raw = nn(r.n1[span, :], r.w1s[z, :, : 3 * 128])
        q = raw[:, :128] + own_row(z, 12)
        k = raw[:, 128:256]
        r.qp[z, span, :] = q
        r.kp[z, span, :] = k
        r.vs[z, span, :] = (raw[:, 256:] + own_row(z, 14)).astype(bf16)
        r.qhs[z, span, :] = (q * head_inverse(q) * own_row(z, 16)).astype(bf16)
        r.khs[z, span, :] = (k * head_inverse(k) * own_row(z, 18)).astype(bf16)
        return carry

    lax.fori_loop(0, ts, qkv, 0)
    z_step(5, 3)
    xy_start(5)
    xy_wait(4)
    fwd_start(4)
    z_step(6, 1)
    z_step(6, 2)
    z_start(7)
    lax.fori_loop(ts, 2 * ts, qkv, 0)
    for src, out in ((r.qp, r.qpre), (r.kp, r.kpre), (r.vs, r.v), (r.qhs, r.qh), (r.khs, r.kh)):
        save(src, out)
    z_step(6, 3)
    xy_start(6)
    z_step(7, 1)
    z_step(7, 2)
    g_start()
    transpose(r.n1)
    n1t = save(r.xt, r.n1t)

    qt = 256

    def attend(z):
        v_t = r.vs[z].T
        tops = [jnp.full((1, qt), masked_score, f32) for _ in range(2)]

        def tile(n, tops):
            span = pl.ds(pl.multiple_of(n * qt, qt), qt)
            allowed = r.idk[...] <= r.idq[:, span]
            outs, peaks = [], []
            for h in range(2):
                lanes = slice(h * HD, (h + 1) * HD)
                s = nt(r.khs[z, :, lanes], r.qhs[z, span, lanes] * 0.125)
                s = jnp.where(allowed, s, masked_score)
                peak = jnp.max(s, axis=0, keepdims=True)
                e = jnp.exp(s - peak)
                total = jnp.sum(e, axis=0, keepdims=True)
                r.lses[z, h : h + 1, span] = peak + jnp.log(total)
                p = (e * (1.0 / total)).astype(bf16)
                outs.append(nn(v_t[h * HD : (h + 1) * HD, :], p))
                peaks.append(jnp.maximum(tops[h], peak))
            r.atts[z, span, :] = jnp.concatenate(outs, axis=0).T.astype(bf16)
            return peaks

        tops = lax.fori_loop(0, tokens // qt, tile, tops)
        for h in range(2):
            r.tops[z, h : h + 1, :] = jnp.broadcast_to(jnp.max(tops[h], axis=1, keepdims=True), (1, 128))

    attend(0)
    xy_wait(5)
    fwd_start(5)
    z_step(7, 3)
    xy_start(7)
    attend(1)
    fwd_wait(4)
    attend(2)
    xy_wait(6)
    fwd_start(6)
    attend(3)
    for src, out in ((r.atts, r.att), (r.lses, r.lse), (r.tops, r.top)):
        save(src, out)

    def pair(e, n):
        span = pl.ds(n * half, half)
        return rcopy(
            r.sendbuf.at[span, :], r.recvs.at[e, span, :], r.e_send.at[e, n], r.e_recv.at[e, n], at.sibling()
        )

    for n in range(2):
        span = slice(n * half, (n + 1) * half)
        for c in range(2):
            cols = slice(c * 512, (c + 1) * 512)
            acc = nt(r.atts[0, span, :], r.w1s[0, cols, 384:])
            for z in range(1, ts):
                acc = acc + nt(r.atts[z, span, :], r.w1s[z, cols, 384:])
            r.sendbuf[span, cols] = acc.astype(bf16)
        pair(0, n).start()
    for n in range(2):
        pair(0, n).wait()

        def tile(i, carry):
            span = pl.ds(pl.multiple_of(n * half + i * step, step), step)
            branch = r.sendbuf[span, :].astype(f32) + r.recvs[0, span, :].astype(f32) + mod(6)
            r.b1[span, :] = branch.astype(bf16)
            middle = (r.xs[span, :].astype(f32) + mod(2) * branch).astype(bf16)
            r.mid[span, :] = middle
            normal, _ = normalize(middle.astype(f32))
            r.n2[span, :] = (normal * (1.0 + mod(4)) + mod(3)).astype(bf16)
            return carry

        lax.fori_loop(0, half // step, tile, 0)
    for src, out in ((r.b1, r.branch1), (r.mid, r.middle), (r.n2, r.normed2)):
        save(src, out)

    def up_part(c):
        cols = slice(c * CHUNK, (c + 1) * CHUNK)

        def body(i, carry):
            z = i // 2
            span = pl.ds(pl.multiple_of(lax.rem(i, 2) * half, half), half)
            pre = nn(r.n2[span, :], r.w2s[z, :, cols])
            bias = [r.psum[z, pl.ds(24 + 4 * at.k + 2 * c + j, 1), :] for j in range(2)]
            pre = pre + jnp.concatenate(bias, axis=1)
            r.hp[z, span, cols] = pre
            inner = jnp.tanh(gelu_a * (pre + gelu_b * pre * pre * pre))
            r.hs[z, span, cols] = (0.5 * pre * (1.0 + inner)).astype(bf16)
            return carry

        lax.fori_loop(0, 2 * ts, body, 0)

    up_part(0)
    g_wait()
    for hi in range(2):
        sib_pair(r.gs, r.gsib_send, r.gsib_recv, hi)[0]().start()
    fwd_wait(5)
    save(r.w2s, r.w2)
    up_part(1)
    save(r.hp, r.hpre)
    save(r.hs, r.hid)
    xy_wait(7)
    fwd_start(7)
    settle(n1t)
    transpose(r.n2)
    n2t = save(r.xt, r.n2t)
    for hi in range(2):
        sib_pair(r.gs, r.gsib_send, r.gsib_recv, hi)[1]().wait()
    save(r.gs, r.g)

    def delta_tile(n, carry):
        span = pl.ds(pl.multiple_of(n * step, step), step)
        delta = (r.gs[span, :].astype(f32) * mod(5)).astype(bf16)
        r.dds[span, :] = delta
        return carry + jnp.sum(delta.astype(f32).reshape(step // 8, 8, features), axis=0)

    r.dbs[...] = lax.fori_loop(0, tokens // step, delta_tile, jnp.zeros((8, features), f32))
    save(r.dbs, r.db)
    save(r.dds, r.dd)
    settle(n2t)
    transpose(r.dds)
    for z in range(ts):

        def grad_tile(m, carry):
            span = pl.ds(pl.multiple_of(m * 256, 256), 256)
            r.d3s[z, span, :] = nn(r.xt[span, :], r.hs[z]).astype(bf16)
            return carry

        lax.fori_loop(0, features // 256, grad_tile, 0)
        save(r.d3s.at[z], r.d3.at[z])

    def down_part(c, first):
        cols = slice(c * CHUNK, (c + 1) * CHUNK)
        for n in range(2):
            span = slice(n * half, (n + 1) * half)
            for m in range(2):
                rows = slice(m * 512, (m + 1) * 512)
                acc = nt(r.hs[0, span, cols], r.w3s[0, rows, cols])
                for z in range(1, ts):
                    acc = acc + nt(r.hs[z, span, cols], r.w3s[z, rows, cols])
                if first:
                    r.acc[span, rows] = acc
                else:
                    r.sendbuf[span, rows] = (r.acc[span, rows] + acc).astype(bf16)
            if not first:
                pair(1, n).start()

    fwd_wait(6)
    down_part(0, True)
    fwd_wait(7)
    save(r.w3s, r.w3)
    down_part(1, False)
    for n in range(2):
        pair(1, n).wait()

        def tile(i, carry):
            span = pl.ds(pl.multiple_of(n * half + i * step, step), step)
            branch = r.sendbuf[span, :].astype(f32) + r.recvs[1, span, :].astype(f32) + mod(7)
            r.bos[span, :] = (r.mid[span, :].astype(f32) + mod(5) * branch).astype(bf16)
            product = r.gs[span, :].astype(f32) * branch
            return carry + jnp.sum(product.reshape(step // 8, 8, features), axis=0)

        part = lax.fori_loop(0, half // step, tile, jnp.zeros((8, features), f32))
        if n == 0:
            r.gates[...] = part
        else:
            r.gates[...] += part
    for src, out in ((r.bos, r.bo), (r.gates, r.gate2), (r.mods, r.mod), (r.psum, r.par)):
        save(src, out)
    for n in range(2, last + 1):
        z_sent(n)
    for n in range(len(saved)):
        settle(n)


def run_forward(fs, cs, ts, sent, padded, per, every, args):
    tokens, features = cs * padded, ts * 256
    sds = jax.ShapeDtypeStruct
    big = (ts, features, GC)
    outs = {
        "w1": (big, bf16), "w2": (big, bf16), "w3": (big, bf16),
        "x": ((tokens, features), bf16), "g": ((tokens, features), bf16), "normed1": ((tokens, features), bf16),
        "qpre": ((ts, tokens, 128), f32), "kpre": ((ts, tokens, 128), f32),
        "v": ((ts, tokens, 128), bf16), "qh": ((ts, tokens, 128), bf16), "kh": ((ts, tokens, 128), bf16),
        "att": ((ts, tokens, 128), bf16), "branch1": ((tokens, features), bf16),
        "middle": ((tokens, features), bf16), "normed2": ((tokens, features), bf16),
        "hpre": ((ts, tokens, GC), f32), "hid": ((ts, tokens, GC), bf16), "bo": ((tokens, features), bf16),
        "lse": ((ts, 2, tokens), f32), "top": ((ts, 2, 128), f32), "mod": ((8, features), f32),
        "par": ((ts, 32, 128), f32), "gate2": ((8, features), f32),
        "dd": ((tokens, features), bf16), "d3": (big, bf16), "n1t": ((features, tokens), bf16),
        "n2t": ((features, tokens), bf16), "db": ((8, features), f32), "condr": ((every, per), f32),
    }
    vm, dma = pltpu.VMEM, pltpu.SemaphoreType.DMA
    local = dict(
        w1s="w1", w2s="w2", w3s="w3", xs="x", gs="g", n1="normed1", qp="qpre", kp="kpre", vs="v", qhs="qh",
        khs="kh", atts="att", b1="branch1", mid="middle", n2="normed2", hp="hpre", hs="hid", bos="bo",
        lses="lse", tops="top", mods="mod", psum="par", gates="gate2",
        dds="dd", d3s="d3", xt="n1t", dbs="db", crow="condr",
    )
    scratch = {k: vm(*outs[v]) for k, v in local.items()}
    items = 4 + 2 * (GC // CHUNK)
    scratch.update(
        sendbuf=vm((tokens, features), bf16), recvs=vm((2, tokens, features), bf16), acc=vm((tokens, features), f32),
        cond_slots=vm((ts, every, per), f32), part=vm((every, 8, 256), f32),
        msg=vm((fs * cs * ts, 8, 256), f32), parts=vm((ts, fs * cs * 32, 128), bf16),
        x_send=dma((2 * ts,)), x_recv=dma((2 * ts,)), g_send=dma((2 * ts,)), g_recv=dma((2 * ts,)), loc=dma((3,)),
        sib_send=dma((2,)), sib_recv=dma((2,)), gsib_send=dma((2,)), gsib_recv=dma((2,)),
        c_send=dma((ts,)), c_recv=dma((ts,)), m_send=dma((fs * cs * ts,)), m_recv=dma((fs * cs * ts,)),
        core_send=dma((items, 2)), core_recv=dma((items, 2)), core_loc=dma((items, 2)),
        z_send=dma((2, items, ts)), z_recv=dma((2, items, ts)), zd_send=dma((2, ts)), zd_recv=dma((2, ts)),
        wot=vm((per, 256), bf16), wdt=vm((per, ts * 256), bf16),
        xs_send=dma((items, fs)), xs_recv=dma((items, fs)), ys_send=dma((items,)), ys_recv=dma((items,)),
        fx_send=dma((items, fs)), fx_recv=dma((items, fs)), fy_send=dma((items, fs)), fy_recv=dma((items, fs)),
        e_send=dma((2, 2)), e_recv=dma((2, 2)), out_sem=dma((len(outs) + ts,)),
    )
    anywhere, on_chip = pl.BlockSpec(memory_space=pl.ANY), pl.BlockSpec(memory_space=vm)
    results = pl.pallas_call(
        functools.partial(
            forward_kernel, fs, cs, ts, sent, padded, per, FORWARD_IN + FORWARD_OUT + tuple(scratch)
        ),
        name="forward",
        out_shape=tuple(sds(*outs[k]) for k in FORWARD_OUT),
        in_specs=[anywhere] * 6 + [on_chip] * 2 + [anywhere] + [on_chip] * 4,
        out_specs=(anywhere,) * len(FORWARD_OUT),
        scratch_shapes=list(scratch.values()),
        compiler_params=pltpu.CompilerParams(
            collective_id=0, has_side_effects=True, vmem_limit_bytes=62 << 20
        ),
    )(*[args[k] for k in FORWARD_IN])
    return bundle(FORWARD_OUT, results)


def attend_back(z, r, query_gain, key_gain):
    tokens = r.vs.shape[1]
    qt = 256
    r.dka[...] = jnp.zeros_like(r.dka)
    r.dva[...] = jnp.zeros_like(r.dva)
    k_t = r.khs[z].T

    def tile(n, carry):
        span = pl.ds(pl.multiple_of(n * qt, qt), qt)
        allowed = r.idk[...] <= r.idq[:, span]
        outs = []
        for h in range(2):
            lanes = slice(h * HD, (h + 1) * HD)
            qh, da = r.qhs[z, span, lanes] * 0.125, r.das[z, span, lanes]
            s = jnp.where(allowed, nt(r.khs[z, :, lanes], qh), masked_score)
            p = jnp.exp(s - r.lses[z, h : h + 1, span])
            dp = nt(r.vs[z, :, lanes], da)
            centre = jnp.sum(p * dp, axis=0, keepdims=True)
            ds = (p * (dp - centre)).astype(bf16)
            r.dva[h] += nn(p.astype(bf16), da)
            r.dka[h] += nn(ds, qh)
            outs.append(nn(k_t[h * HD : (h + 1) * HD, :], ds))
        r.dqa[span, :] = jnp.concatenate(outs, axis=0).T * 0.125
        return carry

    lax.fori_loop(0, tokens // qt, tile, 0)

    def finish(n, sums):
        span = pl.ds(pl.multiple_of(n * qt, qt), qt)
        dk = jnp.concatenate([r.dka[0, span, :], r.dka[1, span, :]], axis=1)
        dv = jnp.concatenate([r.dva[0, span, :], r.dva[1, span, :]], axis=1).astype(bf16)
        r.dqkv[z, span, 256:] = dv
        results = [None, None, None, jnp.sum(dv.astype(f32), axis=0, keepdims=True)]
        for i, (raw_ref, gain, delta) in enumerate(((r.qp, query_gain, r.dqa[span, :]), (r.kp, key_gain, dk))):
            raw = raw_ref[z % 2, span, :]
            inverse = head_inverse(raw)
            results[i] = jnp.sum(delta * raw * inverse, axis=0, keepdims=True)
            t = delta * gain
            out = (inverse * t - raw * (inverse * inverse * inverse) * segment_mean(t * raw)).astype(bf16)
            r.dqkv[z, span, i * 128 : (i + 1) * 128] = out
            if i == 0:
                results[2] = jnp.sum(out.astype(f32), axis=0, keepdims=True)
        return [a + b for a, b in zip(sums, results)]

    sums = lax.fori_loop(0, tokens // qt, finish, [jnp.zeros((1, 128), f32)] * 4)
    for row, value in enumerate((sums[2], sums[3], sums[0], sums[1])):
        r.vec[z, row : row + 1, :] = value


BACKWARD_IN = (
    "w1", "w2", "w3", "x", "g", "qpre", "kpre", "v", "qh", "kh", "att", "branch1",
    "middle", "n2t", "hpre", "hid", "bo", "lse", "top", "mod", "par", "gate2", "dd", "d3", "n1t", "db",
    "idq", "idk", "wm",
)
BACKWARD_OUT = ("o1", "o2", "o3", "dxo", "boo", "maila", "mailb", "sdel")


def backward_kernel(fs, cs, ts, sent, padded, per, keys, *values):
    r = bundle(keys, values)
    at = Place(fs, cs, ts)
    width = 256
    tokens, features = r.gs.shape
    half = tokens // 2
    step = 64
    at.barrier()

    pending = {}
    order = []

    def load(name, src, dst):
        pltpu.make_async_copy(src, dst, r.in_sem.at[len(order)]).start()
        pending[name] = (src, dst, len(order))
        order.append(name)

    def need(*wanted):
        for name in wanted:
            src, dst, n = pending.pop(name)
            pltpu.make_async_copy(src, dst, r.in_sem.at[n]).wait()

    for z in range(ts):
        load("d3%d" % z, r.d3.at[z], r.d.at[z])
    load("dd", r.dd, r.dds)
    load("w3", r.w3, r.wa)
    load("hp0", r.hpre.at[0], r.hp.at[0])
    load("n2t", r.n2t, r.xt)
    load("hp1", r.hpre.at[1], r.hp.at[1])
    load("w2", r.w2, r.wb)
    load("mod", r.mod, r.mods)
    load("g", r.g, r.gs)
    load("mid", r.middle, r.mid)
    load("b1", r.branch1, r.b1)
    load("att", r.att, r.atts)
    load("par", r.par.at[:, pl.ds(16, 8), :], r.psum)
    for name, src, dst in (
        ("qh", r.qh, r.qhs), ("kh", r.kh, r.khs), ("v", r.v, r.vs), ("lse", r.lse, r.lses),
        ("top", r.top, r.tops), ("gate2", r.gate2, r.gates),
        ("db", r.db, r.dbs),
    ):
        load(name, src, dst)

    def load_raw(z):
        load("qp%d" % z, r.qpre.at[z], r.qp.at[z % 2])
        load("kp%d" % z, r.kpre.at[z], r.kp.at[z % 2])

    load_raw(0)
    load_raw(1)

    def block_of(ref):
        def src(i):
            c = (i // ts) * 2 + at.k
            return ref.at[
                pl.ds(pl.multiple_of(c * padded, padded), sent),
                pl.ds(pl.multiple_of(lax.rem(i, ts) * width, width), width),
            ]

        return src

    bo_start, bo_wait = exchange_images(
        at, block_of(r.bo), lambda i: r.boo.at[i], r.bo_send, r.bo_recv, r.loc.at[1]
    )
    dx_start, dx_wait = exchange_images(
        at, block_of(r.dds), lambda i: r.dxo.at[i], r.dx_send, r.dx_recv, r.loc.at[0]
    )
    outs = (r.o1, r.o2, r.o3)

    def parts_of(z):
        cut = GC // 2 if z % 2 == 0 else GC // 4
        return slice(cut, GC), slice(0, cut)

    def slot(g, z):
        return z + (ts if g == 1 else 0)

    def rows(f, hi):
        return pl.ds(pl.multiple_of((f * 2 + hi) * 2 * per, 2 * per), 2 * per)

    def far(s):
        return lax.rem(at.f + s, fs)

    def stage_one(g, z, s):
        n, d = g * ts + z, slot(g, z)
        x_part, y_part = parts_of(z)
        return (
            rcopy(
                r.d.at[d, rows(far(s), 1 - at.hi), y_part], r.r1.at[n, s - 1, :, y_part],
                r.y1_send.at[n, s], r.y1_recv.at[n, s], at.ypeer(),
            ),
            rcopy(
                r.d.at[d, rows(far(s), 1 - at.hi), x_part], r.r1.at[n, s - 1, :, x_part],
                r.x1_send.at[n, s], r.x1_recv.at[n, s], at.xpeer(s),
            ),
        )

    def stage_two(g, z):
        n, d = g * ts + z, slot(g, z)
        copies = [
            rcopy(
                r.d.at[d, rows(far(s), at.hi), :], r.rx2.at[n, s - 1],
                r.x2_send.at[n, s], r.x2_recv.at[n, s], at.xpeer(s),
            )
            for s in range(1, fs)
        ]
        copies.append(
            rcopy(r.d.at[d, rows(at.f, 1 - at.hi), :], r.ry2.at[n], r.y2_send.at[n], r.y2_recv.at[n], at.ypeer())
        )
        return copies

    def rs_a(g, z):
        for s in range(1, fs):
            for copy in stage_one(g, z, s):
                copy.start()

    def rs_b(g, z):
        n, d = g * ts + z, slot(g, z)
        x_part, y_part = parts_of(z)
        for s in range(1, fs):
            for copy in stage_one(g, z, s):
                copy.wait()
        for s in range(1, fs):
            span = rows(far(s), at.hi)
            r.d[d, span, y_part] = (r.d[d, span, y_part].astype(f32) + r.r1[n, s - 1, :, y_part].astype(f32)).astype(bf16)
        span = rows(at.f, 1 - at.hi)
        value = r.d[d, span, x_part].astype(f32)
        for s in range(1, fs):
            value = value + r.r1[n, s - 1, :, x_part].astype(f32)
        r.d[d, span, x_part] = value.astype(bf16)
        for copy in stage_two(g, z):
            copy.start()

    def to_owner(g, z):
        s = lax.rem(at.t + ts - z, ts)
        index = jnp.maximum(s, 1)
        return rcopy(
            r.ry2.at[g * ts + z], r.rz.at[g, index - 1],
            r.z_send.at[g * ts + z], r.z_recv.at[g, index], (at.f, at.c, z),
        )

    def rs_c(g, z):
        n, d = g * ts + z, slot(g, z)
        for copy in stage_two(g, z):
            copy.wait()
        span = rows(at.f, at.hi)
        for part in (slice(0, GC // 2), slice(GC // 2, GC)):
            value = r.d[d, span, part].astype(f32) + r.ry2[n, :, part].astype(f32)
            for s in range(1, fs):
                value = value + r.rx2[n, s - 1, :, part].astype(f32)
            r.ry2[n, :, part] = value.astype(bf16)

        @pl.when(at.t != z)
        def _():
            to_owner(g, z).start()

    def pair_sum(g):
        src = r.total.at[pl.ds(pl.multiple_of((1 - at.k) * per, per), per)]
        own = r.total.at[pl.ds(pl.multiple_of(at.k * per, per), per)]
        keep = pltpu.make_async_copy(own, outs[g].at[at.k], r.k_loc.at[g])
        out = functools.partial(rcopy, src, outs[g].at[at.k], r.k_send.at[g], r.k_recv.at[g], at.sibling())
        inn = functools.partial(rcopy, src, outs[g].at[1 - at.k], r.k_send.at[g], r.k_recv.at[g], at.sibling())
        return keep, out, inn

    def pair_wait(g):
        keep, _, inn = pair_sum(g)
        keep.wait()
        inn().wait()

    def rs_e(g):
        for z in range(ts):

            @pl.when(at.t != z)
            def _():
                to_owner(g, z).wait_send()

        for s in range(1, ts):
            rcopy(
                r.rz.at[g, s - 1], r.rz.at[g, s - 1], r.z_send.at[g * ts], r.z_recv.at[g, s], at.zpeer(s)
            ).wait_recv()
        for part in (slice(0, GC // 2), slice(GC // 2, GC)):
            value = r.ry2[g * ts + at.t, :, part].astype(f32)
            for s in range(1, ts):
                value = value + r.rz[g, s - 1, :, part].astype(f32)
            r.total[:, part] = value
        keep, out, _ = pair_sum(g)
        keep.start()
        out().start()

    def mod(j):
        return r.mods[j : j + 1, :]

    def own_row(z, start):
        return r.psum[z, pl.ds(start + at.k, 1), :]

    def transpose(src):
        def tile(n, carry):
            span = pl.ds(pl.multiple_of(n * 128, 128), 128)
            r.xt[:, span] = src[span, :].T
            return carry

        lax.fori_loop(0, tokens // 128, tile, 0)

    def grad_into(d, cols, right):
        def tile(m, carry):
            span = pl.ds(pl.multiple_of(m * 256, 256), 256)
            r.d[d, span, cols] = nn(r.xt[span, :], right()).astype(bf16)
            return carry

        lax.fori_loop(0, features // 256, tile, 0)

    def eight(values):
        return jnp.sum(values.reshape(values.shape[0] // 8, 8, values.shape[1]), axis=0)

    def collapse(values):
        return jnp.sum(values, axis=0, keepdims=True)

    def pair(e, n):
        span = pl.ds(n * half, half)
        return rcopy(
            r.sendbuf.at[span, :], r.recvs.at[e, span, :], r.e_send.at[e, n], r.e_recv.at[e, n], at.sibling()
        )

    zeros = jnp.zeros((8, features), f32)

    def back_up(z):
        need("hp%d" % z)

        def tile(n, carry):
            span = pl.ds(pl.multiple_of(n * half, half), half)
            hidden_delta = nn(r.dds[span, :], r.wa[z])
            pre = r.hp[z % 2, span, :]
            inner = jnp.tanh(gelu_a * (pre + gelu_b * pre * pre * pre))
            slope = 0.5 * (1.0 + inner) + 0.5 * pre * (1.0 - inner * inner) * (
                gelu_a * (1.0 + 3.0 * gelu_b * pre * pre)
            )
            delta = (hidden_delta * slope).astype(bf16)
            r.hs[z, span, :] = delta
            return carry + eight(delta.astype(f32))

        r.ubs[z] = collapse(lax.fori_loop(0, 2, tile, jnp.zeros((8, GC), f32)))
        if z + 2 < ts:
            load("hp%d" % (z + 2), r.hpre.at[z + 2], r.hp.at[z % 2])

    def grad_up(z):
        grad_into(slot(1, z), slice(None), lambda: r.hs[z])

    need("d30", "d31")
    rs_a(2, 0)
    rs_a(2, 1)
    need("dd", "w3", "n2t", "d32", "d33")
    back_up(0)
    grad_up(0)
    rs_b(2, 0)
    rs_a(2, 2)
    back_up(1)
    rs_b(2, 1)
    rs_a(2, 3)
    grad_up(1)
    bo_start()
    back_up(2)
    rs_c(2, 0)
    grad_up(2)
    back_up(3)
    load("w1", r.w1, r.wa)
    rs_b(2, 2)
    rs_a(1, 0)
    grad_up(3)
    rs_c(2, 1)
    need("w2")
    for n in range(2):
        span = slice(n * half, (n + 1) * half)
        for m in range(2):
            cols = slice(m * 512, (m + 1) * 512)
            acc = nt(r.hs[0, span, :], r.wb[0, cols, :])
            for z in range(1, ts):
                acc = acc + nt(r.hs[z, span, :], r.wb[z, cols, :])
            r.sendbuf[span, cols] = acc.astype(bf16)
        pair(0, n).start()
        if n == 0:
            rs_b(2, 3)
            rs_a(1, 1)
    need("mid", "b1", "mod", "g")

    def norm_two(n):
        def tile(i, sums):
            span = pl.ds(pl.multiple_of(n * half + i * step, step), step)
            incoming = r.sendbuf[span, :].astype(f32) + r.recvs[0, span, :].astype(f32)
            normal, inverse = normalize(r.mid[span, :].astype(f32))
            e = incoming * (1.0 + mod(4))
            mean_e = jnp.mean(e, axis=-1, keepdims=True)
            mean_en = jnp.mean(e * normal, axis=-1, keepdims=True)
            delta = r.gs[span, :].astype(f32) + (e - mean_e - normal * mean_en) * inverse
            r.hp[0, span, :] = delta[:, :512]
            r.hp[1, span, :] = delta[:, 512:]
            low = (delta * mod(2)).astype(bf16)
            r.dds[span, :] = low
            parts = (incoming, incoming * normal, delta * r.b1[span, :].astype(f32), low.astype(f32))
            return [a + eight(b) for a, b in zip(sums, parts)]

        return tile

    sums = [zeros] * 4
    for n in range(2):
        pair(0, n).wait()
        sums = lax.fori_loop(0, half // step, norm_two(n), sums)
    shift_two, scale_two, gate_one, output_bias = (collapse(v) for v in sums)
    load("x", r.x, r.gs)
    rs_b(1, 0)
    rs_a(1, 2)
    rs_c(2, 2)

    transpose(r.dds)
    need("att", "w1")
    for z in range(ts):
        if z == 2:
            rs_b(1, 1)
            rs_a(1, 3)
            rs_c(2, 3)
        grad_into(slot(0, z), slice(384, GC), lambda: r.atts[z])

        def tile(n, carry):
            span = pl.ds(pl.multiple_of(n * half, half), half)
            r.das[z, span, :] = nn(r.dds[span, :], r.wa[z, :, 384:]).astype(bf16)
            return carry

        lax.fori_loop(0, 2, tile, 0)
    load("n1t", r.n1t, r.xt)
    rs_b(1, 2)
    rs_c(1, 0)
    need("par", "qh", "kh", "v", "lse", "top", "gate2", "db")
    for z in range(ts):
        need("qp%d" % z, "kp%d" % z)
        attend_back(z, r, own_row(z, 0), own_row(z, 2))
        if z + 2 < ts:
            load_raw(z + 2)
        if z == 0:
            need("n1t")
        grad_into(slot(0, z), slice(0, 384), lambda: r.dqkv[z])
        rs_a(0, z)
        if z == 0:
            rs_b(1, 3)
            rs_c(1, 1)
        if z == 1:
            rs_b(0, 0)
            rs_c(1, 2)
        if z == 2:
            rs_b(0, 1)
            rs_c(1, 3)
        if z == 3:
            rs_b(0, 2)

    gate_two, down_bias = collapse(r.gates[...]), collapse(r.dbs[...])
    firsts = ((gate_one, shift_two, scale_two), (gate_two, output_bias, down_bias))
    for z in range(ts):
        lanes = slice(z * width, (z + 1) * width)
        for row in range(3):
            r.early[z, row : row + 1, :] = jnp.where(at.k == 0, firsts[0][row][:, lanes], firsts[1][row][:, lanes])
        for row in range(2):
            r.early[z, 3 + row : 4 + row, :128] = r.vec[z, 2 * row : 2 * row + 1, :]
            r.early[z, 3 + row : 4 + row, 128:] = r.vec[z, 2 * row + 1 : 2 * row + 2, :]
            r.early[z, 5 + row : 6 + row, :] = r.ubs[z, :, row * width : (row + 1) * width]
            r.early[z, 7:8, row * 128 : (row + 1) * 128] = r.tops[z, row : row + 1, :]

    def mail_slot(box):
        def slot_of(n):
            f, c, t = at.coords(n)
            return box.at[(f * 2 + c // 2) * ts + t, lax.rem(c, 2)]

        return slot_of

    def toward(box):
        return lambda n: box.at[lax.rem(n, ts)]

    m_start, m_wait = broadcast_messages(
        at, toward(r.early), mail_slot(r.mail_a), r.m_send, r.m_recv, r.loc.at[2]
    )
    l_start, l_wait = broadcast_messages(
        at, toward(r.late), mail_slot(r.mail_b), r.l_send, r.l_recv, r.loc.at[3]
    )
    m_start()
    for n in range(2):
        span = slice(n * half, (n + 1) * half)
        for m in range(2):
            cols = slice(m * 512, (m + 1) * 512)
            acc = nt(r.dqkv[0, span, :], r.wa[0, cols, :384])
            for z in range(1, ts):
                acc = acc + nt(r.dqkv[z, span, :], r.wa[z, cols, :384])
            r.sendbuf[span, cols] = acc.astype(bf16)
        pair(1, n).start()
    need("x")

    def norm_one(n):
        def tile(i, sums):
            span = pl.ds(pl.multiple_of(n * half + i * step, step), step)
            incoming = r.sendbuf[span, :].astype(f32) + r.recvs[1, span, :].astype(f32)
            normal, inverse = normalize(r.gs[span, :].astype(f32))
            e = incoming * (1.0 + mod(1))
            mean_e = jnp.mean(e, axis=-1, keepdims=True)
            mean_en = jnp.mean(e * normal, axis=-1, keepdims=True)
            middle_delta = jnp.concatenate([r.hp[0, span, :], r.hp[1, span, :]], axis=1)
            r.dds[span, :] = (middle_delta + (e - mean_e - normal * mean_en) * inverse).astype(bf16)
            return [a + eight(b) for a, b in zip(sums, (incoming, incoming * normal))]

        return tile

    sums = [zeros] * 2
    for n in range(2):
        pair(1, n).wait()
        sums = lax.fori_loop(0, half // step, norm_one(n), sums)
    shift_one, scale_one = (collapse(v) for v in sums)
    for z in range(ts):
        lanes = slice(z * width, (z + 1) * width)
        r.late[z] = jnp.where(at.k == 0, shift_one[:, lanes], scale_one[:, lanes])
    l_start()
    dx_start()
    rs_b(0, 3)
    rs_c(0, 0)
    rs_c(0, 1)
    rs_e(2)
    m_wait()
    rs_c(0, 2)
    pair_wait(2)
    rs_e(1)
    rs_c(0, 3)

    l_wait()
    partial = jnp.zeros(r.silu.shape, f32)
    six = [(r.mail_b, 0, 0), (r.mail_b, 1, 0), (r.mail_a, 0, 0), (r.mail_a, 0, 1), (r.mail_a, 0, 2), (r.mail_a, 1, 0)]
    for j, (box, side, row) in enumerate(six):
        value = box[:, side, row, :]
        for _ in range(3):
            low = value.astype(bf16)
            partial = partial + nt(low, r.wm[:, j * width : (j + 1) * width])
            value = value - low.astype(f32)
    r.silu[...] = partial
    r.silus[at.t] = partial

    def silu_copy(s, index):
        return rcopy(r.silu, r.silus.at[index], r.s_send.at[s], r.s_recv.at[s], at.zpeer(s))

    for s in range(1, ts):
        silu_copy(s, at.t).start()
    stores = [(r.mail_a, r.maila, 0), (r.mail_b, r.mailb, 1), (r.silu, r.sdel, 2)]
    for src, dst, n in stores[:2]:
        pltpu.make_async_copy(src, dst, r.out_sem.at[n]).start()
    bo_wait()
    pair_wait(1)
    for s in range(1, ts):
        silu_copy(s, at.zfrom(s)).wait()
    total = r.silus[0]
    for z in range(1, ts):
        total = total + r.silus[z]
    r.silu[...] = total
    pltpu.make_async_copy(r.silu, r.sdel, r.out_sem.at[2]).start()
    rs_e(0)
    dx_wait()
    for src, dst, n in stores:
        pltpu.make_async_copy(src, dst, r.out_sem.at[n]).wait()
    pair_wait(0)


def run_backward(fs, cs, ts, sent, padded, per, every, args):
    tokens, features = cs * padded, ts * 256
    f1 = max(fs - 1, 1)
    chunks = 3 * ts
    vm, dma, sds = pltpu.VMEM, pltpu.SemaphoreType.DMA, jax.ShapeDtypeStruct
    rows, cube = (tokens, features), (ts, tokens, 128)
    scratch = dict(
        gs=vm(rows, bf16), hs=vm((ts, tokens, GC), bf16), hp=vm((2, tokens, GC), f32),
        wa=vm((ts, features, GC), bf16), wb=vm((ts, features, GC), bf16),
        mid=vm(rows, bf16), dbs=vm((8, features), f32), b1=vm(rows, bf16), atts=vm(cube, bf16),
        qhs=vm(cube, bf16), khs=vm(cube, bf16), vs=vm(cube, bf16), lses=vm((ts, 2, tokens), f32),
        qp=vm((2, tokens, 128), f32), kp=vm((2, tokens, 128), f32), tops=vm((ts, 2, 128), f32), gates=vm((8, features), f32),
        mods=vm((8, features), f32), psum=vm((ts, 8, 128), f32),
        dds=vm(rows, bf16), xt=vm((features, tokens), bf16), sendbuf=vm(rows, bf16), recvs=vm((2, *rows), bf16),
        das=vm(cube, bf16), dqkv=vm((ts, tokens, 384), bf16), vec=vm((ts, 4, 128), f32), ubs=vm((ts, 1, GC), f32),
        dqa=vm((tokens, 128), f32), dka=vm((2, tokens, HD), f32), dva=vm((2, tokens, HD), f32),
        early=vm((ts, 8, 256), f32), late=vm((ts, 1, 256), f32),
        mail_a=vm((every, 2, 8, 256), f32), mail_b=vm((every, 2, 1, 256), f32),
        silu=vm((every, per), f32), silus=vm((ts, every, per), f32),
        d=vm((2 * ts, features, GC), bf16),
        r1=vm((chunks, f1, 2 * per, GC), bf16),
        rx2=vm((chunks, f1, 2 * per, GC), bf16), ry2=vm((chunks, 2 * per, GC), bf16),
        rz=vm((3, ts - 1, 2 * per, GC), bf16), total=vm((2 * per, GC), f32),
        in_sem=dma((40,)), loc=dma((4,)), out_sem=dma((3,)),
        l_send=dma((fs * cs * ts,)), l_recv=dma((fs * cs * ts,)), s_send=dma((ts,)), s_recv=dma((ts,)),
        bo_send=dma((2 * ts,)), bo_recv=dma((2 * ts,)), dx_send=dma((2 * ts,)), dx_recv=dma((2 * ts,)),
        y1_send=dma((chunks, fs)), y1_recv=dma((chunks, fs)), x1_send=dma((chunks, fs)), x1_recv=dma((chunks, fs)),
        x2_send=dma((chunks, fs)), x2_recv=dma((chunks, fs)), y2_send=dma((chunks,)), y2_recv=dma((chunks,)),
        z_send=dma((chunks,)), z_recv=dma((3, ts)), k_send=dma((3,)), k_recv=dma((3,)), k_loc=dma((3,)),
        e_send=dma((2, 2)), e_recv=dma((2, 2)), m_send=dma((fs * cs * ts,)), m_recv=dma((fs * cs * ts,)),
    )
    anywhere, on_chip = pl.BlockSpec(memory_space=pl.ANY), pl.BlockSpec(memory_space=vm)
    share = sds((2, per, GC), f32)
    blocks = sds((2 * ts, sent, 256), bf16)
    results = pl.pallas_call(
        functools.partial(
            backward_kernel, fs, cs, ts, sent, padded, per, BACKWARD_IN + BACKWARD_OUT + tuple(scratch)
        ),
        name="backward",
        out_shape=(
            share, share, share, blocks, blocks, sds((every, 2, 8, 256), f32), sds((every, 2, 1, 256), f32),
            sds((every, per), f32),
        ),
        in_specs=[anywhere] * (len(BACKWARD_IN) - 3) + [on_chip] * 3,
        out_specs=(anywhere,) * 8,
        scratch_shapes=list(scratch.values()),
        compiler_params=pltpu.CompilerParams(
            collective_id=1, has_side_effects=True, vmem_limit_bytes=63 << 20
        ),
    )(*[args[k] for k in BACKWARD_IN])
    return bundle(BACKWARD_OUT, results)


def on_device(
    fs, cs, ts,
    inputs, cotangent, labels, scale_ids, head_flags, class_table, modulate_weight, modulate_bias,
    query_weight, key_weight, value_weight, query_bias, value_bias, query_gain, key_gain,
    output_weight, output_bias, up_weight, up_bias, down_weight, down_bias,
):
    images, rows_here, width = inputs.shape
    if images != 2 * ts or cs != 4 or ts % 2 or width != 256:
        raise ValueError("unsupported mesh")
    length = scale_ids.shape[0]
    every = labels.shape[0]
    count = fs * cs * ts
    sent = -(-rows_here // 16) * 16
    padded = -(-rows_here // 64) * 64
    tokens = cs * padded
    features = ts * width
    per = query_weight.shape[0]
    part_cols = class_table.shape[1]
    f, c, t = (lax.axis_index(n) for n in ("fsdp", "ctx", "tp"))
    core = lax.rem(c, 2)
    block = f * cs + c

    classes = class_table.shape[0]
    onehot = (labels[:, None] == jnp.arange(classes, dtype=jnp.int32)[None, :]).astype(bf16)
    cond_part = jnp.dot(onehot, class_table, preferred_element_type=f32)
    cond_spread = lax.dynamic_update_slice(
        jnp.zeros((every, per), f32), cond_part, (0, t * part_cols)
    )
    fit = ((0, 0), (0, sent - rows_here), (0, 0))

    lanes = modulate_bias.shape[2]
    small_rows = jnp.concatenate(
        [
            modulate_bias.reshape(-1, lanes), query_bias, value_bias, query_gain, key_gain,
            output_bias, down_bias, up_bias,
        ],
        axis=0,
    )
    small = lax.dynamic_update_slice(
        jnp.zeros((small_rows.shape[0], HD), bf16), small_rows, (0, block * lanes)
    ).reshape(-1, 2 * HD)
    ids = scale_ids.reshape(cs, rows_here)
    spare = ((0, 0), (0, padded - rows_here))
    ids_query = jnp.pad(ids, spare, constant_values=-1).reshape(1, tokens)
    ids_key = jnp.pad(ids, spare, constant_values=1 << 20).reshape(tokens, 1)
    flat_modulate = modulate_weight.reshape(per, 6 * width)
    k = run_forward(
        fs, cs, ts, sent, padded, per, every,
        dict(
            xb=jnp.pad(inputs, fit), gb=jnp.pad(cotangent, fit),
            wq=query_weight, wk=key_weight, wv=value_weight, wu=up_weight, wo=output_weight, wd=down_weight,
            sp=small, cond=cond_spread,
            wm=flat_modulate, idq=ids_query, idk=ids_key,
        ),
    )
    m = run_backward(
        fs, cs, ts, sent, padded, per, every,
        {
            key: {"idq": ids_query, "idk": ids_key, "wm": flat_modulate}.get(key, getattr(k, key, None))
            for key in BACKWARD_IN
        },
    )
    heads = modulate_bias.shape[1]
    sum_one, sum_two, sum_three, dx_blocks, bo_blocks = m.o1, m.o2, m.o3, m.dxo, m.boo

    block_out = bo_blocks[:, :rows_here]
    inputs_grad = dx_blocks[:, :rows_here].astype(f32)

    def joined(parts):
        return parts.transpose(1, 0, 2).reshape(per, -1)

    query_weight_grad = joined(sum_one[:, :, :128])
    key_weight_grad = joined(sum_one[:, :, 128:256])
    value_weight_grad = joined(sum_one[:, :, 256:384])
    output_weight_grad = joined(sum_one[:, :, 384:]).T
    up_weight_grad = joined(sum_two)
    down_weight_grad = joined(sum_three).T
    mod_delta = jnp.concatenate(
        [m.mailb[:, 0], m.mailb[:, 1], m.maila[:, 0, :3], m.maila[:, 1, :1]], axis=1
    )
    sums = jnp.sum(m.maila, axis=0)
    same = jnp.concatenate([jnp.sum(mod_delta, axis=0), sums[1, 1:3]])
    halves_sum = sums[:, 3:7]

    def mine(values):
        return lax.dynamic_slice_in_dim(values, block * lanes, lanes, values.ndim - 1)

    same = mine(same.reshape(8, heads, HD))
    modulate_bias_grad, output_bias_grad, down_bias_grad = same[:6], same[6], same[7]
    quarter = mine(halves_sum[:, :2].reshape(2, 4, heads // 2, HD)).transpose(1, 0, 2, 3).reshape(4, heads, lanes)
    query_bias_grad, value_bias_grad, query_gain_grad, key_gain_grad = (quarter[j] for j in range(4))
    up_bias_grad = mine(halves_sum[:, 2:].reshape(-1, HD))
    head_max = jnp.max(m.maila[:, :, 7], axis=0).reshape(heads, 128)[:, 0]

    cond_rows = k.condr
    silu_cond = jax.nn.silu(cond_rows).astype(bf16)
    flat_delta = mod_delta.reshape(every, 6 * width)
    modulate_weight_grad = jnp.einsum(
        "bd,be->de", silu_cond.astype(f32), flat_delta, precision=precise
    ).reshape(per, 6, width)
    silu_cols = lax.dynamic_slice_in_dim(m.sdel, t * part_cols, part_cols, 1)
    primal, silu_back = jax.vjp(jax.nn.silu, cond_part)
    cond_delta = silu_back(silu_cols)[0]
    class_table_grad = jnp.dot(onehot.astype(f32).T, cond_delta, precision=precise)

    factor = jnp.where(
        head_flags == 1,
        jnp.sqrt(clip_threshold / jnp.maximum(head_max, clip_threshold)),
        jnp.ones_like(head_max),
    )
    columns = jnp.repeat(factor, HD)
    clipped_query = query_weight.astype(f32) * columns[None, :]
    clipped_key = key_weight.astype(f32) * columns[None, :]
    clipped_query_bias = query_bias.astype(f32) * factor[:, None]
    return (
        block_out, inputs_grad, class_table_grad, modulate_weight_grad, modulate_bias_grad,
        query_weight_grad, key_weight_grad, value_weight_grad, query_bias_grad, value_bias_grad,
        query_gain_grad, key_gain_grad, output_weight_grad, output_bias_grad,
        up_weight_grad, up_bias_grad, down_weight_grad, down_bias_grad,
        clipped_query, clipped_key, clipped_query_bias,
    )


def solution(mesh):
    rows = P("fsdp", "ctx", "tp")
    table = P(None, ("fsdp", "ctx", "tp"))
    left = P(("fsdp", "ctx"), "tp")
    right = P("tp", ("fsdp", "ctx"))
    modulate = P(("fsdp", "ctx"), None, "tp")
    modulate_small = P(None, "tp", ("fsdp", "ctx"))
    return jax.shard_map(
        functools.partial(on_device, mesh.shape["fsdp"], mesh.shape["ctx"], mesh.shape["tp"]),
        mesh=mesh,
        in_specs=(
            rows, rows, P(), P(), P("tp"), table, modulate, modulate_small,
            left, left, left, right, right, right, right,
            right, right, left, right, right, right,
        ),
        out_specs=(
            rows, rows, table, modulate, modulate_small,
            left, left, left, right, right, right, right,
            right, right, left, right, right, right,
            left, left, right,
        ),
        check_vma=False,
    )
```

```python
import functools
import math

import jax
import jax.numpy as jnp
from jax import lax
from jax.experimental import pallas as pl
from jax.experimental.pallas import tpu as pltpu
from jax.sharding import PartitionSpec as P

HD = 64
GC = 512
CHUNK = 256
MESH = pl.DeviceIdType.MESH
precise = lax.Precision.HIGHEST
norm_epsilon = 1e-06
clip_threshold = 2.0
masked_score = -1e30
f32, bf16 = jnp.float32, jnp.bfloat16


def product(left, right, form):
    return jnp.einsum(form, left, right, preferred_element_type=f32)


def rcopy(src, dst, send_sem, recv_sem, device):
    return pltpu.make_async_remote_copy(
        src_ref=src,
        dst_ref=dst,
        send_sem=send_sem,
        recv_sem=recv_sem,
        device_id=device,
        device_id_type=MESH,
    )


class Place:
    def __init__(self, fs, cs, ts):
        self.fs, self.cs, self.ts = fs, cs, ts
        self.count = fs * cs * ts
        self.f, self.c, self.t = (lax.axis_index(n) for n in ("fsdp", "ctx", "tp"))
        self.hi, self.k = self.c // 2, lax.rem(self.c, 2)
        self.me = (self.f * cs + self.c) * ts + self.t
        self.slot = self.hi * ts + self.t

    def coords(self, n):
        return (n // (self.cs * self.ts), lax.rem(n // self.ts, self.cs), lax.rem(n, self.ts))

    def sibling(self):
        return (self.f, self.hi * 2 + 1 - self.k, self.t)

    def ypeer(self):
        return (self.f, (1 - self.hi) * 2 + self.k, self.t)

    def xpeer(self, s):
        return (lax.rem(self.f + s, self.fs), self.c, self.t)

    def xfrom(self, s):
        return lax.rem(self.f + self.fs - s, self.fs)

    def zpeer(self, s):
        return (self.f, self.c, lax.rem(self.t + s, self.ts))

    def zto(self, s):
        return lax.rem(self.t + s, self.ts)

    def zfrom(self, s):
        return lax.rem(self.t + self.ts - s, self.ts)

    def barrier(self):
        sem = pltpu.get_barrier_semaphore()

        def greet(n, carry):
            @pl.when(n != self.me)
            def _():
                pl.semaphore_signal(sem, inc=1, device_id=self.coords(n), device_id_type=MESH)

            return carry

        lax.fori_loop(0, self.count, greet, 0)
        pl.semaphore_wait(sem, self.count - 1)


def exchange_images(at, src_of, dst_of, send_sems, recv_sems, local_sem):
    slots = 2 * at.ts

    def start():
        for i in range(slots):
            hi, t = i // at.ts, i % at.ts

            @pl.when(i != at.slot)
            def _():
                rcopy(
                    src_of(i),
                    dst_of(at.slot),
                    send_sems.at[i],
                    recv_sems.at[at.slot],
                    (at.f, hi * 2 + at.k, t),
                ).start()

            @pl.when(i == at.slot)
            def _():
                pltpu.make_async_copy(src_of(i), dst_of(i), local_sem).start()

    def wait():
        for i in range(slots):
            @pl.when(i != at.slot)
            def _():
                rcopy(src_of(i), dst_of(i), send_sems.at[i], recv_sems.at[i], (at.f, at.c, at.t)).wait()

            @pl.when(i == at.slot)
            def _():
                pltpu.make_async_copy(src_of(i), dst_of(i), local_sem).wait()

    return start, wait


def broadcast_messages(at, src_of, slot_of, send_sems, recv_sems, local_sem):
    def start():
        def each(n, carry):
            @pl.when(n != at.me)
            def _():
                rcopy(src_of(n), slot_of(at.me), send_sems.at[n], recv_sems.at[at.me], at.coords(n)).start()

            @pl.when(n == at.me)
            def _():
                pltpu.make_async_copy(src_of(n), slot_of(n), local_sem).start()

            return carry

        lax.fori_loop(0, at.count, each, 0)

    def wait():
        def each(n, carry):
            @pl.when(n != at.me)
            def _():
                rcopy(src_of(n), slot_of(n), send_sems.at[n], recv_sems.at[n], at.coords(n)).wait()

            @pl.when(n == at.me)
            def _():
                pltpu.make_async_copy(src_of(n), slot_of(n), local_sem).wait()

            return carry

        lax.fori_loop(0, at.count, each, 0)

    return start, wait


FORWARD_IN = ("xb", "gb", "wq", "wk", "wv", "wu", "wo", "wd", "sp", "cond", "wm", "idq", "idk")
FORWARD_OUT = (
    "w1", "w2", "w3", "x", "g", "normed1", "qpre", "kpre", "v", "qh", "kh", "att", "branch1",
    "middle", "normed2", "hpre", "hid", "bo", "lse", "top", "mod", "par", "gate2",
    "dd", "d3", "n1t", "n2t", "db", "condr", "r1o",
)


def parts_of(z):
    cut = GC // 2 if z % 2 == 0 else GC // 4
    return slice(cut, GC), slice(0, cut)


class Refs:
    pass


def bundle(keys, values):
    refs = Refs()
    for key, value in zip(keys, values, strict=True):
        setattr(refs, key, value)
    return refs


def normalize(values):
    centered = values - jnp.mean(values, axis=-1, keepdims=True)
    inverse = lax.rsqrt(jnp.mean(centered * centered, axis=-1, keepdims=True) + norm_epsilon)
    return centered * inverse, inverse


def nt(left, right):
    return lax.dot_general(left, right, (((1,), (1,)), ((), ())), preferred_element_type=f32)


def nn(left, right):
    return lax.dot_general(left, right, (((1,), (0,)), ((), ())), preferred_element_type=f32)


def segment_mean(values):
    row = lax.broadcasted_iota(jnp.int32, (2 * HD, 2 * HD), 0) < HD
    col = lax.broadcasted_iota(jnp.int32, (2 * HD, 2 * HD), 1) < HD
    same = jnp.where(row == col, 1.0 / HD, 0.0).astype(bf16)
    high = values.astype(bf16)
    rest = values - high.astype(f32)
    middle = rest.astype(bf16)
    low = (rest - middle.astype(f32)).astype(bf16)
    return nn(high, same) + nn(middle, same) + nn(low, same)


def head_inverse(values):
    return lax.rsqrt(segment_mean(values * values) + norm_epsilon)


gelu_a = math.sqrt(2.0 / math.pi)
gelu_b = 0.044715


def forward_kernel(fs, cs, ts, sent, padded, per, keys, *values):
    r = bundle(keys, values)
    at = Place(fs, cs, ts)
    width = 256
    tokens, features = r.xs.shape
    half = tokens // 2
    quarter = features // ts
    zero = jnp.zeros((padded - sent, features), bf16)
    for c in range(cs):
        r.xs[c * padded + sent : (c + 1) * padded, :] = zero
        r.gs[c * padded + sent : (c + 1) * padded, :] = zero
    at.barrier()

    def block_at(out):
        def dst(i):
            c = (i // ts) * 2 + at.k
            return out.at[
                pl.ds(pl.multiple_of(c * padded, padded), sent),
                pl.ds(pl.multiple_of(lax.rem(i, ts) * width, width), width),
            ]

        return dst

    x_start, x_wait = exchange_images(at, lambda i: r.xb.at[i], block_at(r.xs), r.x_send, r.x_recv, r.loc.at[0])
    g_start, g_wait = exchange_images(at, lambda i: r.gb.at[i], block_at(r.gs), r.g_send, r.g_recv, r.loc.at[1])

    r.wot[...] = r.wo[...].T
    r.wdt[...] = r.wd[...].T
    pieces, items = [[(r.sp, None, None)]], [(r.parts, None, r.sp.shape[0])]
    for col, sources in ((0, (r.wq,)), (128, (r.wk,)), (256, (r.wv, r.wot))):
        pieces.append([(ref, 128, (0, 128, col + 128 * i)) for i, ref in enumerate(sources)])
        items.append((r.w1s, slice(col, col + 128 * len(sources)), per))
    for full, ref, widths in ((r.w2s, r.wu, (256, 256)), (r.w3s, r.wdt, (256, 128, 128))):
        col = 0
        for w in widths:
            pieces.append([(ref, w, (col, GC, col))])
            items.append((full, slice(col, col + w), per))
            col += w

    def slab(n, z, nz, f, hi, k=0, blocks=2):
        full, cols, size = items[n]
        row = pl.multiple_of(((f * 2 + hi) * 2 + k) * size, size)
        span = pl.ds(row, blocks * size)
        return full.at[pl.ds(z, nz), span, :] if cols is None else full.at[pl.ds(z, nz), span, cols]

    def core_pair(n):
        full, _, size = items[n]

        def place(z, k, cols):
            span = pl.ds(pl.multiple_of(((at.f * 2 + at.hi) * 2 + k) * size, size), size)
            return full.at[z, span, :] if cols is None else full.at[z, span, cols]

        copies = []
        for i, (ref, w, where) in enumerate(pieces[n]):
            if where is None:
                mine, theirs, cols = ref, ref, None
            else:
                start, stride, col = where
                mine, theirs = (
                    ref.at[:, pl.ds(pl.multiple_of(start + k * stride, 128), w)] for k in (at.k, 1 - at.k)
                )
                cols = slice(col, col + w)
            sems = (r.core_send.at[n, i], r.core_recv.at[n, i], at.sibling())
            copies.append(
                (
                    functools.partial(pltpu.make_async_copy, mine, place(at.t, at.k, cols), r.core_loc.at[n, i]),
                    functools.partial(rcopy, theirs, place(at.t, at.k, cols), *sems),
                    functools.partial(rcopy, theirs, place(at.t, 1 - at.k, cols), *sems),
                )
            )
        return copies

    def core_start(n):
        for keep, out, _ in core_pair(n):
            keep().start()
            out().start()

    def core_wait(n):
        for keep, _, inn in core_pair(n):
            keep().wait()
            inn().wait()

    def hop(n, d, up, action):
        block = at.t - d if up else at.t + d
        sends = ((block >= 0) & (at.t < ts - 1)) if up else ((block < ts) & (at.t > 0))

        @pl.when(sends)
        def _():
            src = slab(n, block, 1, at.f, at.hi)
            side = 0 if up else 1
            copy = rcopy(
                src, src, r.z_send.at[side, n, d], r.z_recv.at[side, n, d + 1],
                (at.f, at.c, at.t + 1 if up else at.t - 1),
            )
            copy.start() if action == "start" else copy.wait_send()

    def z_start(n):
        hop(n, 0, True, "start")
        hop(n, 0, False, "start")

    def z_step(n, d):
        for up in (True, False):
            block = at.t - d if up else at.t + d

            @pl.when((block >= 0) & (block < ts))
            def _():
                src = slab(n, block, 1, at.f, at.hi)
                side = 0 if up else 1
                rcopy(
                    src, src, r.z_send.at[side, n, d], r.z_recv.at[side, n, d], (at.f, at.c, at.t)
                ).wait_recv()

            if d < ts - 1:
                hop(n, d, up, "start")

    def z_wait(n):
        for d in range(1, ts):
            z_step(n, d)

    def direct_start(n):
        for s in range(1, ts):
            src = slab(n, at.t, 1, at.f, at.hi)
            rcopy(src, src, r.zd_send.at[n, s], r.zd_recv.at[n, s], at.zpeer(s)).start()

    def direct_wait(n):
        for s in range(1, ts):
            src = slab(n, at.zfrom(s), 1, at.f, at.hi)
            rcopy(src, src, r.zd_send.at[n, s], r.zd_recv.at[n, s], at.zpeer(s)).wait()

    def own(f, hi, k=0, n=2):
        return slab(last, at.t, 1, f, hi, k, n)

    def tail_own(action):
        src = own(at.f, at.hi)
        rcopy(src, src, r.ys_send.at[last], r.ys_recv.at[last], at.ypeer()).start()
        for s in range(1, fs):
            rcopy(src, src, r.xs_send.at[last, s], r.xs_recv.at[last, s], at.xpeer(s)).start()

    def tail_forward():
        src = own(at.f, 1 - at.hi)
        rcopy(src, src, r.ys_send.at[last], r.ys_recv.at[last], at.ypeer()).wait()
        for s in range(1, fs):
            src = own(at.xfrom(s), at.hi)
            rcopy(src, src, r.xs_send.at[last, s], r.xs_recv.at[last, s], at.xpeer(s)).wait()
        for s in range(1, fs):
            src = own(at.f, 1 - at.hi, 1, 1)
            rcopy(src, src, r.fx_send.at[last, s], r.fx_recv.at[last, s], at.xpeer(s)).start()
            src = own(at.xfrom(s), at.hi, 0, 1)
            rcopy(src, src, r.fy_send.at[last, s], r.fy_recv.at[last, s], at.ypeer()).start()

    def tail_arrived():
        for s in range(1, fs):
            src = own(at.xfrom(s), 1 - at.hi, 1, 1)
            rcopy(src, src, r.fx_send.at[last, s], r.fx_recv.at[last, s], at.xpeer(s)).wait()
            src = own(at.xfrom(s), 1 - at.hi, 0, 1)
            rcopy(src, src, r.fy_send.at[last, s], r.fy_recv.at[last, s], at.ypeer()).wait()

    def tail_block(z):
        full, cols, _ = items[last]
        return full.at[pl.ds(z, 1), :, cols]

    def tail_hop(d, up, action):
        block = at.t - d if up else at.t + d
        sends = ((block >= 0) & (at.t < ts - 1)) if up else ((block < ts) & (at.t > 0))

        @pl.when(sends)
        def _():
            src = tail_block(block)
            side = 0 if up else 1
            copy = rcopy(
                src, src, r.z_send.at[side, last, d], r.z_recv.at[side, last, d + 1],
                (at.f, at.c, at.t + 1 if up else at.t - 1),
            )
            copy.start() if action == "start" else copy.wait_send()

    def tail_step(d):
        for up in (True, False):
            block = at.t - d if up else at.t + d
            if d > 0:

                @pl.when((block >= 0) & (block < ts))
                def _():
                    src = tail_block(block)
                    side = 0 if up else 1
                    rcopy(
                        src, src, r.z_send.at[side, last, d], r.z_recv.at[side, last, d], (at.f, at.c, at.t)
                    ).wait_recv()

            if d < ts - 1:
                tail_hop(d, up, "start")

    def z_sent(n):
        for d in range(ts - 1):
            for up in (True, False):
                hop(n, d, up, "sent")

    def xy_start(n):
        src = slab(n, 0, ts, at.f, at.hi)
        rcopy(src, src, r.ys_send.at[n], r.ys_recv.at[n], at.ypeer()).start()
        for s in range(1, fs):
            rcopy(src, src, r.xs_send.at[n, s], r.xs_recv.at[n, s], at.xpeer(s)).start()

    def xy_wait(n):
        src = slab(n, 0, ts, at.f, 1 - at.hi)
        rcopy(src, src, r.ys_send.at[n], r.ys_recv.at[n], at.ypeer()).wait()
        for s in range(1, fs):
            src = slab(n, 0, ts, at.xfrom(s), at.hi)
            rcopy(src, src, r.xs_send.at[n, s], r.xs_recv.at[n, s], at.xpeer(s)).wait()

    def fwd_start(n):
        zh = ts // 2 - n % 2
        for s in range(1, fs):
            src = slab(n, zh, ts - zh, at.f, 1 - at.hi)
            rcopy(src, src, r.fx_send.at[n, s], r.fx_recv.at[n, s], at.xpeer(s)).start()
            src = slab(n, 0, zh, at.xfrom(s), at.hi)
            rcopy(src, src, r.fy_send.at[n, s], r.fy_recv.at[n, s], at.ypeer()).start()

    def fwd_wait(n):
        zh = ts // 2 - n % 2
        for s in range(1, fs):
            src = slab(n, zh, ts - zh, at.xfrom(s), 1 - at.hi)
            rcopy(src, src, r.fx_send.at[n, s], r.fx_recv.at[n, s], at.xpeer(s)).wait()
            src = slab(n, 0, zh, at.xfrom(s), 1 - at.hi)
            rcopy(src, src, r.fy_send.at[n, s], r.fy_recv.at[n, s], at.ypeer()).wait()

    last = len(items) - 1
    saved = []

    def save(src, out):
        copy = pltpu.make_async_copy(src, out, r.out_sem.at[len(saved)])
        copy.start()
        saved.append([src, out, True])
        return len(saved) - 1

    def settle(n):
        src, out, waiting = saved[n]
        if waiting:
            pltpu.make_async_copy(src, out, r.out_sem.at[n]).wait()
            saved[n][2] = False

    def transpose(src):
        def tile(n, carry):
            span = pl.ds(pl.multiple_of(n * 128, 128), 128)
            r.xt[:, span] = src[span, :].T
            return carry

        lax.fori_loop(0, tokens // 128, tile, 0)

    r.cond_slots[at.t] = r.cond[...]

    def cond_copy(s, slot):
        return rcopy(r.cond, r.cond_slots.at[slot], r.c_send.at[s], r.c_recv.at[s], at.zpeer(s))

    for s in range(1, ts):
        cond_copy(s, at.t).start()
    for n in (0, 1, last, 2, 3):
        core_start(n)
    core_wait(0)
    direct_start(0)
    core_wait(1)
    direct_start(1)
    core_wait(last)
    tail_own("start")
    for n in range(4, last):
        core_start(n)
    core_wait(2)
    z_start(2)
    direct_wait(0)
    xy_start(0)

    for s in range(1, ts):
        cond_copy(s, at.zfrom(s)).wait()
    cond = r.cond_slots[0]
    for z in range(1, ts):
        cond = cond + r.cond_slots[z]
    r.crow[...] = cond
    save(r.crow, r.condr)
    silu = (cond / (1.0 + jnp.exp(-cond))).astype(bf16)
    for j in range(6):
        r.part[:, j, :] = nn(silu, r.wm[j])

    def image_of(n):
        f, c, t = at.coords(n)
        return (f * 2 + c // 2) * ts + t

    m_start, m_wait = broadcast_messages(
        at, lambda n: r.part.at[image_of(n)], lambda n: r.msg.at[n], r.m_send, r.m_recv, r.loc.at[2]
    )
    xy_wait(0)
    fwd_start(0)
    tail_forward()
    direct_wait(1)
    xy_start(1)
    z_step(2, 1)
    core_wait(3)
    z_start(3)
    z_step(2, 2)
    z_step(2, 3)
    xy_start(2)
    xy_wait(1)
    fwd_start(1)
    z_step(3, 1)
    m_start()
    z_step(3, 2)
    xy_wait(2)
    fwd_start(2)
    z_step(3, 3)
    xy_start(3)
    x_start()
    for n in range(4, last):
        core_wait(n)
    fwd_wait(0)
    m_wait()
    z_start(4)

    blocks = fs * cs
    rows_small = r.sp.shape[0]

    def small_sum(n, carry):
        return carry + r.parts[:, pl.ds(pl.multiple_of(n * rows_small, rows_small), rows_small), :].astype(f32)

    r.psum[...] = lax.fori_loop(0, blocks, small_sum, jnp.zeros(r.psum.shape, f32))
    for z in range(ts):

        def mod_sum(n, carry):
            return carry + r.msg[n * ts + z]

        total = lax.fori_loop(0, blocks, mod_sum, jnp.zeros((8, width), f32))
        for j in range(6):
            for h in range(2):
                value = total[j : j + 1, h * 128 : (h + 1) * 128] + r.psum[z, 2 * j + h : 2 * j + h + 1, :]
                r.mods[j : j + 1, z * width + h * 128 : z * width + (h + 1) * 128] = value.astype(bf16).astype(f32)
                if j < 2:
                    row = r.psum[z, 20 + 2 * j + h : 21 + 2 * j + h, :]
                    r.mods[6 + j : 7 + j, z * width + h * 128 : z * width + (h + 1) * 128] = row

    def mod(j):
        return r.mods[j : j + 1, :]

    def own_row(z, start):
        return r.psum[z, pl.ds(start + at.k, 1), :]

    z_step(4, 1)
    xy_wait(3)
    fwd_start(3)
    z_step(4, 2)
    z_start(5)
    x_wait()

    def sib_pair(buf, send, recv, hi):
        mine = buf.at[pl.ds(pl.multiple_of((hi * 2 + at.k) * padded, padded), sent), :]
        theirs = buf.at[pl.ds(pl.multiple_of((hi * 2 + 1 - at.k) * padded, padded), sent), :]
        return (
            functools.partial(rcopy, mine, mine, send.at[hi], recv.at[hi], at.sibling()),
            functools.partial(rcopy, theirs, theirs, send.at[hi], recv.at[hi], at.sibling()),
        )

    for hi in range(2):
        sib_pair(r.xs, r.sib_send, r.sib_recv, hi)[0]().start()
    z_step(4, 3)
    xy_start(4)
    for hi in range(2):
        sib_pair(r.xs, r.sib_send, r.sib_recv, hi)[1]().wait()
    save(r.xs, r.x)

    step = 64

    def norm_tile(src, dst, shift, scale):
        def tile(n, carry):
            span = pl.ds(pl.multiple_of(n * step, step), step)
            normal, _ = normalize(src[span, :].astype(f32))
            dst[span, :] = (normal * (1.0 + mod(scale)) + mod(shift)).astype(bf16)
            return carry

        lax.fori_loop(0, tokens // step, tile, 0)

    norm_tile(r.xs, r.n1, 0, 1)
    save(r.n1, r.normed1)
    z_step(5, 1)
    fwd_wait(1)
    fwd_wait(2)

    def query_key(i, carry):
        z = i // 2
        span = pl.ds(pl.multiple_of(lax.rem(i, 2) * half, half), half)
        raw = nn(r.n1[span, :], r.w1s[z, :, : 2 * 128])
        q = raw[:, :128] + own_row(z, 12)
        k = raw[:, 128:256]
        r.qp[z, span, :] = q
        r.kp[z, span, :] = k
        r.qhs[z, span, :] = (q * head_inverse(q) * own_row(z, 16)).astype(bf16)
        r.khs[z, span, :] = (k * head_inverse(k) * own_row(z, 18)).astype(bf16)
        return carry

    def value(i, carry):
        z = i // 2
        span = pl.ds(pl.multiple_of(lax.rem(i, 2) * half, half), half)
        r.vs[z, span, :] = (nn(r.n1[span, :], r.w1s[z, :, 2 * 128 : 3 * 128]) + own_row(z, 14)).astype(bf16)
        return carry

    lax.fori_loop(0, ts, query_key, 0)
    z_step(5, 2)
    z_start(6)
    lax.fori_loop(ts, 2 * ts, query_key, 0)
    z_step(5, 3)
    xy_start(5)
    fwd_wait(3)
    save(r.w1s, r.w1)
    lax.fori_loop(0, 2 * ts, value, 0)
    tail_arrived()
    transpose(r.n1)
    n1t = save(r.xt, r.n1t)
    for src, out in ((r.qp, r.qpre), (r.kp, r.kpre), (r.vs, r.v), (r.qhs, r.qh), (r.khs, r.kh)):
        save(src, out)
    z_step(6, 1)

    qt = 256

    def attend(z):
        v_t = r.vs[z].T
        tops = [jnp.full((1, qt), masked_score, f32) for _ in range(2)]

        def tile(n, tops):
            span = pl.ds(pl.multiple_of(n * qt, qt), qt)
            allowed = r.idk[...] <= r.idq[:, span]
            outs, peaks = [], []
            for h in range(2):
                lanes = slice(h * HD, (h + 1) * HD)
                s = nt(r.khs[z, :, lanes], r.qhs[z, span, lanes] * 0.125)
                s = jnp.where(allowed, s, masked_score)
                peak = jnp.max(s, axis=0, keepdims=True)
                e = jnp.exp(s - peak)
                total = jnp.sum(e, axis=0, keepdims=True)
                r.lses[z, h : h + 1, span] = peak + jnp.log(total)
                p = (e * (1.0 / total)).astype(bf16)
                outs.append(nn(v_t[h * HD : (h + 1) * HD, :], p))
                peaks.append(jnp.maximum(tops[h], peak))
            r.atts[z, span, :] = jnp.concatenate(outs, axis=0).T.astype(bf16)
            return peaks

        tops = lax.fori_loop(0, tokens // qt, tile, tops)
        for h in range(2):
            r.tops[z, h : h + 1, :] = jnp.broadcast_to(jnp.max(tops[h], axis=1, keepdims=True), (1, 128))

    attend(0)
    xy_wait(4)
    fwd_start(4)
    z_step(6, 2)
    z_start(7)
    z_step(6, 3)
    xy_start(6)
    tail_step(0)
    attend(1)
    z_step(7, 1)
    z_step(7, 2)
    attend(2)
    xy_wait(5)
    fwd_start(5)
    z_step(7, 3)
    xy_start(7)
    g_start()
    tail_step(1)
    attend(3)
    fwd_wait(4)
    for src, out in ((r.atts, r.att), (r.lses, r.lse), (r.tops, r.top)):
        save(src, out)

    def pair(e, n):
        span = pl.ds(n * half, half)
        return rcopy(
            r.sendbuf.at[span, :], r.recvs.at[e, span, :], r.e_send.at[e, n], r.e_recv.at[e, n], at.sibling()
        )

    for n in range(2):
        span = slice(n * half, (n + 1) * half)
        for c in range(2):
            cols = slice(c * 512, (c + 1) * 512)
            acc = nt(r.atts[0, span, :], r.w1s[0, cols, 384:])
            for z in range(1, ts):
                acc = acc + nt(r.atts[z, span, :], r.w1s[z, cols, 384:])
            r.sendbuf[span, cols] = acc.astype(bf16)
        pair(0, n).start()
    for n in range(2):
        pair(0, n).wait()

        def tile(i, carry):
            span = pl.ds(pl.multiple_of(n * half + i * step, step), step)
            branch = r.sendbuf[span, :].astype(f32) + r.recvs[0, span, :].astype(f32) + mod(6)
            r.b1[span, :] = branch.astype(bf16)
            middle = (r.xs[span, :].astype(f32) + mod(2) * branch).astype(bf16)
            r.mid[span, :] = middle
            normal, _ = normalize(middle.astype(f32))
            r.n2[span, :] = (normal * (1.0 + mod(4)) + mod(3)).astype(bf16)
            return carry

        lax.fori_loop(0, half // step, tile, 0)
    for src, out in ((r.b1, r.branch1), (r.mid, r.middle), (r.n2, r.normed2)):
        save(src, out)

    def up_part(c):
        cols = slice(c * CHUNK, (c + 1) * CHUNK)

        def body(i, carry):
            z = i // 2
            span = pl.ds(pl.multiple_of(lax.rem(i, 2) * half, half), half)
            pre = nn(r.n2[span, :], r.w2s[z, :, cols])
            bias = [r.psum[z, pl.ds(24 + 4 * at.k + 2 * c + j, 1), :] for j in range(2)]
            pre = pre + jnp.concatenate(bias, axis=1)
            r.hp[z, span, cols] = pre
            inner = jnp.tanh(gelu_a * (pre + gelu_b * pre * pre * pre))
            r.hs[z, span, cols] = (0.5 * pre * (1.0 + inner)).astype(bf16)
            return carry

        lax.fori_loop(0, 2 * ts, body, 0)

    xy_wait(6)
    fwd_start(6)
    tail_step(2)
    up_part(0)
    g_wait()
    for hi in range(2):
        sib_pair(r.gs, r.gsib_send, r.gsib_recv, hi)[0]().start()
    fwd_wait(5)
    save(r.w2s, r.w2)
    up_part(1)
    save(r.hp, r.hpre)
    save(r.hs, r.hid)
    xy_wait(7)
    fwd_start(7)
    settle(n1t)
    transpose(r.n2)
    n2t = save(r.xt, r.n2t)
    for hi in range(2):
        sib_pair(r.gs, r.gsib_send, r.gsib_recv, hi)[1]().wait()
    save(r.gs, r.g)

    def diagonal(z):
        copies = []
        x_part, y_part = parts_of(z)
        for s in range(1, fs):
            span = pl.ds(row_of(lax.rem(at.f + s, fs), 1 - at.hi), 2 * per)
            for part, sends, receives, device in (
                (y_part, r.dy_send, r.dy_recv, at.ypeer()), (x_part, r.dx_send, r.dx_recv, at.xpeer(s)),
            ):
                copies.append(
                    rcopy(
                        r.d3s.at[z, span, part], r.r1o.at[z, s - 1, :, part],
                        sends.at[z, s], receives.at[z, s], device,
                    )
                )
        return copies

    def row_of(f, hi):
        return pl.multiple_of((f * 2 + hi) * 2 * per, 2 * per)

    def delta_tile(n, carry):
        span = pl.ds(pl.multiple_of(n * step, step), step)
        delta = (r.gs[span, :].astype(f32) * mod(5)).astype(bf16)
        r.dds[span, :] = delta
        return carry + jnp.sum(delta.astype(f32).reshape(step // 8, 8, features), axis=0)

    r.dbs[...] = lax.fori_loop(0, tokens // step, delta_tile, jnp.zeros((8, features), f32))
    save(r.dbs, r.db)
    save(r.dds, r.dd)
    settle(n2t)
    transpose(r.dds)
    for z in range(ts):

        def grad_tile(m, carry):
            span = pl.ds(pl.multiple_of(m * 256, 256), 256)
            r.d3s[z, span, :] = nn(r.xt[span, :], r.hs[z]).astype(bf16)
            return carry

        lax.fori_loop(0, features // 256, grad_tile, 0)
        save(r.d3s.at[z], r.d3.at[z])
        for copy in diagonal(z):
            copy.start()

    def down_part(c, first):
        cols = slice(c * CHUNK, (c + 1) * CHUNK)
        for n in range(2):
            span = slice(n * half, (n + 1) * half)
            for m in range(2):
                rows = slice(m * 512, (m + 1) * 512)
                acc = nt(r.hs[0, span, cols], r.w3s[0, rows, cols])
                for z in range(1, ts):
                    acc = acc + nt(r.hs[z, span, cols], r.w3s[z, rows, cols])
                if first:
                    r.acc[span, rows] = acc
                else:
                    r.sendbuf[span, rows] = (r.acc[span, rows] + acc).astype(bf16)
            if not first:
                pair(1, n).start()

    fwd_wait(6)
    down_part(0, True)
    fwd_wait(7)
    tail_step(3)
    save(r.w3s, r.w3)
    down_part(1, False)
    for n in range(2):
        pair(1, n).wait()

        def tile(i, carry):
            span = pl.ds(pl.multiple_of(n * half + i * step, step), step)
            branch = r.sendbuf[span, :].astype(f32) + r.recvs[1, span, :].astype(f32) + mod(7)
            r.bos[span, :] = (r.mid[span, :].astype(f32) + mod(5) * branch).astype(bf16)
            product = r.gs[span, :].astype(f32) * branch
            return carry + jnp.sum(product.reshape(step // 8, 8, features), axis=0)

        part = lax.fori_loop(0, half // step, tile, jnp.zeros((8, features), f32))
        if n == 0:
            r.gates[...] = part
        else:
            r.gates[...] += part
    for src, out in ((r.bos, r.bo), (r.gates, r.gate2), (r.mods, r.mod), (r.psum, r.par)):
        save(src, out)
    for z in range(ts):
        for copy in diagonal(z):
            copy.wait()
    for n in range(2, last):
        z_sent(n)
    for d in range(ts - 1):
        for up in (True, False):
            tail_hop(d, up, "sent")
    for n in range(len(saved)):
        settle(n)


def run_forward(fs, cs, ts, sent, padded, per, every, args):
    tokens, features = cs * padded, ts * 256
    sds = jax.ShapeDtypeStruct
    big = (ts, features, GC)
    outs = {
        "w1": (big, bf16), "w2": (big, bf16), "w3": (big, bf16),
        "x": ((tokens, features), bf16), "g": ((tokens, features), bf16), "normed1": ((tokens, features), bf16),
        "qpre": ((ts, tokens, 128), f32), "kpre": ((ts, tokens, 128), f32),
        "v": ((ts, tokens, 128), bf16), "qh": ((ts, tokens, 128), bf16), "kh": ((ts, tokens, 128), bf16),
        "att": ((ts, tokens, 128), bf16), "branch1": ((tokens, features), bf16),
        "middle": ((tokens, features), bf16), "normed2": ((tokens, features), bf16),
        "hpre": ((ts, tokens, GC), f32), "hid": ((ts, tokens, GC), bf16), "bo": ((tokens, features), bf16),
        "lse": ((ts, 2, tokens), f32), "top": ((ts, 2, 128), f32), "mod": ((8, features), f32),
        "par": ((ts, 32, 128), f32), "gate2": ((8, features), f32),
        "dd": ((tokens, features), bf16), "d3": (big, bf16), "n1t": ((features, tokens), bf16),
        "n2t": ((features, tokens), bf16), "db": ((8, features), f32), "condr": ((every, per), f32),
        "r1o": ((ts, max(fs - 1, 1), 2 * per, GC), bf16),
    }
    vm, dma = pltpu.VMEM, pltpu.SemaphoreType.DMA
    local = dict(
        w1s="w1", w2s="w2", w3s="w3", xs="x", gs="g", n1="normed1", qp="qpre", kp="kpre", vs="v", qhs="qh",
        khs="kh", atts="att", b1="branch1", mid="middle", n2="normed2", hp="hpre", hs="hid", bos="bo",
        lses="lse", tops="top", mods="mod", psum="par", gates="gate2",
        dds="dd", d3s="d3", xt="n1t", dbs="db", crow="condr",
    )
    scratch = {k: vm(*outs[v]) for k, v in local.items()}
    items = 9
    scratch.update(
        sendbuf=vm((tokens, features), bf16), recvs=vm((2, tokens, features), bf16), acc=vm((tokens, features), f32),
        cond_slots=vm((ts, every, per), f32), part=vm((every, 8, 256), f32),
        msg=vm((fs * cs * ts, 8, 256), f32), parts=vm((ts, fs * cs * 32, 128), bf16),
        x_send=dma((2 * ts,)), x_recv=dma((2 * ts,)), g_send=dma((2 * ts,)), g_recv=dma((2 * ts,)), loc=dma((3,)),
        sib_send=dma((2,)), sib_recv=dma((2,)), gsib_send=dma((2,)), gsib_recv=dma((2,)),
        c_send=dma((ts,)), c_recv=dma((ts,)), m_send=dma((fs * cs * ts,)), m_recv=dma((fs * cs * ts,)),
        core_send=dma((items, 2)), core_recv=dma((items, 2)), core_loc=dma((items, 2)),
        z_send=dma((2, items, ts)), z_recv=dma((2, items, ts)), zd_send=dma((2, ts)), zd_recv=dma((2, ts)),
        dy_send=dma((ts, fs)), dy_recv=dma((ts, fs)), dx_send=dma((ts, fs)), dx_recv=dma((ts, fs)),
        wot=vm((per, 256), bf16), wdt=vm((per, ts * 256), bf16),
        xs_send=dma((items, fs)), xs_recv=dma((items, fs)), ys_send=dma((items,)), ys_recv=dma((items,)),
        fx_send=dma((items, fs)), fx_recv=dma((items, fs)), fy_send=dma((items, fs)), fy_recv=dma((items, fs)),
        e_send=dma((2, 2)), e_recv=dma((2, 2)), out_sem=dma((len(outs) + ts,)),
    )
    anywhere, on_chip = pl.BlockSpec(memory_space=pl.ANY), pl.BlockSpec(memory_space=vm)
    results = pl.pallas_call(
        functools.partial(
            forward_kernel, fs, cs, ts, sent, padded, per, FORWARD_IN + FORWARD_OUT + tuple(scratch)
        ),
        name="forward",
        out_shape=tuple(sds(*outs[k]) for k in FORWARD_OUT),
        in_specs=[anywhere] * 6 + [on_chip] * 2 + [anywhere] + [on_chip] * 4,
        out_specs=(anywhere,) * len(FORWARD_OUT),
        scratch_shapes=list(scratch.values()),
        compiler_params=pltpu.CompilerParams(
            collective_id=0, has_side_effects=True, vmem_limit_bytes=62 << 20
        ),
    )(*[args[k] for k in FORWARD_IN])
    return bundle(FORWARD_OUT, results)


def attend_back(z, r, query_gain, key_gain):
    tokens = r.vs.shape[1]
    qt = 256
    r.dka[...] = jnp.zeros_like(r.dka)
    r.dva[...] = jnp.zeros_like(r.dva)
    k_t = r.khs[z].T

    def tile(n, carry):
        span = pl.ds(pl.multiple_of(n * qt, qt), qt)
        allowed = r.idk[...] <= r.idq[:, span]
        outs = []
        for h in range(2):
            lanes = slice(h * HD, (h + 1) * HD)
            qh, da = r.qhs[z, span, lanes] * 0.125, r.das[z, span, lanes]
            s = jnp.where(allowed, nt(r.khs[z, :, lanes], qh), masked_score)
            p = jnp.exp(s - r.lses[z, h : h + 1, span])
            dp = nt(r.vs[z, :, lanes], da)
            centre = jnp.sum(p * dp, axis=0, keepdims=True)
            ds = (p * (dp - centre)).astype(bf16)
            r.dva[h] += nn(p.astype(bf16), da)
            r.dka[h] += nn(ds, qh)
            outs.append(nn(k_t[h * HD : (h + 1) * HD, :], ds))
        r.dqa[span, :] = jnp.concatenate(outs, axis=0).T * 0.125
        return carry

    lax.fori_loop(0, tokens // qt, tile, 0)

    def finish(n, sums):
        span = pl.ds(pl.multiple_of(n * qt, qt), qt)
        dk = jnp.concatenate([r.dka[0, span, :], r.dka[1, span, :]], axis=1)
        dv = jnp.concatenate([r.dva[0, span, :], r.dva[1, span, :]], axis=1).astype(bf16)
        r.dqkv[z, span, 256:] = dv
        results = [None, None, None, jnp.sum(dv.astype(f32), axis=0, keepdims=True)]
        for i, (raw_ref, gain, delta) in enumerate(((r.qp, query_gain, r.dqa[span, :]), (r.kp, key_gain, dk))):
            raw = raw_ref[z % 2, span, :]
            inverse = head_inverse(raw)
            results[i] = jnp.sum(delta * raw * inverse, axis=0, keepdims=True)
            t = delta * gain
            out = (inverse * t - raw * (inverse * inverse * inverse) * segment_mean(t * raw)).astype(bf16)
            r.dqkv[z, span, i * 128 : (i + 1) * 128] = out
            if i == 0:
                results[2] = jnp.sum(out.astype(f32), axis=0, keepdims=True)
        return [a + b for a, b in zip(sums, results)]

    sums = lax.fori_loop(0, tokens // qt, finish, [jnp.zeros((1, 128), f32)] * 4)
    for row, value in enumerate((sums[2], sums[3], sums[0], sums[1])):
        r.vec[z, row : row + 1, :] = value


BACKWARD_IN = (
    "w1", "w2", "w3", "x", "g", "qpre", "kpre", "v", "qh", "kh", "att", "branch1",
    "middle", "n2t", "hpre", "hid", "bo", "lse", "top", "mod", "par", "gate2", "dd", "d3", "n1t", "db", "r1o",
    "idq", "idk", "wm",
)
BACKWARD_OUT = ("o1", "o2", "o3", "dxo", "boo", "maila", "mailb", "sdel")


def backward_kernel(fs, cs, ts, sent, padded, per, keys, *values):
    r = bundle(keys, values)
    at = Place(fs, cs, ts)
    width = 256
    tokens, features = r.gs.shape
    half = tokens // 2
    step = 64
    at.barrier()

    pending = {}
    order = []

    def load(name, src, dst):
        pltpu.make_async_copy(src, dst, r.in_sem.at[len(order)]).start()
        pending[name] = (src, dst, len(order))
        order.append(name)

    def need(*wanted):
        for name in wanted:
            src, dst, n = pending.pop(name)
            pltpu.make_async_copy(src, dst, r.in_sem.at[n]).wait()

    for z in range(ts):
        load("d3%d" % z, r.d3.at[z], r.d.at[z])
        load("r1%d" % z, r.r1o.at[z], r.r1.at[2 * ts + z])
    load("dd", r.dd, r.dds)
    load("w3", r.w3, r.wa)
    load("hp0", r.hpre.at[0], r.hp.at[0])
    load("n2t", r.n2t, r.xt)
    load("hp1", r.hpre.at[1], r.hp.at[1])
    load("w2", r.w2, r.wb)
    load("mod", r.mod, r.mods)
    load("g", r.g, r.gs)
    load("mid", r.middle, r.mid)
    load("b1", r.branch1, r.b1)
    load("att", r.att, r.atts)
    load("par", r.par.at[:, pl.ds(16, 8), :], r.psum)
    for name, src, dst in (
        ("qh", r.qh, r.qhs), ("kh", r.kh, r.khs), ("v", r.v, r.vs), ("lse", r.lse, r.lses),
        ("top", r.top, r.tops), ("gate2", r.gate2, r.gates),
        ("db", r.db, r.dbs),
    ):
        load(name, src, dst)

    def load_raw(z):
        load("qp%d" % z, r.qpre.at[z], r.qp.at[z % 2])
        load("kp%d" % z, r.kpre.at[z], r.kp.at[z % 2])

    load_raw(0)
    load_raw(1)

    def block_of(ref):
        def src(i):
            c = (i // ts) * 2 + at.k
            return ref.at[
                pl.ds(pl.multiple_of(c * padded, padded), sent),
                pl.ds(pl.multiple_of(lax.rem(i, ts) * width, width), width),
            ]

        return src

    bo_start, bo_wait = exchange_images(
        at, block_of(r.bo), lambda i: r.boo.at[i], r.bo_send, r.bo_recv, r.loc.at[1]
    )
    dx_start, dx_wait = exchange_images(
        at, block_of(r.dds), lambda i: r.dxo.at[i], r.dx_send, r.dx_recv, r.loc.at[0]
    )
    outs = (r.o1, r.o2, r.o3)

    def slot(g, z):
        return z + (ts if g == 1 else 0)

    def rows(f, hi):
        return pl.ds(pl.multiple_of((f * 2 + hi) * 2 * per, 2 * per), 2 * per)

    def far(s):
        return lax.rem(at.f + s, fs)

    def stage_one(g, z, s):
        n, d = g * ts + z, slot(g, z)
        x_part, y_part = parts_of(z)
        return (
            rcopy(
                r.d.at[d, rows(far(s), 1 - at.hi), y_part], r.r1.at[n, s - 1, :, y_part],
                r.y1_send.at[n, s], r.y1_recv.at[n, s], at.ypeer(),
            ),
            rcopy(
                r.d.at[d, rows(far(s), 1 - at.hi), x_part], r.r1.at[n, s - 1, :, x_part],
                r.x1_send.at[n, s], r.x1_recv.at[n, s], at.xpeer(s),
            ),
        )

    def stage_two(g, z):
        n, d = g * ts + z, slot(g, z)
        copies = [
            rcopy(
                r.d.at[d, rows(far(s), at.hi), :], r.rx2.at[n, s - 1],
                r.x2_send.at[n, s], r.x2_recv.at[n, s], at.xpeer(s),
            )
            for s in range(1, fs)
        ]
        copies.append(
            rcopy(r.d.at[d, rows(at.f, 1 - at.hi), :], r.ry2.at[n], r.y2_send.at[n], r.y2_recv.at[n], at.ypeer())
        )
        return copies

    def rs_a(g, z):
        for s in range(1, fs):
            for copy in stage_one(g, z, s):
                copy.start()

    def rs_b(g, z):
        n, d = g * ts + z, slot(g, z)
        x_part, y_part = parts_of(z)
        for s in range(1, fs) if g < 2 else ():
            for copy in stage_one(g, z, s):
                copy.wait()
        for s in range(1, fs):
            span = rows(far(s), at.hi)
            r.d[d, span, y_part] = (r.d[d, span, y_part].astype(f32) + r.r1[n, s - 1, :, y_part].astype(f32)).astype(bf16)
        span = rows(at.f, 1 - at.hi)
        value = r.d[d, span, x_part].astype(f32)
        for s in range(1, fs):
            value = value + r.r1[n, s - 1, :, x_part].astype(f32)
        r.d[d, span, x_part] = value.astype(bf16)
        for copy in stage_two(g, z):
            copy.start()

    def to_owner(g, z):
        s = lax.rem(at.t + ts - z, ts)
        index = jnp.maximum(s, 1)
        return rcopy(
            r.ry2.at[g * ts + z], r.rz.at[g, index - 1],
            r.z_send.at[g * ts + z], r.z_recv.at[g, index], (at.f, at.c, z),
        )

    def rs_c(g, z):
        n, d = g * ts + z, slot(g, z)
        for copy in stage_two(g, z):
            copy.wait()
        span = rows(at.f, at.hi)
        for part in (slice(0, GC // 2), slice(GC // 2, GC)):
            value = r.d[d, span, part].astype(f32) + r.ry2[n, :, part].astype(f32)
            for s in range(1, fs):
                value = value + r.rx2[n, s - 1, :, part].astype(f32)
            r.ry2[n, :, part] = value.astype(bf16)

        @pl.when(at.t != z)
        def _():
            to_owner(g, z).start()

    def pair_sum(g):
        src = r.total.at[pl.ds(pl.multiple_of((1 - at.k) * per, per), per)]
        own = r.total.at[pl.ds(pl.multiple_of(at.k * per, per), per)]
        keep = pltpu.make_async_copy(own, outs[g].at[at.k], r.k_loc.at[g])
        out = functools.partial(rcopy, src, outs[g].at[at.k], r.k_send.at[g], r.k_recv.at[g], at.sibling())
        inn = functools.partial(rcopy, src, outs[g].at[1 - at.k], r.k_send.at[g], r.k_recv.at[g], at.sibling())
        return keep, out, inn

    def pair_wait(g):
        keep, _, inn = pair_sum(g)
        keep.wait()
        inn().wait()

    def rs_e(g):
        for z in range(ts):

            @pl.when(at.t != z)
            def _():
                to_owner(g, z).wait_send()

        for s in range(1, ts):
            rcopy(
                r.rz.at[g, s - 1], r.rz.at[g, s - 1], r.z_send.at[g * ts], r.z_recv.at[g, s], at.zpeer(s)
            ).wait_recv()
        for part in (slice(0, GC // 2), slice(GC // 2, GC)):
            value = r.ry2[g * ts + at.t, :, part].astype(f32)
            for s in range(1, ts):
                value = value + r.rz[g, s - 1, :, part].astype(f32)
            r.total[:, part] = value
        keep, out, _ = pair_sum(g)
        keep.start()
        out().start()

    def mod(j):
        return r.mods[j : j + 1, :]

    def own_row(z, start):
        return r.psum[z, pl.ds(start + at.k, 1), :]

    def transpose(src):
        def tile(n, carry):
            span = pl.ds(pl.multiple_of(n * 128, 128), 128)
            r.xt[:, span] = src[span, :].T
            return carry

        lax.fori_loop(0, tokens // 128, tile, 0)

    def grad_into(d, cols, right):
        def tile(m, carry):
            span = pl.ds(pl.multiple_of(m * 256, 256), 256)
            r.d[d, span, cols] = nn(r.xt[span, :], right()).astype(bf16)
            return carry

        lax.fori_loop(0, features // 256, tile, 0)

    def eight(values):
        return jnp.sum(values.reshape(values.shape[0] // 8, 8, values.shape[1]), axis=0)

    def collapse(values):
        return jnp.sum(values, axis=0, keepdims=True)

    def pair(e, n):
        span = pl.ds(n * half, half)
        return rcopy(
            r.sendbuf.at[span, :], r.recvs.at[e, span, :], r.e_send.at[e, n], r.e_recv.at[e, n], at.sibling()
        )

    zeros = jnp.zeros((8, features), f32)

    def back_up(z):
        need("hp%d" % z)

        def tile(n, carry):
            span = pl.ds(pl.multiple_of(n * half, half), half)
            hidden_delta = nn(r.dds[span, :], r.wa[z])
            pre = r.hp[z % 2, span, :]
            inner = jnp.tanh(gelu_a * (pre + gelu_b * pre * pre * pre))
            slope = 0.5 * (1.0 + inner) + 0.5 * pre * (1.0 - inner * inner) * (
                gelu_a * (1.0 + 3.0 * gelu_b * pre * pre)
            )
            delta = (hidden_delta * slope).astype(bf16)
            r.hs[z, span, :] = delta
            return carry + eight(delta.astype(f32))

        r.ubs[z] = collapse(lax.fori_loop(0, 2, tile, jnp.zeros((8, GC), f32)))
        if z + 2 < ts:
            load("hp%d" % (z + 2), r.hpre.at[z + 2], r.hp.at[z % 2])

    def grad_up(z):
        grad_into(slot(1, z), slice(None), lambda: r.hs[z])

    need("d30", "d31", "r10", "r11")
    rs_b(2, 0)
    rs_b(2, 1)
    bo_start()
    need("dd", "w3", "n2t", "d32", "d33", "r12", "r13")
    back_up(0)
    grad_up(0)
    rs_a(1, 0)
    back_up(1)
    rs_c(2, 0)
    rs_b(2, 2)
    grad_up(1)
    back_up(2)
    rs_c(2, 1)
    rs_b(2, 3)
    grad_up(2)
    rs_a(1, 1)
    back_up(3)
    load("w1", r.w1, r.wa)
    grad_up(3)
    rs_b(1, 0)
    rs_a(1, 2)
    need("w2")
    for n in range(2):
        span = slice(n * half, (n + 1) * half)
        for m in range(2):
            cols = slice(m * 512, (m + 1) * 512)
            acc = nt(r.hs[0, span, :], r.wb[0, cols, :])
            for z in range(1, ts):
                acc = acc + nt(r.hs[z, span, :], r.wb[z, cols, :])
            r.sendbuf[span, cols] = acc.astype(bf16)
        pair(0, n).start()
    rs_c(2, 2)
    need("mid", "b1", "mod", "g")

    def norm_two(n):
        def tile(i, sums):
            span = pl.ds(pl.multiple_of(n * half + i * step, step), step)
            incoming = r.sendbuf[span, :].astype(f32) + r.recvs[0, span, :].astype(f32)
            normal, inverse = normalize(r.mid[span, :].astype(f32))
            e = incoming * (1.0 + mod(4))
            mean_e = jnp.mean(e, axis=-1, keepdims=True)
            mean_en = jnp.mean(e * normal, axis=-1, keepdims=True)
            delta = r.gs[span, :].astype(f32) + (e - mean_e - normal * mean_en) * inverse
            r.hp[0, span, :] = delta[:, :512]
            r.hp[1, span, :] = delta[:, 512:]
            low = (delta * mod(2)).astype(bf16)
            r.dds[span, :] = low
            parts = (incoming, incoming * normal, delta * r.b1[span, :].astype(f32), low.astype(f32))
            return [a + eight(b) for a, b in zip(sums, parts)]

        return tile

    sums = [zeros] * 4
    for n in range(2):
        pair(0, n).wait()
        sums = lax.fori_loop(0, half // step, norm_two(n), sums)
    shift_two, scale_two, gate_one, output_bias = (collapse(v) for v in sums)
    load("x", r.x, r.gs)
    rs_b(1, 1)
    rs_c(2, 3)
    rs_a(1, 3)

    transpose(r.dds)
    need("att", "w1")
    for z in range(ts):
        if z == 2:
            rs_c(1, 0)
        grad_into(slot(0, z), slice(384, GC), lambda: r.atts[z])

        def tile(n, carry):
            span = pl.ds(pl.multiple_of(n * half, half), half)
            r.das[z, span, :] = nn(r.dds[span, :], r.wa[z, :, 384:]).astype(bf16)
            return carry

        lax.fori_loop(0, 2, tile, 0)
    load("n1t", r.n1t, r.xt)
    rs_b(1, 2)
    need("par", "qh", "kh", "v", "lse", "top", "gate2", "db")
    for z in range(ts):
        need("qp%d" % z, "kp%d" % z)
        attend_back(z, r, own_row(z, 0), own_row(z, 2))
        if z + 2 < ts:
            load_raw(z + 2)
        if z == 0:
            need("n1t")
        grad_into(slot(0, z), slice(0, 384), lambda: r.dqkv[z])
        rs_a(0, z)
        if z == 0:
            rs_c(1, 1)
            rs_b(1, 3)
        if z == 1:
            rs_c(1, 2)
            rs_b(0, 0)
        if z == 2:
            rs_c(1, 3)
            rs_b(0, 1)
        if z == 3:
            rs_c(0, 0)
            rs_b(0, 2)

    gate_two, down_bias = collapse(r.gates[...]), collapse(r.dbs[...])
    firsts = ((gate_one, shift_two, scale_two), (gate_two, output_bias, down_bias))
    for z in range(ts):
        lanes = slice(z * width, (z + 1) * width)
        for row in range(3):
            r.early[z, row : row + 1, :] = jnp.where(at.k == 0, firsts[0][row][:, lanes], firsts[1][row][:, lanes])
        for row in range(2):
            r.early[z, 3 + row : 4 + row, :128] = r.vec[z, 2 * row : 2 * row + 1, :]
            r.early[z, 3 + row : 4 + row, 128:] = r.vec[z, 2 * row + 1 : 2 * row + 2, :]
            r.early[z, 5 + row : 6 + row, :] = r.ubs[z, :, row * width : (row + 1) * width]
            r.early[z, 7:8, row * 128 : (row + 1) * 128] = r.tops[z, row : row + 1, :]

    def mail_slot(box):
        def slot_of(n):
            f, c, t = at.coords(n)
            return box.at[(f * 2 + c // 2) * ts + t, lax.rem(c, 2)]

        return slot_of

    def toward(box):
        return lambda n: box.at[lax.rem(n, ts)]

    m_start, m_wait = broadcast_messages(
        at, toward(r.early), mail_slot(r.mail_a), r.m_send, r.m_recv, r.loc.at[2]
    )
    l_start, l_wait = broadcast_messages(
        at, toward(r.late), mail_slot(r.mail_b), r.l_send, r.l_recv, r.loc.at[3]
    )
    m_start()
    for n in range(2):
        span = slice(n * half, (n + 1) * half)
        for m in range(2):
            cols = slice(m * 512, (m + 1) * 512)
            acc = nt(r.dqkv[0, span, :], r.wa[0, cols, :384])
            for z in range(1, ts):
                acc = acc + nt(r.dqkv[z, span, :], r.wa[z, cols, :384])
            r.sendbuf[span, cols] = acc.astype(bf16)
        pair(1, n).start()
    need("x")

    def norm_one(n):
        def tile(i, sums):
            span = pl.ds(pl.multiple_of(n * half + i * step, step), step)
            incoming = r.sendbuf[span, :].astype(f32) + r.recvs[1, span, :].astype(f32)
            normal, inverse = normalize(r.gs[span, :].astype(f32))
            e = incoming * (1.0 + mod(1))
            mean_e = jnp.mean(e, axis=-1, keepdims=True)
            mean_en = jnp.mean(e * normal, axis=-1, keepdims=True)
            middle_delta = jnp.concatenate([r.hp[0, span, :], r.hp[1, span, :]], axis=1)
            r.dds[span, :] = (middle_delta + (e - mean_e - normal * mean_en) * inverse).astype(bf16)
            return [a + eight(b) for a, b in zip(sums, (incoming, incoming * normal))]

        return tile

    sums = [zeros] * 2
    for n in range(2):
        pair(1, n).wait()
        sums = lax.fori_loop(0, half // step, norm_one(n), sums)
    shift_one, scale_one = (collapse(v) for v in sums)
    for z in range(ts):
        lanes = slice(z * width, (z + 1) * width)
        r.late[z] = jnp.where(at.k == 0, shift_one[:, lanes], scale_one[:, lanes])
    l_start()
    dx_start()
    rs_b(0, 3)
    rs_c(0, 1)
    rs_e(2)
    rs_c(0, 2)
    pair_wait(2)
    rs_e(1)
    rs_c(0, 3)
    m_wait()

    l_wait()
    partial = jnp.zeros(r.silu.shape, f32)
    six = [(r.mail_b, 0, 0), (r.mail_b, 1, 0), (r.mail_a, 0, 0), (r.mail_a, 0, 1), (r.mail_a, 0, 2), (r.mail_a, 1, 0)]
    for j, (box, side, row) in enumerate(six):
        value = box[:, side, row, :]
        for _ in range(3):
            low = value.astype(bf16)
            partial = partial + nt(low, r.wm[j])
            value = value - low.astype(f32)
    r.silu[...] = partial
    r.silus[at.t] = partial

    def silu_copy(s, index):
        return rcopy(r.silu, r.silus.at[index], r.s_send.at[s], r.s_recv.at[s], at.zpeer(s))

    for s in range(1, ts):
        silu_copy(s, at.t).start()
    stores = [(r.mail_a, r.maila, 0), (r.mail_b, r.mailb, 1), (r.silu, r.sdel, 2)]
    for src, dst, n in stores[:2]:
        pltpu.make_async_copy(src, dst, r.out_sem.at[n]).start()
    bo_wait()
    pair_wait(1)
    for s in range(1, ts):
        silu_copy(s, at.zfrom(s)).wait()
    total = r.silus[0]
    for z in range(1, ts):
        total = total + r.silus[z]
    r.silu[...] = total
    pltpu.make_async_copy(r.silu, r.sdel, r.out_sem.at[2]).start()
    rs_e(0)
    dx_wait()
    for src, dst, n in stores:
        pltpu.make_async_copy(src, dst, r.out_sem.at[n]).wait()
    pair_wait(0)


def run_backward(fs, cs, ts, sent, padded, per, every, args):
    tokens, features = cs * padded, ts * 256
    f1 = max(fs - 1, 1)
    chunks = 3 * ts
    vm, dma, sds = pltpu.VMEM, pltpu.SemaphoreType.DMA, jax.ShapeDtypeStruct
    rows, cube = (tokens, features), (ts, tokens, 128)
    scratch = dict(
        gs=vm(rows, bf16), hs=vm((ts, tokens, GC), bf16), hp=vm((2, tokens, GC), f32),
        wa=vm((ts, features, GC), bf16), wb=vm((ts, features, GC), bf16),
        mid=vm(rows, bf16), dbs=vm((8, features), f32), b1=vm(rows, bf16), atts=vm(cube, bf16),
        qhs=vm(cube, bf16), khs=vm(cube, bf16), vs=vm(cube, bf16), lses=vm((ts, 2, tokens), f32),
        qp=vm((2, tokens, 128), f32), kp=vm((2, tokens, 128), f32), tops=vm((ts, 2, 128), f32), gates=vm((8, features), f32),
        mods=vm((8, features), f32), psum=vm((ts, 8, 128), f32),
        dds=vm(rows, bf16), xt=vm((features, tokens), bf16), sendbuf=vm(rows, bf16), recvs=vm((2, *rows), bf16),
        das=vm(cube, bf16), dqkv=vm((ts, tokens, 384), bf16), vec=vm((ts, 4, 128), f32), ubs=vm((ts, 1, GC), f32),
        dqa=vm((tokens, 128), f32), dka=vm((2, tokens, HD), f32), dva=vm((2, tokens, HD), f32),
        early=vm((ts, 8, 256), f32), late=vm((ts, 1, 256), f32),
        mail_a=vm((every, 2, 8, 256), f32), mail_b=vm((every, 2, 1, 256), f32),
        silu=vm((every, per), f32), silus=vm((ts, every, per), f32),
        d=vm((2 * ts, features, GC), bf16),
        r1=vm((chunks, f1, 2 * per, GC), bf16),
        rx2=vm((chunks, f1, 2 * per, GC), bf16), ry2=vm((chunks, 2 * per, GC), bf16),
        rz=vm((3, ts - 1, 2 * per, GC), bf16), total=vm((2 * per, GC), f32),
        in_sem=dma((48,)), loc=dma((4,)), out_sem=dma((3,)),
        l_send=dma((fs * cs * ts,)), l_recv=dma((fs * cs * ts,)), s_send=dma((ts,)), s_recv=dma((ts,)),
        bo_send=dma((2 * ts,)), bo_recv=dma((2 * ts,)), dx_send=dma((2 * ts,)), dx_recv=dma((2 * ts,)),
        y1_send=dma((chunks, fs)), y1_recv=dma((chunks, fs)), x1_send=dma((chunks, fs)), x1_recv=dma((chunks, fs)),
        x2_send=dma((chunks, fs)), x2_recv=dma((chunks, fs)), y2_send=dma((chunks,)), y2_recv=dma((chunks,)),
        z_send=dma((chunks,)), z_recv=dma((3, ts)), k_send=dma((3,)), k_recv=dma((3,)), k_loc=dma((3,)),
        e_send=dma((2, 2)), e_recv=dma((2, 2)), m_send=dma((fs * cs * ts,)), m_recv=dma((fs * cs * ts,)),
    )
    anywhere, on_chip = pl.BlockSpec(memory_space=pl.ANY), pl.BlockSpec(memory_space=vm)
    share = sds((2, per, GC), f32)
    blocks = sds((2 * ts, sent, 256), bf16)
    results = pl.pallas_call(
        functools.partial(
            backward_kernel, fs, cs, ts, sent, padded, per, BACKWARD_IN + BACKWARD_OUT + tuple(scratch)
        ),
        name="backward",
        out_shape=(
            share, share, share, blocks, blocks, sds((every, 2, 8, 256), f32), sds((every, 2, 1, 256), f32),
            sds((every, per), f32),
        ),
        in_specs=[anywhere] * (len(BACKWARD_IN) - 3) + [on_chip] * 3,
        out_specs=(anywhere,) * 8,
        scratch_shapes=list(scratch.values()),
        compiler_params=pltpu.CompilerParams(
            collective_id=1, has_side_effects=True, vmem_limit_bytes=63 << 20
        ),
    )(*[args[k] for k in BACKWARD_IN])
    return bundle(BACKWARD_OUT, results)


FINISH_IN = (
    "one", "two", "three", "bo", "dx", "moda", "modb", "cond", "wq", "wk", "columns",
)
FINISH_OUT = ("block", "dinputs", "dq", "dk", "dv", "dout", "dup", "ddown", "dmod", "cq", "ck")
FINISH_SCRATCH = ("ones", "twos", "threes", "bos", "dxs", "wide", "sem")


def finish_kernel(*values):
    r = bundle(FINISH_IN + FINISH_OUT + FINISH_SCRATCH, values)
    pairs = ((r.bo, r.bos), (r.dx, r.dxs), (r.one, r.ones), (r.two, r.twos), (r.three, r.threes))
    copies = [pltpu.make_async_copy(src, dst, r.sem.at[n]) for n, (src, dst) in enumerate(pairs)]
    for copy in copies:
        copy.start()
    rows, images, _ = r.block.shape
    cond = r.cond[...]
    silu = (cond / (1.0 + jnp.exp(-cond))).astype(bf16).astype(f32)
    left = silu.T.astype(bf16)
    six = [(r.modb, 0, 0), (r.modb, 1, 0), (r.moda, 0, 0), (r.moda, 0, 1), (r.moda, 0, 2), (r.moda, 1, 0)]
    for j, (box, side, row) in enumerate(six):
        value = box[:, side, row, :]
        total = jnp.zeros((left.shape[0], value.shape[1]), f32)
        for _ in range(3):
            low = value.astype(bf16)
            total = total + nn(left, low)
            value = value - low.astype(f32)
        r.dmod[j] = total
    r.cq[...] = r.wq[...].astype(f32) * r.columns[...]
    r.ck[...] = r.wk[...].astype(f32) * r.columns[...]
    copies[0].wait()
    for i in range(images):
        r.wide[:, i, :] = r.bos[i, :rows, :].astype(f32)
    r.block[...] = r.wide[...].astype(bf16)
    copies[1].wait()
    for i in range(images):
        r.dinputs[:, i, :] = r.dxs[i, :rows, :].astype(f32)
    for copy in copies[2:]:
        copy.wait()
    for h in range(2):
        here = slice(h * 128, (h + 1) * 128)
        r.dq[:, here] = r.ones[h, :, :128]
        r.dk[:, here] = r.ones[h, :, 128:256]
        r.dv[:, here] = r.ones[h, :, 256:384]
        r.dout[here, :] = r.ones[h, :, 384:].T
        half = slice(h * GC, (h + 1) * GC)
        r.dup[:, half] = r.twos[h]
        r.ddown[half, :] = r.threes[h].T


def on_device(
    fs, cs, ts,
    inputs, cotangent, labels, scale_ids, head_flags, class_table, modulate_weight, modulate_bias,
    query_weight, key_weight, value_weight, query_bias, value_bias, query_gain, key_gain,
    output_weight, output_bias, up_weight, up_bias, down_weight, down_bias,
):
    images, rows_here, width = inputs.shape
    if images != 2 * ts or cs != 4 or ts % 2 or width != 256:
        raise ValueError("unsupported mesh")
    length = scale_ids.shape[0]
    every = labels.shape[0]
    count = fs * cs * ts
    sent = -(-rows_here // 16) * 16
    padded = -(-rows_here // 64) * 64
    tokens = cs * padded
    features = ts * width
    per = query_weight.shape[0]
    part_cols = class_table.shape[1]
    f, c, t = (lax.axis_index(n) for n in ("fsdp", "ctx", "tp"))
    core = lax.rem(c, 2)
    block = f * cs + c

    classes = class_table.shape[0]
    onehot = (labels[:, None] == jnp.arange(classes, dtype=jnp.int32)[None, :]).astype(bf16)
    cond_part = jnp.dot(onehot, class_table, preferred_element_type=f32)
    cond_spread = lax.dynamic_update_slice(
        jnp.zeros((every, per), f32), cond_part, (0, t * part_cols)
    )
    fit = ((0, 0), (0, sent - rows_here), (0, 0))

    lanes = modulate_bias.shape[2]
    small_rows = jnp.concatenate(
        [
            modulate_bias.reshape(-1, lanes), query_bias, value_bias, query_gain, key_gain,
            output_bias, down_bias, up_bias,
        ],
        axis=0,
    )
    small = lax.dynamic_update_slice(
        jnp.zeros((small_rows.shape[0], HD), bf16), small_rows, (0, block * lanes)
    ).reshape(-1, 2 * HD)
    ids = scale_ids.reshape(cs, rows_here)
    spare = ((0, 0), (0, padded - rows_here))
    ids_query = jnp.pad(ids, spare, constant_values=-1).reshape(1, tokens)
    ids_key = jnp.pad(ids, spare, constant_values=1 << 20).reshape(tokens, 1)
    flat_modulate = modulate_weight.transpose(1, 0, 2)
    k = run_forward(
        fs, cs, ts, sent, padded, per, every,
        dict(
            xb=jnp.pad(inputs, fit), gb=jnp.pad(cotangent, fit),
            wq=query_weight, wk=key_weight, wv=value_weight, wu=up_weight, wo=output_weight, wd=down_weight,
            sp=small, cond=cond_spread,
            wm=flat_modulate, idq=ids_query, idk=ids_key,
        ),
    )
    m = run_backward(
        fs, cs, ts, sent, padded, per, every,
        {
            key: {"idq": ids_query, "idk": ids_key, "wm": flat_modulate}.get(key, getattr(k, key, None))
            for key in BACKWARD_IN
        },
    )
    heads = modulate_bias.shape[1]
    sum_one, sum_two, sum_three, dx_blocks, bo_blocks = m.o1, m.o2, m.o3, m.dxo, m.boo

    sums = jnp.sum(m.maila, axis=0)
    same = jnp.concatenate([jnp.sum(m.mailb, axis=0).reshape(2, width), sums[0, :3], sums[1, :3]])
    halves_sum = sums[:, 3:7]

    def mine(values):
        return lax.dynamic_slice_in_dim(values, block * lanes, lanes, values.ndim - 1)

    same = mine(same.reshape(8, heads, HD))
    modulate_bias_grad, output_bias_grad, down_bias_grad = same[:6], same[6], same[7]
    quarter = mine(halves_sum[:, :2].reshape(2, 4, heads // 2, HD)).transpose(1, 0, 2, 3).reshape(4, heads, lanes)
    query_bias_grad, value_bias_grad, query_gain_grad, key_gain_grad = (quarter[j] for j in range(4))
    up_bias_grad = mine(halves_sum[:, 2:].reshape(-1, HD))
    head_max = jnp.max(m.maila[:, :, 7], axis=0).reshape(heads, 128)[:, 0]

    silu_cols = lax.dynamic_slice_in_dim(m.sdel, t * part_cols, part_cols, 1)
    primal, silu_back = jax.vjp(jax.nn.silu, cond_part)
    cond_delta = silu_back(silu_cols)[0]
    class_table_grad = jnp.dot(onehot.astype(f32).T, cond_delta, precision=precise)

    factor = jnp.where(
        head_flags == 1,
        jnp.sqrt(clip_threshold / jnp.maximum(head_max, clip_threshold)),
        jnp.ones_like(head_max),
    )
    columns = jnp.repeat(factor, HD)
    square, flat_rows = (per, width), (rows_here, images, width)
    share = pltpu.VMEM((2, per, GC), f32)
    sent_rows = pltpu.VMEM((images, sent, width), bf16)
    (
        block_out, inputs_grad, query_weight_grad, key_weight_grad, value_weight_grad, output_weight_grad,
        up_weight_grad, down_weight_grad, modulate_weight_grad, clipped_query, clipped_key,
    ) = pl.pallas_call(
        finish_kernel,
        name="finish",
        out_shape=(
            jax.ShapeDtypeStruct(flat_rows, bf16), jax.ShapeDtypeStruct(flat_rows, f32),
            jax.ShapeDtypeStruct(square, f32), jax.ShapeDtypeStruct(square, f32),
            jax.ShapeDtypeStruct(square, f32), jax.ShapeDtypeStruct((width, per), f32),
            jax.ShapeDtypeStruct(up_weight.shape, f32), jax.ShapeDtypeStruct(down_weight.shape, f32),
            jax.ShapeDtypeStruct((6, per, width), f32),
            jax.ShapeDtypeStruct(square, f32), jax.ShapeDtypeStruct(square, f32),
        ),
        in_specs=[pl.BlockSpec(memory_space=pl.ANY)] * 5 + [pl.BlockSpec(memory_space=pltpu.VMEM)] * 6,
        scratch_shapes=[
            share, share, share, sent_rows, sent_rows, pltpu.VMEM(flat_rows, f32), pltpu.SemaphoreType.DMA((5,)),
        ],
        compiler_params=pltpu.CompilerParams(vmem_limit_bytes=62 << 20),
    )(
        sum_one, sum_two, sum_three, bo_blocks, dx_blocks, m.maila, m.mailb, k.condr,
        query_weight, key_weight, columns[None, :],
    )
    block_out, inputs_grad = block_out.transpose(1, 0, 2), inputs_grad.transpose(1, 0, 2)
    modulate_weight_grad = modulate_weight_grad.transpose(1, 0, 2)
    clipped_query_bias = query_bias.astype(f32) * factor[:, None]
    return (
        block_out, inputs_grad, class_table_grad, modulate_weight_grad, modulate_bias_grad,
        query_weight_grad, key_weight_grad, value_weight_grad, query_bias_grad, value_bias_grad,
        query_gain_grad, key_gain_grad, output_weight_grad, output_bias_grad,
        up_weight_grad, up_bias_grad, down_weight_grad, down_bias_grad,
        clipped_query, clipped_key, clipped_query_bias,
    )


def solution(mesh):
    rows = P("fsdp", "ctx", "tp")
    table = P(None, ("fsdp", "ctx", "tp"))
    left = P(("fsdp", "ctx"), "tp")
    right = P("tp", ("fsdp", "ctx"))
    modulate = P(("fsdp", "ctx"), None, "tp")
    modulate_small = P(None, "tp", ("fsdp", "ctx"))
    return jax.shard_map(
        functools.partial(on_device, mesh.shape["fsdp"], mesh.shape["ctx"], mesh.shape["tp"]),
        mesh=mesh,
        in_specs=(
            rows, rows, P(), P(), P("tp"), table, modulate, modulate_small,
            left, left, left, right, right, right, right,
            right, right, left, right, right, right,
        ),
        out_specs=(
            rows, rows, table, modulate, modulate_small,
            left, left, left, right, right, right, right,
            right, right, left, right, right, right,
            left, left, right,
        ),
        check_vma=False,
    )
```

```python
import functools
import math

import jax
import jax.numpy as jnp
from jax import lax
from jax.experimental import pallas as pl
from jax.experimental.pallas import tpu as pltpu
from jax.sharding import PartitionSpec as P

HD = 64
GC = 512
CHUNK = 256
MESH = pl.DeviceIdType.MESH
precise = lax.Precision.HIGHEST
norm_epsilon = 1e-06
clip_threshold = 2.0
masked_score = -1e30
f32, bf16 = jnp.float32, jnp.bfloat16


def product(left, right, form):
    return jnp.einsum(form, left, right, preferred_element_type=f32)


def rcopy(src, dst, send_sem, recv_sem, device):
    return pltpu.make_async_remote_copy(
        src_ref=src,
        dst_ref=dst,
        send_sem=send_sem,
        recv_sem=recv_sem,
        device_id=device,
        device_id_type=MESH,
    )


class Place:
    def __init__(self, fs, cs, ts):
        self.fs, self.cs, self.ts = fs, cs, ts
        self.count = fs * cs * ts
        self.f, self.c, self.t = (lax.axis_index(n) for n in ("fsdp", "ctx", "tp"))
        self.hi, self.k = self.c // 2, lax.rem(self.c, 2)
        self.me = (self.f * cs + self.c) * ts + self.t
        self.slot = self.hi * ts + self.t

    def coords(self, n):
        return (n // (self.cs * self.ts), lax.rem(n // self.ts, self.cs), lax.rem(n, self.ts))

    def sibling(self):
        return (self.f, self.hi * 2 + 1 - self.k, self.t)

    def ypeer(self):
        return (self.f, (1 - self.hi) * 2 + self.k, self.t)

    def xpeer(self, s):
        return (lax.rem(self.f + s, self.fs), self.c, self.t)

    def xfrom(self, s):
        return lax.rem(self.f + self.fs - s, self.fs)

    def zpeer(self, s):
        return (self.f, self.c, lax.rem(self.t + s, self.ts))

    def zto(self, s):
        return lax.rem(self.t + s, self.ts)

    def zfrom(self, s):
        return lax.rem(self.t + self.ts - s, self.ts)

    def barrier(self):
        sem = pltpu.get_barrier_semaphore()

        def greet(n, carry):
            @pl.when(n != self.me)
            def _():
                pl.semaphore_signal(sem, inc=1, device_id=self.coords(n), device_id_type=MESH)

            return carry

        lax.fori_loop(0, self.count, greet, 0)
        pl.semaphore_wait(sem, self.count - 1)


def exchange_images(at, src_of, dst_of, send_sems, recv_sems, local_sem):
    slots = 2 * at.ts

    def start():
        for i in range(slots):
            hi, t = i // at.ts, i % at.ts

            @pl.when(i != at.slot)
            def _():
                rcopy(
                    src_of(i),
                    dst_of(at.slot),
                    send_sems.at[i],
                    recv_sems.at[at.slot],
                    (at.f, hi * 2 + at.k, t),
                ).start()

            @pl.when(i == at.slot)
            def _():
                pltpu.make_async_copy(src_of(i), dst_of(i), local_sem).start()

    def wait():
        for i in range(slots):
            @pl.when(i != at.slot)
            def _():
                rcopy(src_of(i), dst_of(i), send_sems.at[i], recv_sems.at[i], (at.f, at.c, at.t)).wait()

            @pl.when(i == at.slot)
            def _():
                pltpu.make_async_copy(src_of(i), dst_of(i), local_sem).wait()

    return start, wait


def broadcast_messages(at, src_of, slot_of, send_sems, recv_sems, local_sem):
    def start():
        def each(n, carry):
            @pl.when(n != at.me)
            def _():
                rcopy(src_of(n), slot_of(at.me), send_sems.at[n], recv_sems.at[at.me], at.coords(n)).start()

            @pl.when(n == at.me)
            def _():
                pltpu.make_async_copy(src_of(n), slot_of(n), local_sem).start()

            return carry

        lax.fori_loop(0, at.count, each, 0)

    def wait():
        def each(n, carry):
            @pl.when(n != at.me)
            def _():
                rcopy(src_of(n), slot_of(n), send_sems.at[n], recv_sems.at[n], at.coords(n)).wait()

            @pl.when(n == at.me)
            def _():
                pltpu.make_async_copy(src_of(n), slot_of(n), local_sem).wait()

            return carry

        lax.fori_loop(0, at.count, each, 0)

    return start, wait


FORWARD_IN = ("xb", "gb", "wq", "wk", "wv", "wu", "wo", "wd", "sp", "cond", "wm", "idq", "idk")
FORWARD_OUT = (
    "w1", "w2", "w3", "x", "g", "normed1", "qpre", "kpre", "v", "qh", "kh", "att", "branch1",
    "middle", "normed2", "hpre", "hid", "bo", "lse", "top", "mod", "par", "gate2",
    "dd", "d3", "n1t", "n2t", "db", "condr", "r1o",
)


def parts_of(z):
    cut = GC // 2 if z % 2 == 0 else GC // 4
    return slice(cut, GC), slice(0, cut)


class Refs:
    pass


def bundle(keys, values):
    refs = Refs()
    for key, value in zip(keys, values, strict=True):
        setattr(refs, key, value)
    return refs


def normalize(values):
    centered = values - jnp.mean(values, axis=-1, keepdims=True)
    inverse = lax.rsqrt(jnp.mean(centered * centered, axis=-1, keepdims=True) + norm_epsilon)
    return centered * inverse, inverse


def nt(left, right):
    return lax.dot_general(left, right, (((1,), (1,)), ((), ())), preferred_element_type=f32)


def nn(left, right):
    return lax.dot_general(left, right, (((1,), (0,)), ((), ())), preferred_element_type=f32)


def segment_mean(values):
    row = lax.broadcasted_iota(jnp.int32, (2 * HD, 2 * HD), 0) < HD
    col = lax.broadcasted_iota(jnp.int32, (2 * HD, 2 * HD), 1) < HD
    same = jnp.where(row == col, 1.0 / HD, 0.0).astype(bf16)
    high = values.astype(bf16)
    rest = values - high.astype(f32)
    middle = rest.astype(bf16)
    low = (rest - middle.astype(f32)).astype(bf16)
    return nn(high, same) + nn(middle, same) + nn(low, same)


def head_inverse(values):
    return lax.rsqrt(segment_mean(values * values) + norm_epsilon)


gelu_a = math.sqrt(2.0 / math.pi)
gelu_b = 0.044715


def forward_kernel(fs, cs, ts, sent, padded, per, keys, *values):
    r = bundle(keys, values)
    at = Place(fs, cs, ts)
    width = 256
    tokens, features = r.xs.shape
    half = tokens // 2
    quarter = features // ts
    zero = jnp.zeros((padded - sent, features), bf16)
    for c in range(cs):
        r.xs[c * padded + sent : (c + 1) * padded, :] = zero
        r.gs[c * padded + sent : (c + 1) * padded, :] = zero
    at.barrier()

    def block_at(out):
        def dst(i):
            c = (i // ts) * 2 + at.k
            return out.at[
                pl.ds(pl.multiple_of(c * padded, padded), sent),
                pl.ds(pl.multiple_of(lax.rem(i, ts) * width, width), width),
            ]

        return dst

    x_start, x_wait = exchange_images(at, lambda i: r.xb.at[i], block_at(r.xs), r.x_send, r.x_recv, r.loc.at[0])
    g_start, g_wait = exchange_images(at, lambda i: r.gb.at[i], block_at(r.gs), r.g_send, r.g_recv, r.loc.at[1])

    r.wot[...] = r.wo[...].T
    r.wdt[...] = r.wd[...].T
    pieces, items = [[(r.sp, None, None)]], [(r.parts, None, r.sp.shape[0])]
    for col, sources in ((0, (r.wq,)), (128, (r.wk,)), (256, (r.wv, r.wot))):
        pieces.append([(ref, 128, (0, 128, col + 128 * i)) for i, ref in enumerate(sources)])
        items.append((r.w1s, slice(col, col + 128 * len(sources)), per))
    for full, ref, widths in ((r.w2s, r.wu, (256, 256)), (r.w3s, r.wdt, (256, 128, 128))):
        col = 0
        for w in widths:
            pieces.append([(ref, w, (col, GC, col))])
            items.append((full, slice(col, col + w), per))
            col += w

    def slab(n, z, nz, f, hi, k=0, blocks=2):
        full, cols, size = items[n]
        row = pl.multiple_of(((f * 2 + hi) * 2 + k) * size, size)
        span = pl.ds(row, blocks * size)
        return full.at[pl.ds(z, nz), span, :] if cols is None else full.at[pl.ds(z, nz), span, cols]

    def core_pair(n):
        full, _, size = items[n]

        def place(z, k, cols):
            span = pl.ds(pl.multiple_of(((at.f * 2 + at.hi) * 2 + k) * size, size), size)
            return full.at[z, span, :] if cols is None else full.at[z, span, cols]

        copies = []
        for i, (ref, w, where) in enumerate(pieces[n]):
            if where is None:
                mine, theirs, cols = ref, ref, None
            else:
                start, stride, col = where
                mine, theirs = (
                    ref.at[:, pl.ds(pl.multiple_of(start + k * stride, 128), w)] for k in (at.k, 1 - at.k)
                )
                cols = slice(col, col + w)
            sems = (r.core_send.at[n, i], r.core_recv.at[n, i], at.sibling())
            copies.append(
                (
                    functools.partial(pltpu.make_async_copy, mine, place(at.t, at.k, cols), r.core_loc.at[n, i]),
                    functools.partial(rcopy, theirs, place(at.t, at.k, cols), *sems),
                    functools.partial(rcopy, theirs, place(at.t, 1 - at.k, cols), *sems),
                )
            )
        return copies

    def core_start(n):
        for keep, out, _ in core_pair(n):
            keep().start()
            out().start()

    def core_wait(n):
        for keep, _, inn in core_pair(n):
            keep().wait()
            inn().wait()

    def hop(n, d, up, action):
        block = at.t - d if up else at.t + d
        sends = ((block >= 0) & (at.t < ts - 1)) if up else ((block < ts) & (at.t > 0))

        @pl.when(sends)
        def _():
            src = slab(n, block, 1, at.f, at.hi)
            side = 0 if up else 1
            copy = rcopy(
                src, src, r.z_send.at[side, n, d], r.z_recv.at[side, n, d + 1],
                (at.f, at.c, at.t + 1 if up else at.t - 1),
            )
            copy.start() if action == "start" else copy.wait_send()

    def z_start(n):
        hop(n, 0, True, "start")
        hop(n, 0, False, "start")

    def z_step(n, d):
        for up in (True, False):
            block = at.t - d if up else at.t + d

            @pl.when((block >= 0) & (block < ts))
            def _():
                src = slab(n, block, 1, at.f, at.hi)
                side = 0 if up else 1
                rcopy(
                    src, src, r.z_send.at[side, n, d], r.z_recv.at[side, n, d], (at.f, at.c, at.t)
                ).wait_recv()

            if d < ts - 1:
                hop(n, d, up, "start")

    def z_wait(n):
        for d in range(1, ts):
            z_step(n, d)

    def direct_start(n):
        for s in range(1, ts):
            src = slab(n, at.t, 1, at.f, at.hi)
            rcopy(src, src, r.zd_send.at[n, s], r.zd_recv.at[n, s], at.zpeer(s)).start()

    def direct_wait(n):
        for s in range(1, ts):
            src = slab(n, at.zfrom(s), 1, at.f, at.hi)
            rcopy(src, src, r.zd_send.at[n, s], r.zd_recv.at[n, s], at.zpeer(s)).wait()

    def own(f, hi, k=0, n=2):
        return slab(last, at.t, 1, f, hi, k, n)

    def tail_own(action):
        src = own(at.f, at.hi)
        rcopy(src, src, r.ys_send.at[last], r.ys_recv.at[last], at.ypeer()).start()
        for s in range(1, fs):
            rcopy(src, src, r.xs_send.at[last, s], r.xs_recv.at[last, s], at.xpeer(s)).start()

    def tail_forward():
        src = own(at.f, 1 - at.hi)
        rcopy(src, src, r.ys_send.at[last], r.ys_recv.at[last], at.ypeer()).wait()
        for s in range(1, fs):
            src = own(at.xfrom(s), at.hi)
            rcopy(src, src, r.xs_send.at[last, s], r.xs_recv.at[last, s], at.xpeer(s)).wait()
        for s in range(1, fs):
            src = own(at.f, 1 - at.hi, 1, 1)
            rcopy(src, src, r.fx_send.at[last, s], r.fx_recv.at[last, s], at.xpeer(s)).start()
            src = own(at.xfrom(s), at.hi, 0, 1)
            rcopy(src, src, r.fy_send.at[last, s], r.fy_recv.at[last, s], at.ypeer()).start()

    def tail_arrived():
        for s in range(1, fs):
            src = own(at.xfrom(s), 1 - at.hi, 1, 1)
            rcopy(src, src, r.fx_send.at[last, s], r.fx_recv.at[last, s], at.xpeer(s)).wait()
            src = own(at.xfrom(s), 1 - at.hi, 0, 1)
            rcopy(src, src, r.fy_send.at[last, s], r.fy_recv.at[last, s], at.ypeer()).wait()

    def tail_block(z):
        full, cols, _ = items[last]
        return full.at[pl.ds(z, 1), :, cols]

    def tail_hop(d, up, action):
        block = at.t - d if up else at.t + d
        sends = ((block >= 0) & (at.t < ts - 1)) if up else ((block < ts) & (at.t > 0))

        @pl.when(sends)
        def _():
            src = tail_block(block)
            side = 0 if up else 1
            copy = rcopy(
                src, src, r.z_send.at[side, last, d], r.z_recv.at[side, last, d + 1],
                (at.f, at.c, at.t + 1 if up else at.t - 1),
            )
            copy.start() if action == "start" else copy.wait_send()

    def tail_step(d):
        for up in (True, False):
            block = at.t - d if up else at.t + d
            if d > 0:

                @pl.when((block >= 0) & (block < ts))
                def _():
                    src = tail_block(block)
                    side = 0 if up else 1
                    rcopy(
                        src, src, r.z_send.at[side, last, d], r.z_recv.at[side, last, d], (at.f, at.c, at.t)
                    ).wait_recv()

            if d < ts - 1:
                tail_hop(d, up, "start")

    def z_sent(n):
        for d in range(ts - 1):
            for up in (True, False):
                hop(n, d, up, "sent")

    def xy_start(n):
        src = slab(n, 0, ts, at.f, at.hi)
        rcopy(src, src, r.ys_send.at[n], r.ys_recv.at[n], at.ypeer()).start()
        for s in range(1, fs):
            rcopy(src, src, r.xs_send.at[n, s], r.xs_recv.at[n, s], at.xpeer(s)).start()

    def xy_wait(n):
        src = slab(n, 0, ts, at.f, 1 - at.hi)
        rcopy(src, src, r.ys_send.at[n], r.ys_recv.at[n], at.ypeer()).wait()
        for s in range(1, fs):
            src = slab(n, 0, ts, at.xfrom(s), at.hi)
            rcopy(src, src, r.xs_send.at[n, s], r.xs_recv.at[n, s], at.xpeer(s)).wait()

    def fwd_start(n):
        zh = ts // 2 - n % 2
        for s in range(1, fs):
            src = slab(n, zh, ts - zh, at.f, 1 - at.hi)
            rcopy(src, src, r.fx_send.at[n, s], r.fx_recv.at[n, s], at.xpeer(s)).start()
            src = slab(n, 0, zh, at.xfrom(s), at.hi)
            rcopy(src, src, r.fy_send.at[n, s], r.fy_recv.at[n, s], at.ypeer()).start()

    def fwd_wait(n):
        zh = ts // 2 - n % 2
        for s in range(1, fs):
            src = slab(n, zh, ts - zh, at.xfrom(s), 1 - at.hi)
            rcopy(src, src, r.fx_send.at[n, s], r.fx_recv.at[n, s], at.xpeer(s)).wait()
            src = slab(n, 0, zh, at.xfrom(s), 1 - at.hi)
            rcopy(src, src, r.fy_send.at[n, s], r.fy_recv.at[n, s], at.ypeer()).wait()

    last = len(items) - 1
    saved = []

    def save(src, out):
        copy = pltpu.make_async_copy(src, out, r.out_sem.at[len(saved)])
        copy.start()
        saved.append([src, out, True])
        return len(saved) - 1

    def settle(n):
        src, out, waiting = saved[n]
        if waiting:
            pltpu.make_async_copy(src, out, r.out_sem.at[n]).wait()
            saved[n][2] = False

    def transpose(src):
        def tile(n, carry):
            span = pl.ds(pl.multiple_of(n * 128, 128), 128)
            r.xt[:, span] = src[span, :].T
            return carry

        lax.fori_loop(0, tokens // 128, tile, 0)

    r.cond_slots[at.t] = r.cond[...]

    def cond_copy(s, slot):
        return rcopy(r.cond, r.cond_slots.at[slot], r.c_send.at[s], r.c_recv.at[s], at.zpeer(s))

    for s in range(1, ts):
        cond_copy(s, at.t).start()
    for n in (0, 1, last, 2, 3):
        core_start(n)
    core_wait(0)
    direct_start(0)
    core_wait(1)
    direct_start(1)
    core_wait(last)
    tail_own("start")
    for n in range(4, last):
        core_start(n)
    core_wait(2)
    z_start(2)
    direct_wait(0)
    xy_start(0)

    for s in range(1, ts):
        cond_copy(s, at.zfrom(s)).wait()
    cond = r.cond_slots[0]
    for z in range(1, ts):
        cond = cond + r.cond_slots[z]
    r.crow[...] = cond
    save(r.crow, r.condr)
    silu = (cond / (1.0 + jnp.exp(-cond))).astype(bf16)
    for j in range(6):
        r.part[:, j, :] = nn(silu, r.wm[j])

    def image_of(n):
        f, c, t = at.coords(n)
        return (f * 2 + c // 2) * ts + t

    m_start, m_wait = broadcast_messages(
        at, lambda n: r.part.at[image_of(n)], lambda n: r.msg.at[n], r.m_send, r.m_recv, r.loc.at[2]
    )
    xy_wait(0)
    fwd_start(0)
    tail_forward()
    direct_wait(1)
    xy_start(1)
    z_step(2, 1)
    core_wait(3)
    z_start(3)
    z_step(2, 2)
    z_step(2, 3)
    xy_start(2)
    xy_wait(1)
    fwd_start(1)
    z_step(3, 1)
    m_start()
    z_step(3, 2)
    xy_wait(2)
    fwd_start(2)
    z_step(3, 3)
    xy_start(3)
    x_start()
    for n in range(4, last):
        core_wait(n)
    fwd_wait(0)
    m_wait()
    z_start(4)

    blocks = fs * cs
    rows_small = r.sp.shape[0]

    def small_sum(n, carry):
        return carry + r.parts[:, pl.ds(pl.multiple_of(n * rows_small, rows_small), rows_small), :].astype(f32)

    r.psum[...] = lax.fori_loop(0, blocks, small_sum, jnp.zeros(r.psum.shape, f32))
    for z in range(ts):

        def mod_sum(n, carry):
            return carry + r.msg[n * ts + z]

        total = lax.fori_loop(0, blocks, mod_sum, jnp.zeros((8, width), f32))
        for j in range(6):
            for h in range(2):
                value = total[j : j + 1, h * 128 : (h + 1) * 128] + r.psum[z, 2 * j + h : 2 * j + h + 1, :]
                r.mods[j : j + 1, z * width + h * 128 : z * width + (h + 1) * 128] = value.astype(bf16).astype(f32)
                if j < 2:
                    row = r.psum[z, 20 + 2 * j + h : 21 + 2 * j + h, :]
                    r.mods[6 + j : 7 + j, z * width + h * 128 : z * width + (h + 1) * 128] = row

    def mod(j):
        return r.mods[j : j + 1, :]

    def own_row(z, start):
        return r.psum[z, pl.ds(start + at.k, 1), :]

    z_step(4, 1)
    xy_wait(3)
    fwd_start(3)
    z_step(4, 2)
    z_start(5)
    x_wait()

    def sib_pair(buf, send, recv, hi):
        mine = buf.at[pl.ds(pl.multiple_of((hi * 2 + at.k) * padded, padded), sent), :]
        theirs = buf.at[pl.ds(pl.multiple_of((hi * 2 + 1 - at.k) * padded, padded), sent), :]
        return (
            functools.partial(rcopy, mine, mine, send.at[hi], recv.at[hi], at.sibling()),
            functools.partial(rcopy, theirs, theirs, send.at[hi], recv.at[hi], at.sibling()),
        )

    for hi in range(2):
        sib_pair(r.xs, r.sib_send, r.sib_recv, hi)[0]().start()
    z_step(4, 3)
    xy_start(4)
    for hi in range(2):
        sib_pair(r.xs, r.sib_send, r.sib_recv, hi)[1]().wait()
    save(r.xs, r.x)

    step = 64

    def norm_tile(src, dst, shift, scale):
        def tile(n, carry):
            span = pl.ds(pl.multiple_of(n * step, step), step)
            normal, _ = normalize(src[span, :].astype(f32))
            dst[span, :] = (normal * (1.0 + mod(scale)) + mod(shift)).astype(bf16)
            return carry

        lax.fori_loop(0, tokens // step, tile, 0)

    norm_tile(r.xs, r.n1, 0, 1)
    save(r.n1, r.normed1)
    z_step(5, 1)
    fwd_wait(1)
    fwd_wait(2)

    def query_key(i, carry):
        z = i // 2
        span = pl.ds(pl.multiple_of(lax.rem(i, 2) * half, half), half)
        raw = nn(r.n1[span, :], r.w1s[z, :, : 2 * 128])
        q = raw[:, :128] + own_row(z, 12)
        k = raw[:, 128:256]
        r.qp[z, span, :] = q
        r.kp[z, span, :] = k
        r.qhs[z, span, :] = (q * head_inverse(q) * own_row(z, 16)).astype(bf16)
        r.khs[z, span, :] = (k * head_inverse(k) * own_row(z, 18)).astype(bf16)
        return carry

    def value(i, carry):
        z = i // 2
        span = pl.ds(pl.multiple_of(lax.rem(i, 2) * half, half), half)
        r.vs[z, span, :] = (nn(r.n1[span, :], r.w1s[z, :, 2 * 128 : 3 * 128]) + own_row(z, 14)).astype(bf16)
        return carry

    lax.fori_loop(0, ts, query_key, 0)
    z_step(5, 2)
    z_start(6)
    lax.fori_loop(ts, 2 * ts, query_key, 0)
    z_step(5, 3)
    xy_start(5)
    fwd_wait(3)
    save(r.w1s, r.w1)
    lax.fori_loop(0, 2 * ts, value, 0)
    tail_arrived()
    transpose(r.n1)
    n1t = save(r.xt, r.n1t)
    for src, out in ((r.qp, r.qpre), (r.kp, r.kpre), (r.vs, r.v), (r.qhs, r.qh), (r.khs, r.kh)):
        save(src, out)
    z_step(6, 1)

    qt = 256

    def attend(z):
        v_t = r.vs[z].T
        tops = [jnp.full((1, qt), masked_score, f32) for _ in range(2)]

        def tile(n, tops):
            span = pl.ds(pl.multiple_of(n * qt, qt), qt)
            allowed = r.idk[...] <= r.idq[:, span]
            outs, peaks = [], []
            for h in range(2):
                lanes = slice(h * HD, (h + 1) * HD)
                s = nt(r.khs[z, :, lanes], r.qhs[z, span, lanes] * 0.125)
                s = jnp.where(allowed, s, masked_score)
                peak = jnp.max(s, axis=0, keepdims=True)
                e = jnp.exp(s - peak)
                total = jnp.sum(e, axis=0, keepdims=True)
                r.lses[z, h : h + 1, span] = peak + jnp.log(total)
                p = (e * (1.0 / total)).astype(bf16)
                outs.append(nn(v_t[h * HD : (h + 1) * HD, :], p))
                peaks.append(jnp.maximum(tops[h], peak))
            r.atts[z, span, :] = jnp.concatenate(outs, axis=0).T.astype(bf16)
            return peaks

        tops = lax.fori_loop(0, tokens // qt, tile, tops)
        for h in range(2):
            r.tops[z, h : h + 1, :] = jnp.broadcast_to(jnp.max(tops[h], axis=1, keepdims=True), (1, 128))

    attend(0)
    xy_wait(4)
    fwd_start(4)
    z_step(6, 2)
    z_start(7)
    z_step(6, 3)
    xy_start(6)
    tail_step(0)
    attend(1)
    z_step(7, 1)
    z_step(7, 2)
    attend(2)
    xy_wait(5)
    fwd_start(5)
    z_step(7, 3)
    xy_start(7)
    g_start()
    tail_step(1)
    attend(3)
    fwd_wait(4)
    for src, out in ((r.atts, r.att), (r.lses, r.lse), (r.tops, r.top)):
        save(src, out)

    def pair(e, n):
        span = pl.ds(n * half, half)
        return rcopy(
            r.sendbuf.at[span, :], r.recvs.at[e, span, :], r.e_send.at[e, n], r.e_recv.at[e, n], at.sibling()
        )

    for n in range(2):
        span = slice(n * half, (n + 1) * half)
        for c in range(2):
            cols = slice(c * 512, (c + 1) * 512)
            acc = nt(r.atts[0, span, :], r.w1s[0, cols, 384:])
            for z in range(1, ts):
                acc = acc + nt(r.atts[z, span, :], r.w1s[z, cols, 384:])
            r.sendbuf[span, cols] = acc.astype(bf16)
        pair(0, n).start()
    for n in range(2):
        pair(0, n).wait()

        def tile(i, carry):
            span = pl.ds(pl.multiple_of(n * half + i * step, step), step)
            branch = r.sendbuf[span, :].astype(f32) + r.recvs[0, span, :].astype(f32) + mod(6)
            r.b1[span, :] = branch.astype(bf16)
            middle = (r.xs[span, :].astype(f32) + mod(2) * branch).astype(bf16)
            r.mid[span, :] = middle
            normal, _ = normalize(middle.astype(f32))
            r.n2[span, :] = (normal * (1.0 + mod(4)) + mod(3)).astype(bf16)
            return carry

        lax.fori_loop(0, half // step, tile, 0)
    for src, out in ((r.b1, r.branch1), (r.mid, r.middle), (r.n2, r.normed2)):
        save(src, out)

    def up_part(c):
        cols = slice(c * CHUNK, (c + 1) * CHUNK)

        def body(i, carry):
            z = i // 2
            span = pl.ds(pl.multiple_of(lax.rem(i, 2) * half, half), half)
            pre = nn(r.n2[span, :], r.w2s[z, :, cols])
            bias = [r.psum[z, pl.ds(24 + 4 * at.k + 2 * c + j, 1), :] for j in range(2)]
            pre = pre + jnp.concatenate(bias, axis=1)
            r.hp[z, span, cols] = pre
            inner = jnp.tanh(gelu_a * (pre + gelu_b * pre * pre * pre))
            r.hs[z, span, cols] = (0.5 * pre * (1.0 + inner)).astype(bf16)
            return carry

        lax.fori_loop(0, 2 * ts, body, 0)

    xy_wait(6)
    fwd_start(6)
    tail_step(2)
    up_part(0)
    g_wait()
    for hi in range(2):
        sib_pair(r.gs, r.gsib_send, r.gsib_recv, hi)[0]().start()
    fwd_wait(5)
    save(r.w2s, r.w2)
    up_part(1)
    save(r.hp, r.hpre)
    save(r.hs, r.hid)
    xy_wait(7)
    fwd_start(7)
    settle(n1t)
    transpose(r.n2)
    n2t = save(r.xt, r.n2t)
    for hi in range(2):
        sib_pair(r.gs, r.gsib_send, r.gsib_recv, hi)[1]().wait()
    save(r.gs, r.g)

    def diagonal(z):
        copies = []
        x_part, y_part = parts_of(z)
        for s in range(1, fs):
            span = pl.ds(row_of(lax.rem(at.f + s, fs), 1 - at.hi), 2 * per)
            for part, sends, receives, device in (
                (y_part, r.dy_send, r.dy_recv, at.ypeer()), (x_part, r.dx_send, r.dx_recv, at.xpeer(s)),
            ):
                copies.append(
                    rcopy(
                        r.d3s.at[z, span, part], r.r1o.at[z, s - 1, :, part],
                        sends.at[z, s], receives.at[z, s], device,
                    )
                )
        return copies

    def row_of(f, hi):
        return pl.multiple_of((f * 2 + hi) * 2 * per, 2 * per)

    def delta_tile(n, carry):
        span = pl.ds(pl.multiple_of(n * step, step), step)
        delta = (r.gs[span, :].astype(f32) * mod(5)).astype(bf16)
        r.dds[span, :] = delta
        return carry + jnp.sum(delta.astype(f32).reshape(step // 8, 8, features), axis=0)

    r.dbs[...] = lax.fori_loop(0, tokens // step, delta_tile, jnp.zeros((8, features), f32))
    save(r.dbs, r.db)
    save(r.dds, r.dd)
    settle(n2t)
    transpose(r.dds)
    for z in range(ts):

        def grad_tile(m, carry):
            span = pl.ds(pl.multiple_of(m * 256, 256), 256)
            r.d3s[z, span, :] = nn(r.xt[span, :], r.hs[z]).astype(bf16)
            return carry

        lax.fori_loop(0, features // 256, grad_tile, 0)
        save(r.d3s.at[z], r.d3.at[z])
        for copy in diagonal(z):
            copy.start()

    def down_part(c, first):
        cols = slice(c * CHUNK, (c + 1) * CHUNK)
        for n in range(2):
            span = slice(n * half, (n + 1) * half)
            for m in range(2):
                rows = slice(m * 512, (m + 1) * 512)
                acc = nt(r.hs[0, span, cols], r.w3s[0, rows, cols])
                for z in range(1, ts):
                    acc = acc + nt(r.hs[z, span, cols], r.w3s[z, rows, cols])
                if first:
                    r.acc[span, rows] = acc
                else:
                    r.sendbuf[span, rows] = (r.acc[span, rows] + acc).astype(bf16)
            if not first:
                pair(1, n).start()

    fwd_wait(6)
    down_part(0, True)
    fwd_wait(7)
    tail_step(3)
    save(r.w3s, r.w3)
    down_part(1, False)
    for n in range(2):
        pair(1, n).wait()

        def tile(i, carry):
            span = pl.ds(pl.multiple_of(n * half + i * step, step), step)
            branch = r.sendbuf[span, :].astype(f32) + r.recvs[1, span, :].astype(f32) + mod(7)
            r.bos[span, :] = (r.mid[span, :].astype(f32) + mod(5) * branch).astype(bf16)
            product = r.gs[span, :].astype(f32) * branch
            return carry + jnp.sum(product.reshape(step // 8, 8, features), axis=0)

        part = lax.fori_loop(0, half // step, tile, jnp.zeros((8, features), f32))
        if n == 0:
            r.gates[...] = part
        else:
            r.gates[...] += part
    for src, out in ((r.bos, r.bo), (r.gates, r.gate2), (r.mods, r.mod), (r.psum, r.par)):
        save(src, out)
    for z in range(ts):
        for copy in diagonal(z):
            copy.wait()
    for n in range(2, last):
        z_sent(n)
    for d in range(ts - 1):
        for up in (True, False):
            tail_hop(d, up, "sent")
    for n in range(len(saved)):
        settle(n)


def run_forward(fs, cs, ts, sent, padded, per, every, args):
    tokens, features = cs * padded, ts * 256
    sds = jax.ShapeDtypeStruct
    big = (ts, features, GC)
    outs = {
        "w1": (big, bf16), "w2": (big, bf16), "w3": (big, bf16),
        "x": ((tokens, features), bf16), "g": ((tokens, features), bf16), "normed1": ((tokens, features), bf16),
        "qpre": ((ts, tokens, 128), f32), "kpre": ((ts, tokens, 128), f32),
        "v": ((ts, tokens, 128), bf16), "qh": ((ts, tokens, 128), bf16), "kh": ((ts, tokens, 128), bf16),
        "att": ((ts, tokens, 128), bf16), "branch1": ((tokens, features), bf16),
        "middle": ((tokens, features), bf16), "normed2": ((tokens, features), bf16),
        "hpre": ((ts, tokens, GC), f32), "hid": ((ts, tokens, GC), bf16), "bo": ((tokens, features), bf16),
        "lse": ((ts, 2, tokens), f32), "top": ((ts, 2, 128), f32), "mod": ((8, features), f32),
        "par": ((ts, 32, 128), f32), "gate2": ((8, features), f32),
        "dd": ((tokens, features), bf16), "d3": (big, bf16), "n1t": ((features, tokens), bf16),
        "n2t": ((features, tokens), bf16), "db": ((8, features), f32), "condr": ((every, per), f32),
        "r1o": ((ts, max(fs - 1, 1), 2 * per, GC), bf16),
    }
    vm, dma = pltpu.VMEM, pltpu.SemaphoreType.DMA
    local = dict(
        w1s="w1", w2s="w2", w3s="w3", xs="x", gs="g", n1="normed1", qp="qpre", kp="kpre", vs="v", qhs="qh",
        khs="kh", atts="att", b1="branch1", mid="middle", n2="normed2", hp="hpre", hs="hid", bos="bo",
        lses="lse", tops="top", mods="mod", psum="par", gates="gate2",
        dds="dd", d3s="d3", xt="n1t", dbs="db", crow="condr",
    )
    scratch = {k: vm(*outs[v]) for k, v in local.items()}
    items = 9
    scratch.update(
        sendbuf=vm((tokens, features), bf16), recvs=vm((2, tokens, features), bf16), acc=vm((tokens, features), f32),
        cond_slots=vm((ts, every, per), f32), part=vm((every, 8, 256), f32),
        msg=vm((fs * cs * ts, 8, 256), f32), parts=vm((ts, fs * cs * 32, 128), bf16),
        x_send=dma((2 * ts,)), x_recv=dma((2 * ts,)), g_send=dma((2 * ts,)), g_recv=dma((2 * ts,)), loc=dma((3,)),
        sib_send=dma((2,)), sib_recv=dma((2,)), gsib_send=dma((2,)), gsib_recv=dma((2,)),
        c_send=dma((ts,)), c_recv=dma((ts,)), m_send=dma((fs * cs * ts,)), m_recv=dma((fs * cs * ts,)),
        core_send=dma((items, 2)), core_recv=dma((items, 2)), core_loc=dma((items, 2)),
        z_send=dma((2, items, ts)), z_recv=dma((2, items, ts)), zd_send=dma((2, ts)), zd_recv=dma((2, ts)),
        dy_send=dma((ts, fs)), dy_recv=dma((ts, fs)), dx_send=dma((ts, fs)), dx_recv=dma((ts, fs)),
        wot=vm((per, 256), bf16), wdt=vm((per, ts * 256), bf16),
        xs_send=dma((items, fs)), xs_recv=dma((items, fs)), ys_send=dma((items,)), ys_recv=dma((items,)),
        fx_send=dma((items, fs)), fx_recv=dma((items, fs)), fy_send=dma((items, fs)), fy_recv=dma((items, fs)),
        e_send=dma((2, 2)), e_recv=dma((2, 2)), out_sem=dma((len(outs) + ts,)),
    )
    anywhere, on_chip = pl.BlockSpec(memory_space=pl.ANY), pl.BlockSpec(memory_space=vm)
    results = pl.pallas_call(
        functools.partial(
            forward_kernel, fs, cs, ts, sent, padded, per, FORWARD_IN + FORWARD_OUT + tuple(scratch)
        ),
        name="forward",
        out_shape=tuple(sds(*outs[k]) for k in FORWARD_OUT),
        in_specs=[anywhere] * 6 + [on_chip] * 2 + [anywhere] + [on_chip] * 4,
        out_specs=(anywhere,) * len(FORWARD_OUT),
        scratch_shapes=list(scratch.values()),
        compiler_params=pltpu.CompilerParams(
            collective_id=0, has_side_effects=True, vmem_limit_bytes=62 << 20
        ),
    )(*[args[k] for k in FORWARD_IN])
    return bundle(FORWARD_OUT, results)


def attend_back(z, r, query_gain, key_gain):
    tokens = r.vs.shape[1]
    qt = 256
    r.dka[...] = jnp.zeros_like(r.dka)
    r.dva[...] = jnp.zeros_like(r.dva)
    k_t = r.khs[z].T

    def tile(n, carry):
        span = pl.ds(pl.multiple_of(n * qt, qt), qt)
        allowed = r.idk[...] <= r.idq[:, span]
        outs = []
        for h in range(2):
            lanes = slice(h * HD, (h + 1) * HD)
            qh, da = r.qhs[z, span, lanes] * 0.125, r.das[z, span, lanes]
            s = jnp.where(allowed, nt(r.khs[z, :, lanes], qh), masked_score)
            p = jnp.exp(s - r.lses[z, h : h + 1, span])
            dp = nt(r.vs[z, :, lanes], da)
            centre = jnp.sum(p * dp, axis=0, keepdims=True)
            ds = (p * (dp - centre)).astype(bf16)
            r.dva[h] += nn(p.astype(bf16), da)
            r.dka[h] += nn(ds, qh)
            outs.append(nn(k_t[h * HD : (h + 1) * HD, :], ds))
        r.dqa[span, :] = jnp.concatenate(outs, axis=0).T * 0.125
        return carry

    lax.fori_loop(0, tokens // qt, tile, 0)

    def finish(n, sums):
        span = pl.ds(pl.multiple_of(n * qt, qt), qt)
        dk = jnp.concatenate([r.dka[0, span, :], r.dka[1, span, :]], axis=1)
        dv = jnp.concatenate([r.dva[0, span, :], r.dva[1, span, :]], axis=1).astype(bf16)
        r.dqkv[z, span, 256:] = dv
        results = [None, None, None, jnp.sum(dv.astype(f32), axis=0, keepdims=True)]
        for i, (raw_ref, gain, delta) in enumerate(((r.qp, query_gain, r.dqa[span, :]), (r.kp, key_gain, dk))):
            raw = raw_ref[z % 2, span, :]
            inverse = head_inverse(raw)
            results[i] = jnp.sum(delta * raw * inverse, axis=0, keepdims=True)
            t = delta * gain
            out = (inverse * t - raw * (inverse * inverse * inverse) * segment_mean(t * raw)).astype(bf16)
            r.dqkv[z, span, i * 128 : (i + 1) * 128] = out
            if i == 0:
                results[2] = jnp.sum(out.astype(f32), axis=0, keepdims=True)
        return [a + b for a, b in zip(sums, results)]

    sums = lax.fori_loop(0, tokens // qt, finish, [jnp.zeros((1, 128), f32)] * 4)
    for row, value in enumerate((sums[2], sums[3], sums[0], sums[1])):
        r.vec[z, row : row + 1, :] = value


BACKWARD_IN = (
    "w1", "w2", "w3", "x", "g", "qpre", "kpre", "v", "qh", "kh", "att", "branch1",
    "middle", "n2t", "hpre", "hid", "bo", "lse", "top", "mod", "par", "gate2", "dd", "d3", "n1t", "db", "r1o",
    "idq", "idk", "wm",
)
BACKWARD_OUT = ("o1", "o2", "o3", "dxo", "boo", "maila", "mailb", "sdel", "suma", "sumb")


def backward_kernel(fs, cs, ts, sent, padded, per, keys, *values):
    r = bundle(keys, values)
    assert ts == 4
    at = Place(fs, cs, ts)
    width = 256
    tokens, features = r.gs.shape
    half = tokens // 2
    step = 64
    at.barrier()

    pending = {}
    order = []

    def load(name, src, dst):
        pltpu.make_async_copy(src, dst, r.in_sem.at[len(order)]).start()
        pending[name] = (src, dst, len(order))
        order.append(name)

    def need(*wanted):
        for name in wanted:
            src, dst, n = pending.pop(name)
            pltpu.make_async_copy(src, dst, r.in_sem.at[n]).wait()

    def load_chunk(z):
        load("d3%d" % z, r.d3.at[z], r.d.at[z])
        load("r1%d" % z, r.r1o.at[z], r.r1.at[2 * ts + z])

    load_chunk(0)
    load_chunk(1)
    load("dd", r.dd, r.dds)
    load("w3", r.w3, r.wa)
    load("hp0", r.hpre.at[0], r.hp.at[0])

    def load_rest():
        load("n2t", r.n2t, r.xt)
        load("hp1", r.hpre.at[1], r.hp.at[1])
        load_chunk(2)
        load_chunk(3)
        load("w2", r.w2, r.wb)
        load_more()

    def load_more():
        load("mod", r.mod, r.mods)
        load("g", r.g, r.gs)
        load("mid", r.middle, r.mid)
        load("b1", r.branch1, r.b1)
        load("att", r.att, r.atts)
        load("par", r.par.at[:, pl.ds(16, 8), :], r.psum)
        for name, src, dst in (
            ("qh", r.qh, r.qhs), ("kh", r.kh, r.khs), ("v", r.v, r.vs), ("lse", r.lse, r.lses),
            ("top", r.top, r.tops), ("gate2", r.gate2, r.gates),
            ("db", r.db, r.dbs),
        ):
            load(name, src, dst)
        load_raw(0)
        load_raw(1)

    def load_raw(z):
        load("qp%d" % z, r.qpre.at[z], r.qp.at[z % 2])
        load("kp%d" % z, r.kpre.at[z], r.kp.at[z % 2])

    def block_of(ref):
        def src(i):
            c = (i // ts) * 2 + at.k
            return ref.at[
                pl.ds(pl.multiple_of(c * padded, padded), sent),
                pl.ds(pl.multiple_of(lax.rem(i, ts) * width, width), width),
            ]

        return src

    bo_start, bo_wait = exchange_images(
        at, block_of(r.bo), lambda i: r.boo.at[i], r.bo_send, r.bo_recv, r.loc.at[1]
    )
    dx_start, dx_wait = exchange_images(
        at, block_of(r.dds), lambda i: r.dxo.at[i], r.dx_send, r.dx_recv, r.loc.at[0]
    )
    outs = (r.o1, r.o2, r.o3)

    def slot(g, z):
        return z + (ts if g == 1 else 0)

    def rows(f, hi):
        return pl.ds(pl.multiple_of((f * 2 + hi) * 2 * per, 2 * per), 2 * per)

    def far(s):
        return lax.rem(at.f + s, fs)

    def stage_one(g, z, s):
        n, d = g * ts + z, slot(g, z)
        x_part, y_part = parts_of(z)
        return (
            rcopy(
                r.d.at[d, rows(far(s), 1 - at.hi), y_part], r.r1.at[n, s - 1, :, y_part],
                r.y1_send.at[n, s], r.y1_recv.at[n, s], at.ypeer(),
            ),
            rcopy(
                r.d.at[d, rows(far(s), 1 - at.hi), x_part], r.r1.at[n, s - 1, :, x_part],
                r.x1_send.at[n, s], r.x1_recv.at[n, s], at.xpeer(s),
            ),
        )

    def stage_two(g, z):
        n, d = g * ts + z, slot(g, z)
        copies = [
            rcopy(
                r.d.at[d, rows(far(s), at.hi), :], r.rx2.at[n, s - 1],
                r.x2_send.at[n, s], r.x2_recv.at[n, s], at.xpeer(s),
            )
            for s in range(1, fs)
        ]
        copies.append(
            rcopy(r.d.at[d, rows(at.f, 1 - at.hi), :], r.ry2.at[n], r.y2_send.at[n], r.y2_recv.at[n], at.ypeer())
        )
        return copies

    def rs_a(g, z):
        for s in range(1, fs):
            for copy in stage_one(g, z, s):
                copy.start()

    def rs_b(g, z):
        n, d = g * ts + z, slot(g, z)
        x_part, y_part = parts_of(z)
        for s in range(1, fs) if g < 2 else ():
            for copy in stage_one(g, z, s):
                copy.wait()
        for s in range(1, fs):
            span = rows(far(s), at.hi)
            r.d[d, span, y_part] = (r.d[d, span, y_part].astype(f32) + r.r1[n, s - 1, :, y_part].astype(f32)).astype(bf16)
        span = rows(at.f, 1 - at.hi)
        value = r.d[d, span, x_part].astype(f32)
        for s in range(1, fs):
            value = value + r.r1[n, s - 1, :, x_part].astype(f32)
        r.d[d, span, x_part] = value.astype(bf16)
        for copy in stage_two(g, z):
            copy.start()

    def roles(z):
        low = z < ts // 2
        near = z + 1 if z % 2 == 0 else z - 1
        relay, feeder = (ts // 2, ts - 1) if low else (ts // 2 - 1, 0)
        return near, relay, feeder

    def z_copy(g, z, role):
        n = g * ts + z
        near, relay, feeder = roles(z)
        if role == "near":
            return rcopy(r.ry2.at[n], r.rz.at[g, 0], r.z_send.at[n], r.z_recv.at[g, 0], (at.f, at.c, z))
        if role == "relay":
            return rcopy(r.ry2.at[n], r.rz.at[g, 1], r.z_send.at[n], r.z_recv.at[g, 1], (at.f, at.c, z))
        return rcopy(r.ry2.at[n], r.feed.at[g, z % 2], r.z_send.at[n], r.f_recv.at[g, z % 2], (at.f, at.c, relay))

    def rs_c(g, z):
        n, d = g * ts + z, slot(g, z)
        for copy in stage_two(g, z):
            copy.wait()
        span = rows(at.f, at.hi)
        for part in (slice(0, GC // 2), slice(GC // 2, GC)):
            value = r.d[d, span, part].astype(f32) + r.ry2[n, :, part].astype(f32)
            for s in range(1, fs):
                value = value + r.rx2[n, s - 1, :, part].astype(f32)
            r.ry2[n, :, part] = value.astype(bf16)

        near, relay, feeder = roles(z)

        @pl.when(at.t == near)
        def _():
            z_copy(g, z, "near").start()

        @pl.when(at.t == feeder)
        def _():
            z_copy(g, z, "feeder").start()

    def rs_d(g, z):
        n = g * ts + z

        @pl.when(at.t == roles(z)[1])
        def _():
            z_copy(g, z, "feeder").wait_recv()
            for part in (slice(0, GC // 2), slice(GC // 2, GC)):
                value = r.ry2[n, :, part].astype(f32) + r.feed[g, z % 2, :, part].astype(f32)
                r.ry2[n, :, part] = value.astype(bf16)
            z_copy(g, z, "relay").start()

    def pair_sum(g):
        src = r.total.at[pl.ds(pl.multiple_of((1 - at.k) * per, per), per)]
        own = r.total.at[pl.ds(pl.multiple_of(at.k * per, per), per)]
        keep = pltpu.make_async_copy(own, outs[g].at[at.k], r.k_loc.at[g])
        out = functools.partial(rcopy, src, outs[g].at[at.k], r.k_send.at[g], r.k_recv.at[g], at.sibling())
        inn = functools.partial(rcopy, src, outs[g].at[1 - at.k], r.k_send.at[g], r.k_recv.at[g], at.sibling())
        return keep, out, inn

    def pair_wait(g):
        keep, _, inn = pair_sum(g)
        keep.wait()
        inn().wait()

    def rs_e(g):
        for z in range(ts):

            @pl.when(at.t != z)
            def _():
                z_copy(g, z, "near").wait_send()

        for n in range(2):
            rcopy(
                r.rz.at[g, n], r.rz.at[g, n], r.z_send.at[g * ts], r.z_recv.at[g, n], at.zpeer(1)
            ).wait_recv()
        for part in (slice(0, GC // 2), slice(GC // 2, GC)):
            value = r.ry2[g * ts + at.t, :, part].astype(f32)
            for n in range(2):
                value = value + r.rz[g, n, :, part].astype(f32)
            r.total[:, part] = value
        keep, out, _ = pair_sum(g)
        keep.start()
        out().start()

    def mod(j):
        return r.mods[j : j + 1, :]

    def own_row(z, start):
        return r.psum[z, pl.ds(start + at.k, 1), :]

    def transpose(src):
        def tile(n, carry):
            span = pl.ds(pl.multiple_of(n * 128, 128), 128)
            r.xt[:, span] = src[span, :].T
            return carry

        lax.fori_loop(0, tokens // 128, tile, 0)

    def grad_into(d, cols, right):
        def tile(m, carry):
            span = pl.ds(pl.multiple_of(m * 256, 256), 256)
            r.d[d, span, cols] = nn(r.xt[span, :], right()).astype(bf16)
            return carry

        lax.fori_loop(0, features // 256, tile, 0)

    def eight(values):
        return jnp.sum(values.reshape(values.shape[0] // 8, 8, values.shape[1]), axis=0)

    def collapse(values):
        return jnp.sum(values, axis=0, keepdims=True)

    def pair(e, n):
        span = pl.ds(n * half, half)
        return rcopy(
            r.sendbuf.at[span, :], r.recvs.at[e, span, :], r.e_send.at[e, n], r.e_recv.at[e, n], at.sibling()
        )

    zeros = jnp.zeros((8, features), f32)

    def back_up(z):
        need("hp%d" % z)

        def tile(n, carry):
            span = pl.ds(pl.multiple_of(n * half, half), half)
            hidden_delta = nn(r.dds[span, :], r.wa[z])
            pre = r.hp[z % 2, span, :]
            inner = jnp.tanh(gelu_a * (pre + gelu_b * pre * pre * pre))
            slope = 0.5 * (1.0 + inner) + 0.5 * pre * (1.0 - inner * inner) * (
                gelu_a * (1.0 + 3.0 * gelu_b * pre * pre)
            )
            delta = (hidden_delta * slope).astype(bf16)
            r.hs[z, span, :] = delta
            return carry + eight(delta.astype(f32))

        r.ubs[z] = collapse(lax.fori_loop(0, 2, tile, jnp.zeros((8, GC), f32)))
        if z + 2 < ts:
            load("hp%d" % (z + 2), r.hpre.at[z + 2], r.hp.at[z % 2])

    def grad_up(z):
        grad_into(slot(1, z), slice(None), lambda: r.hs[z])

    need("d30", "d31", "r10", "r11")
    rs_b(2, 0)
    rs_b(2, 1)
    bo_start()
    load_rest()
    need("dd", "w3")
    back_up(0)
    need("n2t", "d32", "d33", "r12", "r13")
    grad_up(0)
    rs_a(1, 0)
    rs_b(2, 2)
    back_up(1)
    grad_up(1)
    rs_b(2, 3)
    back_up(2)
    grad_up(2)
    rs_a(1, 1)
    rs_c(2, 0)
    back_up(3)
    load("w1", r.w1, r.wa)
    rs_c(2, 1)
    rs_d(2, 0)
    grad_up(3)
    rs_b(1, 0)
    rs_a(1, 2)
    need("w2")
    for n in range(2):
        span = slice(n * half, (n + 1) * half)
        for m in range(2):
            cols = slice(m * 512, (m + 1) * 512)
            acc = nt(r.hs[0, span, :], r.wb[0, cols, :])
            for z in range(1, ts):
                acc = acc + nt(r.hs[z, span, :], r.wb[z, cols, :])
            r.sendbuf[span, cols] = acc.astype(bf16)
        pair(0, n).start()
    rs_c(2, 2)
    rs_d(2, 1)
    need("mid", "b1", "mod", "g")

    def norm_two(n):
        def tile(i, sums):
            span = pl.ds(pl.multiple_of(n * half + i * step, step), step)
            incoming = r.sendbuf[span, :].astype(f32) + r.recvs[0, span, :].astype(f32)
            normal, inverse = normalize(r.mid[span, :].astype(f32))
            e = incoming * (1.0 + mod(4))
            mean_e = jnp.mean(e, axis=-1, keepdims=True)
            mean_en = jnp.mean(e * normal, axis=-1, keepdims=True)
            delta = r.gs[span, :].astype(f32) + (e - mean_e - normal * mean_en) * inverse
            r.hp[0, span, :] = delta[:, :512]
            r.hp[1, span, :] = delta[:, 512:]
            low = (delta * mod(2)).astype(bf16)
            r.dds[span, :] = low
            parts = (incoming, incoming * normal, delta * r.b1[span, :].astype(f32), low.astype(f32))
            return [a + eight(b) for a, b in zip(sums, parts)]

        return tile

    sums = [zeros] * 4
    for n in range(2):
        pair(0, n).wait()
        sums = lax.fori_loop(0, half // step, norm_two(n), sums)
    shift_two, scale_two, gate_one, output_bias = (collapse(v) for v in sums)
    load("x", r.x, r.gs)
    rs_b(1, 1)
    rs_c(2, 3)
    rs_d(2, 2)
    rs_a(1, 3)

    transpose(r.dds)
    need("att", "w1")
    for z in range(ts):
        if z == 2:
            rs_d(2, 3)
            rs_c(1, 0)
        grad_into(slot(0, z), slice(384, GC), lambda: r.atts[z])

        def tile(n, carry):
            span = pl.ds(pl.multiple_of(n * half, half), half)
            r.das[z, span, :] = nn(r.dds[span, :], r.wa[z, :, 384:]).astype(bf16)
            return carry

        lax.fori_loop(0, 2, tile, 0)
    load("n1t", r.n1t, r.xt)
    rs_b(1, 2)
    need("par", "qh", "kh", "v", "lse", "top", "gate2", "db")
    for z in range(ts):
        need("qp%d" % z, "kp%d" % z)
        attend_back(z, r, own_row(z, 0), own_row(z, 2))
        if z + 2 < ts:
            load_raw(z + 2)
        if z == 0:
            need("n1t")
        grad_into(slot(0, z), slice(0, 384), lambda: r.dqkv[z])
        rs_a(0, z)
        if z == 0:
            rs_c(1, 1)
            rs_d(1, 0)
            rs_b(1, 3)
        if z == 1:
            rs_c(1, 2)
            rs_d(1, 1)
            rs_b(0, 0)
        if z == 2:
            rs_c(1, 3)
            rs_d(1, 2)
            rs_b(0, 1)
        if z == 3:
            rs_c(0, 0)
            rs_d(1, 3)
            rs_b(0, 2)

    for n in range(2):
        span = slice(n * half, (n + 1) * half)
        for m in range(2):
            cols = slice(m * 512, (m + 1) * 512)
            acc = nt(r.dqkv[0, span, :], r.wa[0, cols, :384])
            for z in range(1, ts):
                acc = acc + nt(r.dqkv[z, span, :], r.wa[z, cols, :384])
            r.sendbuf[span, cols] = acc.astype(bf16)
        pair(1, n).start()
    gate_two, down_bias = collapse(r.gates[...]), collapse(r.dbs[...])
    firsts = ((gate_one, shift_two, scale_two), (gate_two, output_bias, down_bias))
    for z in range(ts):
        lanes = slice(z * width, (z + 1) * width)
        for row in range(3):
            r.early[z, row : row + 1, :] = jnp.where(at.k == 0, firsts[0][row][:, lanes], firsts[1][row][:, lanes])
        for row in range(2):
            r.early[z, 3 + row : 4 + row, :128] = r.vec[z, 2 * row : 2 * row + 1, :]
            r.early[z, 3 + row : 4 + row, 128:] = r.vec[z, 2 * row + 1 : 2 * row + 2, :]
            r.early[z, 5 + row : 6 + row, :] = r.ubs[z, :, row * width : (row + 1) * width]
            r.early[z, 7:8, row * 128 : (row + 1) * 128] = r.tops[z, row : row + 1, :]

    def mail_slot(box):
        def slot_of(n):
            f, c, t = at.coords(n)
            return box.at[(f * 2 + c // 2) * ts + t, lax.rem(c, 2)]

        return slot_of

    def toward(box):
        return lambda n: box.at[lax.rem(n, ts)]

    m_start, m_wait = broadcast_messages(
        at, toward(r.early), mail_slot(r.mail_a), r.m_send, r.m_recv, r.loc.at[2]
    )
    l_start, l_wait = broadcast_messages(
        at, toward(r.late), mail_slot(r.mail_b), r.l_send, r.l_recv, r.loc.at[3]
    )
    m_start()
    need("x")

    def norm_one(n):
        def tile(i, sums):
            span = pl.ds(pl.multiple_of(n * half + i * step, step), step)
            incoming = r.sendbuf[span, :].astype(f32) + r.recvs[1, span, :].astype(f32)
            normal, inverse = normalize(r.gs[span, :].astype(f32))
            e = incoming * (1.0 + mod(1))
            mean_e = jnp.mean(e, axis=-1, keepdims=True)
            mean_en = jnp.mean(e * normal, axis=-1, keepdims=True)
            middle_delta = jnp.concatenate([r.hp[0, span, :], r.hp[1, span, :]], axis=1)
            r.dds[span, :] = (middle_delta + (e - mean_e - normal * mean_en) * inverse).astype(bf16)
            return [a + eight(b) for a, b in zip(sums, (incoming, incoming * normal))]

        return tile

    sums = [zeros] * 2
    for n in range(2):
        pair(1, n).wait()
        sums = lax.fori_loop(0, half // step, norm_one(n), sums)
    shift_one, scale_one = (collapse(v) for v in sums)
    for z in range(ts):
        lanes = slice(z * width, (z + 1) * width)
        r.late[z] = jnp.where(at.k == 0, shift_one[:, lanes], scale_one[:, lanes])
    l_start()
    dx_start()
    rs_b(0, 3)
    rs_c(0, 1)
    rs_d(0, 0)
    rs_e(2)
    rs_c(0, 2)
    rs_c(0, 3)
    rs_d(0, 1)
    rs_d(0, 2)
    pair_wait(2)
    rs_e(1)
    rs_d(0, 3)
    m_wait()

    l_wait()
    partial = jnp.zeros(r.silus.shape[1:], f32)
    six = [(r.mail_b, 0, 0), (r.mail_b, 1, 0), (r.mail_a, 0, 0), (r.mail_a, 0, 1), (r.mail_a, 0, 2), (r.mail_a, 1, 0)]
    for j, (box, side, row) in enumerate(six):
        value = box[:, side, row, :]
        for _ in range(3):
            low = value.astype(bf16)
            partial = partial + nt(low, r.wm[j])
            value = value - low.astype(f32)
    r.silus[at.t] = partial

    def silu_copy(s, index):
        return rcopy(r.silus.at[at.t], r.silus.at[index], r.s_send.at[s], r.s_recv.at[s], at.zpeer(s))

    for s in range(1, ts):
        silu_copy(s, at.t).start()
    def over_images(n, carry):
        plain, high, few = carry
        return plain + r.mail_a[n], jnp.maximum(high, r.mail_a[n]), few + r.mail_b[n]

    plain, high, few = lax.fori_loop(1, r.mail_a.shape[0], over_images, (r.mail_a[0], r.mail_a[0], r.mail_b[0]))
    row = lax.broadcasted_iota(jnp.int32, plain.shape, 1)
    r.sum_a[...] = jnp.where(row == 7, high, plain)
    r.sum_b[...] = few
    stores = [
        (r.mail_a, r.maila, 0), (r.mail_b, r.mailb, 1), (r.silus.at[at.t], r.sdel, 2), (r.sum_a, r.suma, 3), (r.sum_b, r.sumb, 4),
    ]
    for src, dst, n in stores[:2] + stores[3:]:
        pltpu.make_async_copy(src, dst, r.out_sem.at[n]).start()
    bo_wait()
    pair_wait(1)
    for s in range(1, ts):
        silu_copy(s, at.zfrom(s)).wait()
    total = r.silus[0]
    for z in range(1, ts):
        total = total + r.silus[z]
    r.silus[at.t] = total
    pltpu.make_async_copy(r.silus.at[at.t], r.sdel, r.out_sem.at[2]).start()
    rs_e(0)
    dx_wait()
    for src, dst, n in stores:
        pltpu.make_async_copy(src, dst, r.out_sem.at[n]).wait()
    pair_wait(0)


def run_backward(fs, cs, ts, sent, padded, per, every, args):
    tokens, features = cs * padded, ts * 256
    f1 = max(fs - 1, 1)
    chunks = 3 * ts
    vm, dma, sds = pltpu.VMEM, pltpu.SemaphoreType.DMA, jax.ShapeDtypeStruct
    rows, cube = (tokens, features), (ts, tokens, 128)
    scratch = dict(
        gs=vm(rows, bf16), hs=vm((ts, tokens, GC), bf16), hp=vm((2, tokens, GC), f32),
        wa=vm((ts, features, GC), bf16), wb=vm((ts, features, GC), bf16),
        mid=vm(rows, bf16), dbs=vm((8, features), f32), b1=vm(rows, bf16), atts=vm(cube, bf16),
        qhs=vm(cube, bf16), khs=vm(cube, bf16), vs=vm(cube, bf16), lses=vm((ts, 2, tokens), f32),
        qp=vm((2, tokens, 128), f32), kp=vm((2, tokens, 128), f32), tops=vm((ts, 2, 128), f32), gates=vm((8, features), f32),
        mods=vm((8, features), f32), psum=vm((ts, 8, 128), f32),
        dds=vm(rows, bf16), xt=vm((features, tokens), bf16), sendbuf=vm(rows, bf16), recvs=vm((2, *rows), bf16),
        das=vm(cube, bf16), dqkv=vm((ts, tokens, 384), bf16), vec=vm((ts, 4, 128), f32), ubs=vm((ts, 1, GC), f32),
        dqa=vm((tokens, 128), f32), dka=vm((2, tokens, HD), f32), dva=vm((2, tokens, HD), f32),
        early=vm((ts, 8, 256), f32), late=vm((ts, 1, 256), f32),
        mail_a=vm((every, 2, 8, 256), f32), mail_b=vm((every, 2, 1, 256), f32),
        silus=vm((ts, every, per), f32),
        d=vm((2 * ts, features, GC), bf16),
        r1=vm((chunks, f1, 2 * per, GC), bf16),
        rx2=vm((chunks, f1, 2 * per, GC), bf16), ry2=vm((chunks, 2 * per, GC), bf16),
        rz=vm((3, 2, 2 * per, GC), bf16), feed=vm((3, 2, 2 * per, GC), bf16), total=vm((2 * per, GC), f32),
        in_sem=dma((48,)), loc=dma((4,)), out_sem=dma((5,)),
        sum_a=vm((2, 8, 256), f32), sum_b=vm((2, 1, 256), f32),
        l_send=dma((fs * cs * ts,)), l_recv=dma((fs * cs * ts,)), s_send=dma((ts,)), s_recv=dma((ts,)),
        bo_send=dma((2 * ts,)), bo_recv=dma((2 * ts,)), dx_send=dma((2 * ts,)), dx_recv=dma((2 * ts,)),
        y1_send=dma((chunks, fs)), y1_recv=dma((chunks, fs)), x1_send=dma((chunks, fs)), x1_recv=dma((chunks, fs)),
        x2_send=dma((chunks, fs)), x2_recv=dma((chunks, fs)), y2_send=dma((chunks,)), y2_recv=dma((chunks,)),
        z_send=dma((chunks,)), z_recv=dma((3, 2)), f_recv=dma((3, 2)), k_send=dma((3,)), k_recv=dma((3,)), k_loc=dma((3,)),
        e_send=dma((2, 2)), e_recv=dma((2, 2)), m_send=dma((fs * cs * ts,)), m_recv=dma((fs * cs * ts,)),
    )
    anywhere, on_chip = pl.BlockSpec(memory_space=pl.ANY), pl.BlockSpec(memory_space=vm)
    share = sds((2, per, GC), f32)
    blocks = sds((2 * ts, sent, 256), bf16)
    results = pl.pallas_call(
        functools.partial(
            backward_kernel, fs, cs, ts, sent, padded, per, BACKWARD_IN + BACKWARD_OUT + tuple(scratch)
        ),
        name="backward",
        out_shape=(
            share, share, share, blocks, blocks, sds((every, 2, 8, 256), f32), sds((every, 2, 1, 256), f32),
            sds((every, per), f32), sds((2, 8, 256), f32), sds((2, 1, 256), f32),
        ),
        in_specs=[anywhere] * (len(BACKWARD_IN) - 3) + [on_chip] * 3,
        out_specs=(anywhere,) * 10,
        scratch_shapes=list(scratch.values()),
        compiler_params=pltpu.CompilerParams(
            collective_id=1, has_side_effects=True, vmem_limit_bytes=63 << 20
        ),
    )(*[args[k] for k in BACKWARD_IN])
    return bundle(BACKWARD_OUT, results)


FINISH_IN = (
    "one", "two", "three", "bo", "dx", "moda", "modb", "cond", "wq", "wk", "columns",
)
FINISH_OUT = ("block", "dinputs", "dq", "dk", "dv", "dout", "dup", "ddown", "dmod", "cq", "ck")
FINISH_SCRATCH = ("ones", "twos", "threes", "bos", "dxs", "wide", "sem")


def finish_kernel(*values):
    r = bundle(FINISH_IN + FINISH_OUT + FINISH_SCRATCH, values)
    pairs = ((r.bo, r.bos), (r.dx, r.dxs), (r.one, r.ones), (r.two, r.twos), (r.three, r.threes))
    copies = [pltpu.make_async_copy(src, dst, r.sem.at[n]) for n, (src, dst) in enumerate(pairs)]
    for copy in copies:
        copy.start()
    rows, images, _ = r.block.shape
    cond = r.cond[...]
    silu = (cond / (1.0 + jnp.exp(-cond))).astype(bf16).astype(f32)
    left = silu.T.astype(bf16)
    six = [(r.modb, 0, 0), (r.modb, 1, 0), (r.moda, 0, 0), (r.moda, 0, 1), (r.moda, 0, 2), (r.moda, 1, 0)]
    for j, (box, side, row) in enumerate(six):
        value = box[:, side, row, :]
        total = jnp.zeros((left.shape[0], value.shape[1]), f32)
        for _ in range(3):
            low = value.astype(bf16)
            total = total + nn(left, low)
            value = value - low.astype(f32)
        r.dmod[j] = total
    r.cq[...] = r.wq[...].astype(f32) * r.columns[...]
    r.ck[...] = r.wk[...].astype(f32) * r.columns[...]
    copies[0].wait()
    for i in range(images):
        r.wide[:, i, :] = r.bos[i, :rows, :].astype(f32)
    r.block[...] = r.wide[...].astype(bf16)
    copies[1].wait()
    for i in range(images):
        r.dinputs[:, i, :] = r.dxs[i, :rows, :].astype(f32)
    for copy in copies[2:]:
        copy.wait()
    for h in range(2):
        here = slice(h * 128, (h + 1) * 128)
        r.dq[:, here] = r.ones[h, :, :128]
        r.dk[:, here] = r.ones[h, :, 128:256]
        r.dv[:, here] = r.ones[h, :, 256:384]
        r.dout[here, :] = r.ones[h, :, 384:].T
        half = slice(h * GC, (h + 1) * GC)
        r.dup[:, half] = r.twos[h]
        r.ddown[half, :] = r.threes[h].T


def on_device(
    fs, cs, ts,
    inputs, cotangent, labels, scale_ids, head_flags, class_table, modulate_weight, modulate_bias,
    query_weight, key_weight, value_weight, query_bias, value_bias, query_gain, key_gain,
    output_weight, output_bias, up_weight, up_bias, down_weight, down_bias,
):
    images, rows_here, width = inputs.shape
    if images != 2 * ts or cs != 4 or ts % 2 or width != 256:
        raise ValueError("unsupported mesh")
    length = scale_ids.shape[0]
    every = labels.shape[0]
    count = fs * cs * ts
    sent = -(-rows_here // 16) * 16
    padded = -(-rows_here // 64) * 64
    tokens = cs * padded
    features = ts * width
    per = query_weight.shape[0]
    part_cols = class_table.shape[1]
    f, c, t = (lax.axis_index(n) for n in ("fsdp", "ctx", "tp"))
    core = lax.rem(c, 2)
    block = f * cs + c

    classes = class_table.shape[0]
    onehot = (labels[:, None] == jnp.arange(classes, dtype=jnp.int32)[None, :]).astype(bf16)
    cond_part = jnp.dot(onehot, class_table, preferred_element_type=f32)
    cond_spread = lax.dynamic_update_slice(
        jnp.zeros((every, per), f32), cond_part, (0, t * part_cols)
    )
    fit = ((0, 0), (0, sent - rows_here), (0, 0))

    lanes = modulate_bias.shape[2]
    small_parts = (
        modulate_bias.reshape(-1, lanes), query_bias, value_bias, query_gain, key_gain,
        output_bias, down_bias, up_bias,
    )
    total_rows, start, small_rows = sum(v.shape[0] for v in small_parts), 0, 0
    for part in small_parts:
        stop = start + part.shape[0]
        small_rows = small_rows + jnp.pad(part, ((start, total_rows - stop), (0, 0)))
        start = stop
    small = lax.dynamic_update_slice(
        jnp.zeros((small_rows.shape[0], HD), bf16), small_rows, (0, block * lanes)
    ).reshape(-1, 2 * HD)
    ids = scale_ids.reshape(cs, rows_here)
    spare = ((0, 0), (0, padded - rows_here))
    ids_query = jnp.pad(ids, spare, constant_values=-1).reshape(1, tokens)
    ids_key = jnp.pad(ids, spare, constant_values=1 << 20).reshape(tokens, 1)
    flat_modulate = modulate_weight.transpose(1, 0, 2)
    k = run_forward(
        fs, cs, ts, sent, padded, per, every,
        dict(
            xb=jnp.pad(inputs, fit), gb=jnp.pad(cotangent, fit),
            wq=query_weight, wk=key_weight, wv=value_weight, wu=up_weight, wo=output_weight, wd=down_weight,
            sp=small, cond=cond_spread,
            wm=flat_modulate, idq=ids_query, idk=ids_key,
        ),
    )
    m = run_backward(
        fs, cs, ts, sent, padded, per, every,
        {
            key: {"idq": ids_query, "idk": ids_key, "wm": flat_modulate}.get(key, getattr(k, key, None))
            for key in BACKWARD_IN
        },
    )
    heads = modulate_bias.shape[1]
    sum_one, sum_two, sum_three, dx_blocks, bo_blocks = m.o1, m.o2, m.o3, m.dxo, m.boo

    sums = m.suma
    same = jnp.concatenate([m.sumb.reshape(2, width), sums[0, :3], sums[1, :3]])
    halves_sum = sums[:, 3:7]

    def mine(values):
        return lax.dynamic_slice_in_dim(values, block * lanes, lanes, values.ndim - 1)

    same = mine(same.reshape(8, heads, HD))
    modulate_bias_grad, output_bias_grad, down_bias_grad = same[:6], same[6], same[7]
    quarter = mine(halves_sum[:, :2].reshape(2, 4, heads // 2, HD)).transpose(1, 0, 2, 3).reshape(4, heads, lanes)
    query_bias_grad, value_bias_grad, query_gain_grad, key_gain_grad = (quarter[j] for j in range(4))
    up_bias_grad = mine(halves_sum[:, 2:].reshape(-1, HD))
    head_max = sums[:, 7].reshape(heads, 128)[:, 0]

    silu_cols = lax.dynamic_slice_in_dim(m.sdel, t * part_cols, part_cols, 1)
    primal, silu_back = jax.vjp(jax.nn.silu, cond_part)
    cond_delta = silu_back(silu_cols)[0]
    class_table_grad = jnp.dot(onehot.astype(f32).T, cond_delta, precision=precise)

    factor = jnp.where(
        head_flags == 1,
        jnp.sqrt(clip_threshold / jnp.maximum(head_max, clip_threshold)),
        jnp.ones_like(head_max),
    )
    columns = jnp.repeat(factor, HD)
    square, flat_rows = (per, width), (rows_here, images, width)
    share = pltpu.VMEM((2, per, GC), f32)
    sent_rows = pltpu.VMEM((images, sent, width), bf16)
    (
        block_out, inputs_grad, query_weight_grad, key_weight_grad, value_weight_grad, output_weight_grad,
        up_weight_grad, down_weight_grad, modulate_weight_grad, clipped_query, clipped_key,
    ) = pl.pallas_call(
        finish_kernel,
        name="finish",
        out_shape=(
            jax.ShapeDtypeStruct(flat_rows, bf16), jax.ShapeDtypeStruct(flat_rows, f32),
            jax.ShapeDtypeStruct(square, f32), jax.ShapeDtypeStruct(square, f32),
            jax.ShapeDtypeStruct(square, f32), jax.ShapeDtypeStruct((width, per), f32),
            jax.ShapeDtypeStruct(up_weight.shape, f32), jax.ShapeDtypeStruct(down_weight.shape, f32),
            jax.ShapeDtypeStruct((6, per, width), f32),
            jax.ShapeDtypeStruct(square, f32), jax.ShapeDtypeStruct(square, f32),
        ),
        in_specs=[pl.BlockSpec(memory_space=pl.ANY)] * 5 + [pl.BlockSpec(memory_space=pltpu.VMEM)] * 6,
        scratch_shapes=[
            share, share, share, sent_rows, sent_rows, pltpu.VMEM(flat_rows, f32), pltpu.SemaphoreType.DMA((5,)),
        ],
        compiler_params=pltpu.CompilerParams(vmem_limit_bytes=62 << 20),
    )(
        sum_one, sum_two, sum_three, bo_blocks, dx_blocks, m.maila, m.mailb, k.condr,
        query_weight, key_weight, columns[None, :],
    )
    block_out, inputs_grad = block_out.transpose(1, 0, 2), inputs_grad.transpose(1, 0, 2)
    modulate_weight_grad = modulate_weight_grad.transpose(1, 0, 2)
    clipped_query_bias = query_bias.astype(f32) * factor[:, None]
    return (
        block_out, inputs_grad, class_table_grad, modulate_weight_grad, modulate_bias_grad,
        query_weight_grad, key_weight_grad, value_weight_grad, query_bias_grad, value_bias_grad,
        query_gain_grad, key_gain_grad, output_weight_grad, output_bias_grad,
        up_weight_grad, up_bias_grad, down_weight_grad, down_bias_grad,
        clipped_query, clipped_key, clipped_query_bias,
    )


def solution(mesh):
    rows = P("fsdp", "ctx", "tp")
    table = P(None, ("fsdp", "ctx", "tp"))
    left = P(("fsdp", "ctx"), "tp")
    right = P("tp", ("fsdp", "ctx"))
    modulate = P(("fsdp", "ctx"), None, "tp")
    modulate_small = P(None, "tp", ("fsdp", "ctx"))
    return jax.shard_map(
        functools.partial(on_device, mesh.shape["fsdp"], mesh.shape["ctx"], mesh.shape["tp"]),
        mesh=mesh,
        in_specs=(
            rows, rows, P(), P(), P("tp"), table, modulate, modulate_small,
            left, left, left, right, right, right, right,
            right, right, left, right, right, right,
        ),
        out_specs=(
            rows, rows, table, modulate, modulate_small,
            left, left, left, right, right, right, right,
            right, right, left, right, right, right,
            left, left, right,
        ),
        check_vma=False,
    )
```

```python
import functools
import math

import jax
import jax.numpy as jnp
from jax import lax
from jax.experimental import pallas as pl
from jax.experimental.pallas import tpu as pltpu
from jax.sharding import PartitionSpec as P

HD = 64
GC = 512
CHUNK = 256
MESH = pl.DeviceIdType.MESH
precise = lax.Precision.HIGHEST
norm_epsilon = 1e-06
clip_threshold = 2.0
masked_score = -1e30
f32, bf16 = jnp.float32, jnp.bfloat16


def product(left, right, form):
    return jnp.einsum(form, left, right, preferred_element_type=f32)


def rcopy(src, dst, send_sem, recv_sem, device):
    return pltpu.make_async_remote_copy(
        src_ref=src,
        dst_ref=dst,
        send_sem=send_sem,
        recv_sem=recv_sem,
        device_id=device,
        device_id_type=MESH,
    )


class Place:
    def __init__(self, fs, cs, ts):
        self.fs, self.cs, self.ts = fs, cs, ts
        self.count = fs * cs * ts
        self.f, self.c, self.t = (lax.axis_index(n) for n in ("fsdp", "ctx", "tp"))
        self.hi, self.k = self.c // 2, lax.rem(self.c, 2)
        self.me = (self.f * cs + self.c) * ts + self.t
        self.slot = self.hi * ts + self.t

    def coords(self, n):
        return (n // (self.cs * self.ts), lax.rem(n // self.ts, self.cs), lax.rem(n, self.ts))

    def sibling(self):
        return (self.f, self.hi * 2 + 1 - self.k, self.t)

    def ypeer(self):
        return (self.f, (1 - self.hi) * 2 + self.k, self.t)

    def xpeer(self, s):
        return (lax.rem(self.f + s, self.fs), self.c, self.t)

    def xfrom(self, s):
        return lax.rem(self.f + self.fs - s, self.fs)

    def zpeer(self, s):
        return (self.f, self.c, lax.rem(self.t + s, self.ts))

    def zto(self, s):
        return lax.rem(self.t + s, self.ts)

    def zfrom(self, s):
        return lax.rem(self.t + self.ts - s, self.ts)

    def barrier(self):
        sem = pltpu.get_barrier_semaphore()

        def greet(n, carry):
            @pl.when(n != self.me)
            def _():
                pl.semaphore_signal(sem, inc=1, device_id=self.coords(n), device_id_type=MESH)

            return carry

        lax.fori_loop(0, self.count, greet, 0)
        pl.semaphore_wait(sem, self.count - 1)


def exchange_images(at, src_of, dst_of, send_sems, recv_sems, local_sem):
    slots = 2 * at.ts

    def start():
        for i in range(slots):
            hi, t = i // at.ts, i % at.ts

            @pl.when(i != at.slot)
            def _():
                rcopy(
                    src_of(i),
                    dst_of(at.slot),
                    send_sems.at[i],
                    recv_sems.at[at.slot],
                    (at.f, hi * 2 + at.k, t),
                ).start()

            @pl.when(i == at.slot)
            def _():
                pltpu.make_async_copy(src_of(i), dst_of(i), local_sem).start()

    def wait():
        for i in range(slots):
            @pl.when(i != at.slot)
            def _():
                rcopy(src_of(i), dst_of(i), send_sems.at[i], recv_sems.at[i], (at.f, at.c, at.t)).wait()

            @pl.when(i == at.slot)
            def _():
                pltpu.make_async_copy(src_of(i), dst_of(i), local_sem).wait()

    return start, wait


def broadcast_messages(at, src_of, slot_of, send_sems, recv_sems, local_sem):
    def start():
        def each(n, carry):
            @pl.when(n != at.me)
            def _():
                rcopy(src_of(n), slot_of(at.me), send_sems.at[n], recv_sems.at[at.me], at.coords(n)).start()

            @pl.when(n == at.me)
            def _():
                pltpu.make_async_copy(src_of(n), slot_of(n), local_sem).start()

            return carry

        lax.fori_loop(0, at.count, each, 0)

    def wait():
        def each(n, carry):
            @pl.when(n != at.me)
            def _():
                rcopy(src_of(n), slot_of(n), send_sems.at[n], recv_sems.at[n], at.coords(n)).wait()

            @pl.when(n == at.me)
            def _():
                pltpu.make_async_copy(src_of(n), slot_of(n), local_sem).wait()

            return carry

        lax.fori_loop(0, at.count, each, 0)

    return start, wait


FORWARD_IN = ("xb", "gb", "wq", "wk", "wv", "wu", "wo", "wd", "sp", "cond", "wm", "idq", "idk")
FORWARD_OUT = (
    "w1", "w2", "w3", "x", "g", "normed1", "qpre", "kpre", "v", "qh", "kh", "att", "branch1",
    "middle", "normed2", "hpre", "hid", "bo", "lse", "top", "mod", "par", "gate2",
    "dd", "d3", "n1t", "n2t", "db", "condr", "r1o",
)


def parts_of(z):
    cut = GC // 2 if z % 2 == 0 else GC // 4
    return slice(cut, GC), slice(0, cut)


class Refs:
    pass


def bundle(keys, values):
    refs = Refs()
    for key, value in zip(keys, values, strict=True):
        setattr(refs, key, value)
    return refs


def normalize(values):
    centered = values - jnp.mean(values, axis=-1, keepdims=True)
    inverse = lax.rsqrt(jnp.mean(centered * centered, axis=-1, keepdims=True) + norm_epsilon)
    return centered * inverse, inverse


def nt(left, right):
    return lax.dot_general(left, right, (((1,), (1,)), ((), ())), preferred_element_type=f32)


def nn(left, right):
    return lax.dot_general(left, right, (((1,), (0,)), ((), ())), preferred_element_type=f32)


def segment_mean(values):
    row = lax.broadcasted_iota(jnp.int32, (2 * HD, 2 * HD), 0) < HD
    col = lax.broadcasted_iota(jnp.int32, (2 * HD, 2 * HD), 1) < HD
    same = jnp.where(row == col, 1.0 / HD, 0.0).astype(bf16)
    high = values.astype(bf16)
    rest = values - high.astype(f32)
    middle = rest.astype(bf16)
    low = (rest - middle.astype(f32)).astype(bf16)
    return nn(high, same) + nn(middle, same) + nn(low, same)


def head_inverse(values):
    return lax.rsqrt(segment_mean(values * values) + norm_epsilon)


gelu_a = math.sqrt(2.0 / math.pi)
gelu_b = 0.044715


def forward_kernel(fs, cs, ts, sent, padded, per, keys, *values):
    r = bundle(keys, values)
    at = Place(fs, cs, ts)
    width = 256
    tokens, features = r.xs.shape
    half = tokens // 2
    quarter = features // ts
    zero = jnp.zeros((padded - sent, features), bf16)
    for c in range(cs):
        r.xs[c * padded + sent : (c + 1) * padded, :] = zero
        r.gs[c * padded + sent : (c + 1) * padded, :] = zero
    at.barrier()

    def block_at(out):
        def dst(i):
            c = (i // ts) * 2 + at.k
            return out.at[
                pl.ds(pl.multiple_of(c * padded, padded), sent),
                pl.ds(pl.multiple_of(lax.rem(i, ts) * width, width), width),
            ]

        return dst

    def staged(i):
        return r.d3s.at[i // 2, pl.ds((i % 2) * sent, sent), pl.ds(0, width)]

    x_start, x_wait = exchange_images(at, staged, block_at(r.xs), r.x_send, r.x_recv, r.loc.at[0])
    g_start, g_wait = exchange_images(at, staged, block_at(r.gs), r.g_send, r.g_recv, r.loc.at[1])

    def stage_images(src):
        count, images, _ = src.shape
        for lanes in (slice(0, 128), slice(128, 256)):
            r.wide[...] = src[:, :, lanes].astype(f32)
            for i in range(images):
                top = (i % 2) * sent
                r.d3s[i // 2, top : top + count, lanes] = r.wide[:, i, :].astype(bf16)
                if sent > count:
                    r.d3s[i // 2, top + count : top + sent, lanes] = jnp.zeros((sent - count, 128), bf16)

    r.wot[...] = r.wo[...].T
    r.wdt[...] = r.wd[...].T
    pieces, items = [[(r.sp, None, None)]], [(r.parts, None, r.sp.shape[0])]
    for col, sources in ((0, (r.wq,)), (128, (r.wk,)), (256, (r.wv, r.wot))):
        pieces.append([(ref, 128, (0, 128, col + 128 * i)) for i, ref in enumerate(sources)])
        items.append((r.w1s, slice(col, col + 128 * len(sources)), per))
    for full, ref, widths in ((r.w2s, r.wu, (256, 256)), (r.w3s, r.wdt, (256, 128, 128))):
        col = 0
        for w in widths:
            pieces.append([(ref, w, (col, GC, col))])
            items.append((full, slice(col, col + w), per))
            col += w

    def slab(n, z, nz, f, hi, k=0, blocks=2):
        full, cols, size = items[n]
        row = pl.multiple_of(((f * 2 + hi) * 2 + k) * size, size)
        span = pl.ds(row, blocks * size)
        return full.at[pl.ds(z, nz), span, :] if cols is None else full.at[pl.ds(z, nz), span, cols]

    def core_pair(n):
        full, _, size = items[n]

        def place(z, k, cols):
            span = pl.ds(pl.multiple_of(((at.f * 2 + at.hi) * 2 + k) * size, size), size)
            return full.at[z, span, :] if cols is None else full.at[z, span, cols]

        copies = []
        for i, (ref, w, where) in enumerate(pieces[n]):
            if where is None:
                mine, theirs, cols = ref, ref, None
            else:
                start, stride, col = where
                mine, theirs = (
                    ref.at[:, pl.ds(pl.multiple_of(start + k * stride, 128), w)] for k in (at.k, 1 - at.k)
                )
                cols = slice(col, col + w)
            sems = (r.core_send.at[n, i], r.core_recv.at[n, i], at.sibling())
            copies.append(
                (
                    functools.partial(pltpu.make_async_copy, mine, place(at.t, at.k, cols), r.core_loc.at[n, i]),
                    functools.partial(rcopy, theirs, place(at.t, at.k, cols), *sems),
                    functools.partial(rcopy, theirs, place(at.t, 1 - at.k, cols), *sems),
                )
            )
        return copies

    def core_start(n):
        for keep, out, _ in core_pair(n):
            keep().start()
            out().start()

    def core_wait(n):
        for keep, _, inn in core_pair(n):
            keep().wait()
            inn().wait()

    def hop(n, d, up, action):
        block = at.t - d if up else at.t + d
        sends = ((block >= 0) & (at.t < ts - 1)) if up else ((block < ts) & (at.t > 0))

        @pl.when(sends)
        def _():
            src = slab(n, block, 1, at.f, at.hi)
            side = 0 if up else 1
            copy = rcopy(
                src, src, r.z_send.at[side, n, d], r.z_recv.at[side, n, d + 1],
                (at.f, at.c, at.t + 1 if up else at.t - 1),
            )
            copy.start() if action == "start" else copy.wait_send()

    def z_start(n):
        hop(n, 0, True, "start")
        hop(n, 0, False, "start")

    def z_step(n, d):
        for up in (True, False):
            block = at.t - d if up else at.t + d

            @pl.when((block >= 0) & (block < ts))
            def _():
                src = slab(n, block, 1, at.f, at.hi)
                side = 0 if up else 1
                rcopy(
                    src, src, r.z_send.at[side, n, d], r.z_recv.at[side, n, d], (at.f, at.c, at.t)
                ).wait_recv()

            if d < ts - 1:
                hop(n, d, up, "start")

    def z_wait(n):
        for d in range(1, ts):
            z_step(n, d)

    def direct_start(n):
        for s in range(1, ts):
            src = slab(n, at.t, 1, at.f, at.hi)
            rcopy(src, src, r.zd_send.at[n, s], r.zd_recv.at[n, s], at.zpeer(s)).start()

    def direct_wait(n):
        for s in range(1, ts):
            src = slab(n, at.zfrom(s), 1, at.f, at.hi)
            rcopy(src, src, r.zd_send.at[n, s], r.zd_recv.at[n, s], at.zpeer(s)).wait()

    def own(f, hi, k=0, n=2):
        return slab(last, at.t, 1, f, hi, k, n)

    def tail_own(action):
        src = own(at.f, at.hi)
        rcopy(src, src, r.ys_send.at[last], r.ys_recv.at[last], at.ypeer()).start()
        for s in range(1, fs):
            rcopy(src, src, r.xs_send.at[last, s], r.xs_recv.at[last, s], at.xpeer(s)).start()

    def tail_forward():
        src = own(at.f, 1 - at.hi)
        rcopy(src, src, r.ys_send.at[last], r.ys_recv.at[last], at.ypeer()).wait()
        for s in range(1, fs):
            src = own(at.xfrom(s), at.hi)
            rcopy(src, src, r.xs_send.at[last, s], r.xs_recv.at[last, s], at.xpeer(s)).wait()
        for s in range(1, fs):
            src = own(at.f, 1 - at.hi, 1, 1)
            rcopy(src, src, r.fx_send.at[last, s], r.fx_recv.at[last, s], at.xpeer(s)).start()
            src = own(at.xfrom(s), at.hi, 0, 1)
            rcopy(src, src, r.fy_send.at[last, s], r.fy_recv.at[last, s], at.ypeer()).start()

    def tail_arrived():
        for s in range(1, fs):
            src = own(at.xfrom(s), 1 - at.hi, 1, 1)
            rcopy(src, src, r.fx_send.at[last, s], r.fx_recv.at[last, s], at.xpeer(s)).wait()
            src = own(at.xfrom(s), 1 - at.hi, 0, 1)
            rcopy(src, src, r.fy_send.at[last, s], r.fy_recv.at[last, s], at.ypeer()).wait()

    def tail_block(z):
        full, cols, _ = items[last]
        return full.at[pl.ds(z, 1), :, cols]

    def tail_hop(d, up, action):
        block = at.t - d if up else at.t + d
        sends = ((block >= 0) & (at.t < ts - 1)) if up else ((block < ts) & (at.t > 0))

        @pl.when(sends)
        def _():
            src = tail_block(block)
            side = 0 if up else 1
            copy = rcopy(
                src, src, r.z_send.at[side, last, d], r.z_recv.at[side, last, d + 1],
                (at.f, at.c, at.t + 1 if up else at.t - 1),
            )
            copy.start() if action == "start" else copy.wait_send()

    def tail_step(d):
        for up in (True, False):
            block = at.t - d if up else at.t + d
            if d > 0:

                @pl.when((block >= 0) & (block < ts))
                def _():
                    src = tail_block(block)
                    side = 0 if up else 1
                    rcopy(
                        src, src, r.z_send.at[side, last, d], r.z_recv.at[side, last, d], (at.f, at.c, at.t)
                    ).wait_recv()

            if d < ts - 1:
                tail_hop(d, up, "start")

    def z_sent(n):
        for d in range(ts - 1):
            for up in (True, False):
                hop(n, d, up, "sent")

    def xy_start(n):
        src = slab(n, 0, ts, at.f, at.hi)
        rcopy(src, src, r.ys_send.at[n], r.ys_recv.at[n], at.ypeer()).start()
        for s in range(1, fs):
            rcopy(src, src, r.xs_send.at[n, s], r.xs_recv.at[n, s], at.xpeer(s)).start()

    def xy_wait(n):
        src = slab(n, 0, ts, at.f, 1 - at.hi)
        rcopy(src, src, r.ys_send.at[n], r.ys_recv.at[n], at.ypeer()).wait()
        for s in range(1, fs):
            src = slab(n, 0, ts, at.xfrom(s), at.hi)
            rcopy(src, src, r.xs_send.at[n, s], r.xs_recv.at[n, s], at.xpeer(s)).wait()

    def fwd_start(n):
        zh = ts // 2 - n % 2
        for s in range(1, fs):
            src = slab(n, zh, ts - zh, at.f, 1 - at.hi)
            rcopy(src, src, r.fx_send.at[n, s], r.fx_recv.at[n, s], at.xpeer(s)).start()
            src = slab(n, 0, zh, at.xfrom(s), at.hi)
            rcopy(src, src, r.fy_send.at[n, s], r.fy_recv.at[n, s], at.ypeer()).start()

    def fwd_wait(n):
        zh = ts // 2 - n % 2
        for s in range(1, fs):
            src = slab(n, zh, ts - zh, at.xfrom(s), 1 - at.hi)
            rcopy(src, src, r.fx_send.at[n, s], r.fx_recv.at[n, s], at.xpeer(s)).wait()
            src = slab(n, 0, zh, at.xfrom(s), 1 - at.hi)
            rcopy(src, src, r.fy_send.at[n, s], r.fy_recv.at[n, s], at.ypeer()).wait()

    last = len(items) - 1
    saved = []

    def save(src, out):
        copy = pltpu.make_async_copy(src, out, r.out_sem.at[len(saved)])
        copy.start()
        saved.append([src, out, True])
        return len(saved) - 1

    def settle(n):
        src, out, waiting = saved[n]
        if waiting:
            pltpu.make_async_copy(src, out, r.out_sem.at[n]).wait()
            saved[n][2] = False

    def transpose(src):
        def tile(n, carry):
            span = pl.ds(pl.multiple_of(n * 128, 128), 128)
            r.xt[:, span] = src[span, :].T
            return carry

        lax.fori_loop(0, tokens // 128, tile, 0)

    r.cond_slots[at.t] = r.cond[...]

    def cond_copy(s, slot):
        return rcopy(r.cond, r.cond_slots.at[slot], r.c_send.at[s], r.c_recv.at[s], at.zpeer(s))

    for s in range(1, ts):
        cond_copy(s, at.t).start()
    for n in (0, 1, last, 2, 3):
        core_start(n)
    core_wait(0)
    direct_start(0)
    core_wait(1)
    direct_start(1)
    core_wait(last)
    tail_own("start")
    for n in range(4, last):
        core_start(n)
    core_wait(2)
    z_start(2)
    direct_wait(0)
    xy_start(0)

    stage_images(r.xb)

    for s in range(1, ts):
        cond_copy(s, at.zfrom(s)).wait()
    cond = r.cond_slots[0]
    for z in range(1, ts):
        cond = cond + r.cond_slots[z]
    r.crow[...] = cond
    save(r.crow, r.condr)
    silu = (cond / (1.0 + jnp.exp(-cond))).astype(bf16)
    for j in range(6):
        r.part[:, j, :] = nn(silu, r.wm[j])

    def image_of(n):
        f, c, t = at.coords(n)
        return (f * 2 + c // 2) * ts + t

    m_start, m_wait = broadcast_messages(
        at, lambda n: r.part.at[image_of(n)], lambda n: r.msg.at[n], r.m_send, r.m_recv, r.loc.at[2]
    )
    xy_wait(0)
    fwd_start(0)
    tail_forward()
    direct_wait(1)
    xy_start(1)
    z_step(2, 1)
    core_wait(3)
    z_start(3)
    z_step(2, 2)
    z_step(2, 3)
    xy_start(2)
    xy_wait(1)
    fwd_start(1)
    z_step(3, 1)
    m_start()
    z_step(3, 2)
    xy_wait(2)
    fwd_start(2)
    z_step(3, 3)
    xy_start(3)
    x_start()
    for n in range(4, last):
        core_wait(n)
    fwd_wait(0)
    m_wait()
    z_start(4)

    blocks = fs * cs
    rows_small = r.sp.shape[0]

    def small_sum(n, carry):
        return carry + r.parts[:, pl.ds(pl.multiple_of(n * rows_small, rows_small), rows_small), :].astype(f32)

    r.psum[...] = lax.fori_loop(0, blocks, small_sum, jnp.zeros(r.psum.shape, f32))
    for z in range(ts):

        def mod_sum(n, carry):
            return carry + r.msg[n * ts + z]

        total = lax.fori_loop(0, blocks, mod_sum, jnp.zeros((8, width), f32))
        for j in range(6):
            for h in range(2):
                value = total[j : j + 1, h * 128 : (h + 1) * 128] + r.psum[z, 2 * j + h : 2 * j + h + 1, :]
                r.mods[j : j + 1, z * width + h * 128 : z * width + (h + 1) * 128] = value.astype(bf16).astype(f32)
                if j < 2:
                    row = r.psum[z, 20 + 2 * j + h : 21 + 2 * j + h, :]
                    r.mods[6 + j : 7 + j, z * width + h * 128 : z * width + (h + 1) * 128] = row

    def mod(j):
        return r.mods[j : j + 1, :]

    def own_row(z, start):
        return r.psum[z, pl.ds(start + at.k, 1), :]

    z_step(4, 1)
    xy_wait(3)
    fwd_start(3)
    z_step(4, 2)
    z_start(5)
    x_wait()

    def sib_pair(buf, send, recv, hi):
        mine = buf.at[pl.ds(pl.multiple_of((hi * 2 + at.k) * padded, padded), sent), :]
        theirs = buf.at[pl.ds(pl.multiple_of((hi * 2 + 1 - at.k) * padded, padded), sent), :]
        return (
            functools.partial(rcopy, mine, mine, send.at[hi], recv.at[hi], at.sibling()),
            functools.partial(rcopy, theirs, theirs, send.at[hi], recv.at[hi], at.sibling()),
        )

    for hi in range(2):
        sib_pair(r.xs, r.sib_send, r.sib_recv, hi)[0]().start()
    z_step(4, 3)
    xy_start(4)
    for hi in range(2):
        sib_pair(r.xs, r.sib_send, r.sib_recv, hi)[1]().wait()
    save(r.xs, r.x)

    step = 64

    def norm_tile(src, dst, shift, scale):
        def tile(n, carry):
            span = pl.ds(pl.multiple_of(n * step, step), step)
            normal, _ = normalize(src[span, :].astype(f32))
            dst[span, :] = (normal * (1.0 + mod(scale)) + mod(shift)).astype(bf16)
            return carry

        lax.fori_loop(0, tokens // step, tile, 0)

    norm_tile(r.xs, r.n1, 0, 1)
    stage_images(r.gb)
    save(r.n1, r.normed1)
    z_step(5, 1)
    fwd_wait(1)
    fwd_wait(2)

    def query_key(i, carry):
        z = i // 2
        span = pl.ds(pl.multiple_of(lax.rem(i, 2) * half, half), half)
        raw = nn(r.n1[span, :], r.w1s[z, :, : 2 * 128])
        q = raw[:, :128] + own_row(z, 12)
        k = raw[:, 128:256]
        r.qp[z, span, :] = q
        r.kp[z, span, :] = k
        r.qhs[z, span, :] = (q * head_inverse(q) * own_row(z, 16)).astype(bf16)
        r.khs[z, span, :] = (k * head_inverse(k) * own_row(z, 18)).astype(bf16)
        return carry

    def value(i, carry):
        z = i // 2
        span = pl.ds(pl.multiple_of(lax.rem(i, 2) * half, half), half)
        r.vs[z, span, :] = (nn(r.n1[span, :], r.w1s[z, :, 2 * 128 : 3 * 128]) + own_row(z, 14)).astype(bf16)
        return carry

    lax.fori_loop(0, ts, query_key, 0)
    z_step(5, 2)
    z_start(6)
    lax.fori_loop(ts, 2 * ts, query_key, 0)
    z_step(5, 3)
    xy_start(5)
    fwd_wait(3)
    save(r.w1s, r.w1)
    lax.fori_loop(0, 2 * ts, value, 0)
    tail_arrived()
    transpose(r.n1)
    n1t = save(r.xt, r.n1t)
    for src, out in ((r.qp, r.qpre), (r.kp, r.kpre), (r.vs, r.v), (r.qhs, r.qh), (r.khs, r.kh)):
        save(src, out)
    z_step(6, 1)

    qt = 256

    def attend(z):
        v_t = r.vs[z].T
        tops = [jnp.full((1, qt), masked_score, f32) for _ in range(2)]

        def tile(n, tops):
            span = pl.ds(pl.multiple_of(n * qt, qt), qt)
            allowed = r.idk[...] <= r.idq[:, span]
            outs, peaks = [], []
            for h in range(2):
                lanes = slice(h * HD, (h + 1) * HD)
                s = nt(r.khs[z, :, lanes], r.qhs[z, span, lanes] * 0.125)
                s = jnp.where(allowed, s, masked_score)
                peak = jnp.max(s, axis=0, keepdims=True)
                e = jnp.exp(s - peak)
                total = jnp.sum(e, axis=0, keepdims=True)
                r.lses[z, h : h + 1, span] = peak + jnp.log(total)
                p = (e * (1.0 / total)).astype(bf16)
                outs.append(nn(v_t[h * HD : (h + 1) * HD, :], p))
                peaks.append(jnp.maximum(tops[h], peak))
            r.atts[z, span, :] = jnp.concatenate(outs, axis=0).T.astype(bf16)
            return peaks

        tops = lax.fori_loop(0, tokens // qt, tile, tops)
        for h in range(2):
            r.tops[z, h : h + 1, :] = jnp.broadcast_to(jnp.max(tops[h], axis=1, keepdims=True), (1, 128))

    attend(0)
    xy_wait(4)
    fwd_start(4)
    z_step(6, 2)
    z_start(7)
    z_step(6, 3)
    xy_start(6)
    tail_step(0)
    attend(1)
    z_step(7, 1)
    z_step(7, 2)
    attend(2)
    xy_wait(5)
    fwd_start(5)
    z_step(7, 3)
    xy_start(7)
    g_start()
    tail_step(1)
    attend(3)
    fwd_wait(4)
    for src, out in ((r.atts, r.att), (r.lses, r.lse), (r.tops, r.top)):
        save(src, out)

    def pair(e, n):
        span = pl.ds(n * half, half)
        return rcopy(
            r.sendbuf.at[span, :], r.recvs.at[e, span, :], r.e_send.at[e, n], r.e_recv.at[e, n], at.sibling()
        )

    for n in range(2):
        span = slice(n * half, (n + 1) * half)
        for c in range(2):
            cols = slice(c * 512, (c + 1) * 512)
            acc = nt(r.atts[0, span, :], r.w1s[0, cols, 384:])
            for z in range(1, ts):
                acc = acc + nt(r.atts[z, span, :], r.w1s[z, cols, 384:])
            r.sendbuf[span, cols] = acc.astype(bf16)
        pair(0, n).start()
    for n in range(2):
        pair(0, n).wait()

        def tile(i, carry):
            span = pl.ds(pl.multiple_of(n * half + i * step, step), step)
            branch = r.sendbuf[span, :].astype(f32) + r.recvs[0, span, :].astype(f32) + mod(6)
            r.b1[span, :] = branch.astype(bf16)
            middle = (r.xs[span, :].astype(f32) + mod(2) * branch).astype(bf16)
            r.mid[span, :] = middle
            normal, _ = normalize(middle.astype(f32))
            r.n2[span, :] = (normal * (1.0 + mod(4)) + mod(3)).astype(bf16)
            return carry

        lax.fori_loop(0, half // step, tile, 0)
    for src, out in ((r.b1, r.branch1), (r.mid, r.middle), (r.n2, r.normed2)):
        save(src, out)

    def up_part(c):
        cols = slice(c * CHUNK, (c + 1) * CHUNK)

        def body(i, carry):
            z = i // 2
            span = pl.ds(pl.multiple_of(lax.rem(i, 2) * half, half), half)
            pre = nn(r.n2[span, :], r.w2s[z, :, cols])
            bias = [r.psum[z, pl.ds(24 + 4 * at.k + 2 * c + j, 1), :] for j in range(2)]
            pre = pre + jnp.concatenate(bias, axis=1)
            r.hp[z, span, cols] = pre
            inner = jnp.tanh(gelu_a * (pre + gelu_b * pre * pre * pre))
            r.hs[z, span, cols] = (0.5 * pre * (1.0 + inner)).astype(bf16)
            return carry

        lax.fori_loop(0, 2 * ts, body, 0)

    xy_wait(6)
    fwd_start(6)
    tail_step(2)
    up_part(0)
    g_wait()
    for hi in range(2):
        sib_pair(r.gs, r.gsib_send, r.gsib_recv, hi)[0]().start()
    fwd_wait(5)
    save(r.w2s, r.w2)
    up_part(1)
    save(r.hp, r.hpre)
    save(r.hs, r.hid)
    xy_wait(7)
    fwd_start(7)
    settle(n1t)
    transpose(r.n2)
    n2t = save(r.xt, r.n2t)
    for hi in range(2):
        sib_pair(r.gs, r.gsib_send, r.gsib_recv, hi)[1]().wait()
    save(r.gs, r.g)

    def diagonal(z):
        copies = []
        x_part, y_part = parts_of(z)
        for s in range(1, fs):
            span = pl.ds(row_of(lax.rem(at.f + s, fs), 1 - at.hi), 2 * per)
            for part, sends, receives, device in (
                (y_part, r.dy_send, r.dy_recv, at.ypeer()), (x_part, r.dx_send, r.dx_recv, at.xpeer(s)),
            ):
                copies.append(
                    rcopy(
                        r.d3s.at[z, span, part], r.r1o.at[z, s - 1, :, part],
                        sends.at[z, s], receives.at[z, s], device,
                    )
                )
        return copies

    def row_of(f, hi):
        return pl.multiple_of((f * 2 + hi) * 2 * per, 2 * per)

    def delta_tile(n, carry):
        span = pl.ds(pl.multiple_of(n * step, step), step)
        delta = (r.gs[span, :].astype(f32) * mod(5)).astype(bf16)
        r.dds[span, :] = delta
        return carry + jnp.sum(delta.astype(f32).reshape(step // 8, 8, features), axis=0)

    r.dbs[...] = lax.fori_loop(0, tokens // step, delta_tile, jnp.zeros((8, features), f32))
    save(r.dbs, r.db)
    save(r.dds, r.dd)
    settle(n2t)
    transpose(r.dds)
    for z in range(ts):

        def grad_tile(m, carry):
            span = pl.ds(pl.multiple_of(m * 256, 256), 256)
            r.d3s[z, span, :] = nn(r.xt[span, :], r.hs[z]).astype(bf16)
            return carry

        lax.fori_loop(0, features // 256, grad_tile, 0)
        save(r.d3s.at[z], r.d3.at[z])
        for copy in diagonal(z):
            copy.start()

    def down_part(c, first):
        cols = slice(c * CHUNK, (c + 1) * CHUNK)
        for n in range(2):
            span = slice(n * half, (n + 1) * half)
            for m in range(2):
                rows = slice(m * 512, (m + 1) * 512)
                acc = nt(r.hs[0, span, cols], r.w3s[0, rows, cols])
                for z in range(1, ts):
                    acc = acc + nt(r.hs[z, span, cols], r.w3s[z, rows, cols])
                if first:
                    r.acc[span, rows] = acc
                else:
                    r.sendbuf[span, rows] = (r.acc[span, rows] + acc).astype(bf16)
            if not first:
                pair(1, n).start()

    fwd_wait(6)
    down_part(0, True)
    fwd_wait(7)
    tail_step(3)
    save(r.w3s, r.w3)
    down_part(1, False)
    for n in range(2):
        pair(1, n).wait()

        def tile(i, carry):
            span = pl.ds(pl.multiple_of(n * half + i * step, step), step)
            branch = r.sendbuf[span, :].astype(f32) + r.recvs[1, span, :].astype(f32) + mod(7)
            r.bos[span, :] = (r.mid[span, :].astype(f32) + mod(5) * branch).astype(bf16)
            product = r.gs[span, :].astype(f32) * branch
            return carry + jnp.sum(product.reshape(step // 8, 8, features), axis=0)

        part = lax.fori_loop(0, half // step, tile, jnp.zeros((8, features), f32))
        if n == 0:
            r.gates[...] = part
        else:
            r.gates[...] += part
    for src, out in ((r.bos, r.bo), (r.gates, r.gate2), (r.mods, r.mod), (r.psum, r.par)):
        save(src, out)
    for z in range(ts):
        for copy in diagonal(z):
            copy.wait()
    for n in range(2, last):
        z_sent(n)
    for d in range(ts - 1):
        for up in (True, False):
            tail_hop(d, up, "sent")
    for n in range(len(saved)):
        settle(n)


def run_forward(fs, cs, ts, sent, padded, per, every, args):
    tokens, features = cs * padded, ts * 256
    sds = jax.ShapeDtypeStruct
    big = (ts, features, GC)
    outs = {
        "w1": (big, bf16), "w2": (big, bf16), "w3": (big, bf16),
        "x": ((tokens, features), bf16), "g": ((tokens, features), bf16), "normed1": ((tokens, features), bf16),
        "qpre": ((ts, tokens, 128), f32), "kpre": ((ts, tokens, 128), f32),
        "v": ((ts, tokens, 128), bf16), "qh": ((ts, tokens, 128), bf16), "kh": ((ts, tokens, 128), bf16),
        "att": ((ts, tokens, 128), bf16), "branch1": ((tokens, features), bf16),
        "middle": ((tokens, features), bf16), "normed2": ((tokens, features), bf16),
        "hpre": ((ts, tokens, GC), f32), "hid": ((ts, tokens, GC), bf16), "bo": ((tokens, features), bf16),
        "lse": ((ts, 2, tokens), f32), "top": ((ts, 2, 128), f32), "mod": ((8, features), f32),
        "par": ((ts, 32, 128), f32), "gate2": ((8, features), f32),
        "dd": ((tokens, features), bf16), "d3": (big, bf16), "n1t": ((features, tokens), bf16),
        "n2t": ((features, tokens), bf16), "db": ((8, features), f32), "condr": ((every, per), f32),
        "r1o": ((ts, max(fs - 1, 1), 2 * per, GC), bf16),
    }
    vm, dma = pltpu.VMEM, pltpu.SemaphoreType.DMA
    local = dict(
        w1s="w1", w2s="w2", w3s="w3", xs="x", gs="g", n1="normed1", qp="qpre", kp="kpre", vs="v", qhs="qh",
        khs="kh", atts="att", b1="branch1", mid="middle", n2="normed2", hp="hpre", hs="hid", bos="bo",
        lses="lse", tops="top", mods="mod", psum="par", gates="gate2",
        dds="dd", d3s="d3", xt="n1t", dbs="db", crow="condr",
    )
    scratch = {k: vm(*outs[v]) for k, v in local.items()}
    items = 9
    scratch.update(
        sendbuf=vm((tokens, features), bf16), recvs=vm((2, tokens, features), bf16), acc=vm((tokens, features), f32),
        cond_slots=vm((ts, every, per), f32), part=vm((every, 8, 256), f32),
        msg=vm((fs * cs * ts, 8, 256), f32), parts=vm((ts, fs * cs * 32, 128), bf16),
        x_send=dma((2 * ts,)), x_recv=dma((2 * ts,)), g_send=dma((2 * ts,)), g_recv=dma((2 * ts,)), loc=dma((3,)),
        sib_send=dma((2,)), sib_recv=dma((2,)), gsib_send=dma((2,)), gsib_recv=dma((2,)),
        c_send=dma((ts,)), c_recv=dma((ts,)), m_send=dma((fs * cs * ts,)), m_recv=dma((fs * cs * ts,)),
        core_send=dma((items, 2)), core_recv=dma((items, 2)), core_loc=dma((items, 2)),
        z_send=dma((2, items, ts)), z_recv=dma((2, items, ts)), zd_send=dma((2, ts)), zd_recv=dma((2, ts)),
        dy_send=dma((ts, fs)), dy_recv=dma((ts, fs)), dx_send=dma((ts, fs)), dx_recv=dma((ts, fs)),
        wot=vm((per, 256), bf16), wdt=vm((per, ts * 256), bf16),
        wide=vm((*args["xb"].shape[:2], 128), f32),
        xs_send=dma((items, fs)), xs_recv=dma((items, fs)), ys_send=dma((items,)), ys_recv=dma((items,)),
        fx_send=dma((items, fs)), fx_recv=dma((items, fs)), fy_send=dma((items, fs)), fy_recv=dma((items, fs)),
        e_send=dma((2, 2)), e_recv=dma((2, 2)), out_sem=dma((len(outs) + ts,)),
    )
    anywhere, on_chip = pl.BlockSpec(memory_space=pl.ANY), pl.BlockSpec(memory_space=vm)
    results = pl.pallas_call(
        functools.partial(
            forward_kernel, fs, cs, ts, sent, padded, per, FORWARD_IN + FORWARD_OUT + tuple(scratch)
        ),
        name="forward",
        out_shape=tuple(sds(*outs[k]) for k in FORWARD_OUT),
        in_specs=[on_chip] * 2 + [anywhere] * 4 + [on_chip] * 2 + [anywhere] + [on_chip] * 4,
        out_specs=(anywhere,) * len(FORWARD_OUT),
        scratch_shapes=list(scratch.values()),
        compiler_params=pltpu.CompilerParams(
            collective_id=0, has_side_effects=True, vmem_limit_bytes=62 << 20
        ),
    )(*[args[k] for k in FORWARD_IN])
    return bundle(FORWARD_OUT, results)


def attend_back(z, r, query_gain, key_gain):
    tokens = r.vs.shape[1]
    qt = 256
    r.dka[...] = jnp.zeros_like(r.dka)
    r.dva[...] = jnp.zeros_like(r.dva)
    k_t = r.khs[z].T

    def tile(n, carry):
        span = pl.ds(pl.multiple_of(n * qt, qt), qt)
        allowed = r.idk[...] <= r.idq[:, span]
        outs = []
        for h in range(2):
            lanes = slice(h * HD, (h + 1) * HD)
            qh, da = r.qhs[z, span, lanes] * 0.125, r.das[z, span, lanes]
            s = jnp.where(allowed, nt(r.khs[z, :, lanes], qh), masked_score)
            p = jnp.exp(s - r.lses[z, h : h + 1, span])
            dp = nt(r.vs[z, :, lanes], da)
            centre = jnp.sum(p * dp, axis=0, keepdims=True)
            ds = (p * (dp - centre)).astype(bf16)
            r.dva[h] += nn(p.astype(bf16), da)
            r.dka[h] += nn(ds, qh)
            outs.append(nn(k_t[h * HD : (h + 1) * HD, :], ds))
        r.dqa[span, :] = jnp.concatenate(outs, axis=0).T * 0.125
        return carry

    lax.fori_loop(0, tokens // qt, tile, 0)

    def finish(n, sums):
        span = pl.ds(pl.multiple_of(n * qt, qt), qt)
        dk = jnp.concatenate([r.dka[0, span, :], r.dka[1, span, :]], axis=1)
        dv = jnp.concatenate([r.dva[0, span, :], r.dva[1, span, :]], axis=1).astype(bf16)
        r.dqkv[z, span, 256:] = dv
        results = [None, None, None, jnp.sum(dv.astype(f32), axis=0, keepdims=True)]
        for i, (raw_ref, gain, delta) in enumerate(((r.qp, query_gain, r.dqa[span, :]), (r.kp, key_gain, dk))):
            raw = raw_ref[z % 2, span, :]
            inverse = head_inverse(raw)
            results[i] = jnp.sum(delta * raw * inverse, axis=0, keepdims=True)
            t = delta * gain
            out = (inverse * t - raw * (inverse * inverse * inverse) * segment_mean(t * raw)).astype(bf16)
            r.dqkv[z, span, i * 128 : (i + 1) * 128] = out
            if i == 0:
                results[2] = jnp.sum(out.astype(f32), axis=0, keepdims=True)
        return [a + b for a, b in zip(sums, results)]

    sums = lax.fori_loop(0, tokens // qt, finish, [jnp.zeros((1, 128), f32)] * 4)
    for row, value in enumerate((sums[2], sums[3], sums[0], sums[1])):
        r.vec[z, row : row + 1, :] = value


BACKWARD_IN = (
    "w1", "w2", "w3", "x", "g", "qpre", "kpre", "v", "qh", "kh", "att", "branch1",
    "middle", "n2t", "hpre", "hid", "bo", "lse", "top", "mod", "par", "gate2", "dd", "d3", "n1t", "db", "r1o",
    "idq", "idk", "wm",
)
BACKWARD_OUT = ("o1", "o2", "o3", "dxo", "boo", "maila", "mailb", "sdel", "suma", "sumb")


def backward_kernel(fs, cs, ts, sent, padded, per, keys, *values):
    r = bundle(keys, values)
    assert ts == 4
    at = Place(fs, cs, ts)
    width = 256
    tokens, features = r.gs.shape
    half = tokens // 2
    step = 64
    at.barrier()

    pending = {}
    order = []

    def load(name, src, dst):
        pltpu.make_async_copy(src, dst, r.in_sem.at[len(order)]).start()
        pending[name] = (src, dst, len(order))
        order.append(name)

    def need(*wanted):
        for name in wanted:
            src, dst, n = pending.pop(name)
            pltpu.make_async_copy(src, dst, r.in_sem.at[n]).wait()

    def load_chunk(z):
        load("d3%d" % z, r.d3.at[z], r.d.at[z])
        load("r1%d" % z, r.r1o.at[z], r.r1.at[2 * ts + z])

    load_chunk(0)
    load_chunk(1)
    load("dd", r.dd, r.dds)
    load("w3", r.w3, r.wa)
    load("hp0", r.hpre.at[0], r.hp.at[0])

    def load_rest():
        load("n2t", r.n2t, r.xt)
        load("hp1", r.hpre.at[1], r.hp.at[1])
        load_chunk(2)
        load_chunk(3)
        load("w2", r.w2, r.wb)
        load_more()

    def load_more():
        load("mod", r.mod, r.mods)
        load("g", r.g, r.gs)
        load("mid", r.middle, r.mid)
        load("b1", r.branch1, r.b1)
        load("att", r.att, r.atts)
        load("par", r.par.at[:, pl.ds(16, 8), :], r.psum)
        for name, src, dst in (
            ("qh", r.qh, r.qhs), ("kh", r.kh, r.khs), ("v", r.v, r.vs), ("lse", r.lse, r.lses),
            ("top", r.top, r.tops), ("gate2", r.gate2, r.gates),
            ("db", r.db, r.dbs),
        ):
            load(name, src, dst)
        load_raw(0)
        load_raw(1)

    def load_raw(z):
        load("qp%d" % z, r.qpre.at[z], r.qp.at[z % 2])
        load("kp%d" % z, r.kpre.at[z], r.kp.at[z % 2])

    def block_of(ref):
        def src(i):
            c = (i // ts) * 2 + at.k
            return ref.at[
                pl.ds(pl.multiple_of(c * padded, padded), sent),
                pl.ds(pl.multiple_of(lax.rem(i, ts) * width, width), width),
            ]

        return src

    bo_start, bo_wait = exchange_images(
        at, block_of(r.bo), lambda i: r.boo.at[i], r.bo_send, r.bo_recv, r.loc.at[1]
    )
    dx_start, dx_wait = exchange_images(
        at, block_of(r.dds), lambda i: r.dxo.at[i], r.dx_send, r.dx_recv, r.loc.at[0]
    )
    outs = (r.o1, r.o2, r.o3)

    def slot(g, z):
        return z + (ts if g == 1 else 0)

    def rows(f, hi):
        return pl.ds(pl.multiple_of((f * 2 + hi) * 2 * per, 2 * per), 2 * per)

    def far(s):
        return lax.rem(at.f + s, fs)

    def stage_one(g, z, s):
        n, d = g * ts + z, slot(g, z)
        x_part, y_part = parts_of(z)
        return (
            rcopy(
                r.d.at[d, rows(far(s), 1 - at.hi), y_part], r.r1.at[n, s - 1, :, y_part],
                r.y1_send.at[n, s], r.y1_recv.at[n, s], at.ypeer(),
            ),
            rcopy(
                r.d.at[d, rows(far(s), 1 - at.hi), x_part], r.r1.at[n, s - 1, :, x_part],
                r.x1_send.at[n, s], r.x1_recv.at[n, s], at.xpeer(s),
            ),
        )

    def stage_two(g, z):
        n, d = g * ts + z, slot(g, z)
        copies = [
            rcopy(
                r.d.at[d, rows(far(s), at.hi), :], r.rx2.at[n, s - 1],
                r.x2_send.at[n, s], r.x2_recv.at[n, s], at.xpeer(s),
            )
            for s in range(1, fs)
        ]
        copies.append(
            rcopy(r.d.at[d, rows(at.f, 1 - at.hi), :], r.ry2.at[n], r.y2_send.at[n], r.y2_recv.at[n], at.ypeer())
        )
        return copies

    def rs_a(g, z):
        for s in range(1, fs):
            for copy in stage_one(g, z, s):
                copy.start()

    def rs_b(g, z):
        n, d = g * ts + z, slot(g, z)
        x_part, y_part = parts_of(z)
        for s in range(1, fs) if g < 2 else ():
            for copy in stage_one(g, z, s):
                copy.wait()
        for s in range(1, fs):
            span = rows(far(s), at.hi)
            r.d[d, span, y_part] = (r.d[d, span, y_part].astype(f32) + r.r1[n, s - 1, :, y_part].astype(f32)).astype(bf16)
        span = rows(at.f, 1 - at.hi)
        value = r.d[d, span, x_part].astype(f32)
        for s in range(1, fs):
            value = value + r.r1[n, s - 1, :, x_part].astype(f32)
        r.d[d, span, x_part] = value.astype(bf16)
        for copy in stage_two(g, z):
            copy.start()

    def roles(z):
        low = z < ts // 2
        near = z + 1 if z % 2 == 0 else z - 1
        relay, feeder = (ts // 2, ts - 1) if low else (ts // 2 - 1, 0)
        return near, relay, feeder

    def z_copy(g, z, role):
        n = g * ts + z
        near, relay, feeder = roles(z)
        if role == "near":
            return rcopy(r.ry2.at[n], r.rz.at[g, 0], r.z_send.at[n], r.z_recv.at[g, 0], (at.f, at.c, z))
        if role == "relay":
            return rcopy(r.ry2.at[n], r.rz.at[g, 1], r.z_send.at[n], r.z_recv.at[g, 1], (at.f, at.c, z))
        return rcopy(r.ry2.at[n], r.feed.at[g, z % 2], r.z_send.at[n], r.f_recv.at[g, z % 2], (at.f, at.c, relay))

    def rs_c(g, z):
        n, d = g * ts + z, slot(g, z)
        for copy in stage_two(g, z):
            copy.wait()
        span = rows(at.f, at.hi)
        for part in (slice(0, GC // 2), slice(GC // 2, GC)):
            value = r.d[d, span, part].astype(f32) + r.ry2[n, :, part].astype(f32)
            for s in range(1, fs):
                value = value + r.rx2[n, s - 1, :, part].astype(f32)
            r.ry2[n, :, part] = value.astype(bf16)

        near, relay, feeder = roles(z)

        @pl.when(at.t == near)
        def _():
            z_copy(g, z, "near").start()

        @pl.when(at.t == feeder)
        def _():
            z_copy(g, z, "feeder").start()

    def rs_d(g, z):
        n = g * ts + z

        @pl.when(at.t == roles(z)[1])
        def _():
            z_copy(g, z, "feeder").wait_recv()
            for part in (slice(0, GC // 2), slice(GC // 2, GC)):
                value = r.ry2[n, :, part].astype(f32) + r.feed[g, z % 2, :, part].astype(f32)
                r.ry2[n, :, part] = value.astype(bf16)
            z_copy(g, z, "relay").start()

    def pair_sum(g):
        src = r.total.at[pl.ds(pl.multiple_of((1 - at.k) * per, per), per)]
        own = r.total.at[pl.ds(pl.multiple_of(at.k * per, per), per)]
        keep = pltpu.make_async_copy(own, outs[g].at[at.k], r.k_loc.at[g])
        out = functools.partial(rcopy, src, outs[g].at[at.k], r.k_send.at[g], r.k_recv.at[g], at.sibling())
        inn = functools.partial(rcopy, src, outs[g].at[1 - at.k], r.k_send.at[g], r.k_recv.at[g], at.sibling())
        return keep, out, inn

    def pair_wait(g):
        keep, _, inn = pair_sum(g)
        keep.wait()
        inn().wait()

    def rs_e(g):
        for z in range(ts):

            @pl.when(at.t != z)
            def _():
                z_copy(g, z, "near").wait_send()

        for n in range(2):
            rcopy(
                r.rz.at[g, n], r.rz.at[g, n], r.z_send.at[g * ts], r.z_recv.at[g, n], at.zpeer(1)
            ).wait_recv()
        for part in (slice(0, GC // 2), slice(GC // 2, GC)):
            value = r.ry2[g * ts + at.t, :, part].astype(f32)
            for n in range(2):
                value = value + r.rz[g, n, :, part].astype(f32)
            r.total[:, part] = value
        keep, out, _ = pair_sum(g)
        keep.start()
        out().start()

    def mod(j):
        return r.mods[j : j + 1, :]

    def own_row(z, start):
        return r.psum[z, pl.ds(start + at.k, 1), :]

    def transpose(src):
        def tile(n, carry):
            span = pl.ds(pl.multiple_of(n * 128, 128), 128)
            r.xt[:, span] = src[span, :].T
            return carry

        lax.fori_loop(0, tokens // 128, tile, 0)

    def grad_into(d, cols, right):
        def tile(m, carry):
            span = pl.ds(pl.multiple_of(m * 256, 256), 256)
            r.d[d, span, cols] = nn(r.xt[span, :], right()).astype(bf16)
            return carry

        lax.fori_loop(0, features // 256, tile, 0)

    def eight(values):
        return jnp.sum(values.reshape(values.shape[0] // 8, 8, values.shape[1]), axis=0)

    def collapse(values):
        return jnp.sum(values, axis=0, keepdims=True)

    def pair(e, n):
        span = pl.ds(n * half, half)
        return rcopy(
            r.sendbuf.at[span, :], r.recvs.at[e, span, :], r.e_send.at[e, n], r.e_recv.at[e, n], at.sibling()
        )

    zeros = jnp.zeros((8, features), f32)

    def back_up(z):
        need("hp%d" % z)

        def tile(n, carry):
            span = pl.ds(pl.multiple_of(n * half, half), half)
            hidden_delta = nn(r.dds[span, :], r.wa[z])
            pre = r.hp[z % 2, span, :]
            inner = jnp.tanh(gelu_a * (pre + gelu_b * pre * pre * pre))
            slope = 0.5 * (1.0 + inner) + 0.5 * pre * (1.0 - inner * inner) * (
                gelu_a * (1.0 + 3.0 * gelu_b * pre * pre)
            )
            delta = (hidden_delta * slope).astype(bf16)
            r.hs[z, span, :] = delta
            return carry + eight(delta.astype(f32))

        r.ubs[z] = collapse(lax.fori_loop(0, 2, tile, jnp.zeros((8, GC), f32)))
        if z + 2 < ts:
            load("hp%d" % (z + 2), r.hpre.at[z + 2], r.hp.at[z % 2])

    def grad_up(z):
        grad_into(slot(1, z), slice(None), lambda: r.hs[z])

    need("d30", "d31", "r10", "r11")
    rs_b(2, 0)
    rs_b(2, 1)
    bo_start()
    load_rest()
    need("dd", "w3")
    back_up(0)
    need("n2t", "d32", "d33", "r12", "r13")
    grad_up(0)
    rs_a(1, 0)
    rs_b(2, 2)
    back_up(1)
    grad_up(1)
    rs_b(2, 3)
    back_up(2)
    grad_up(2)
    rs_a(1, 1)
    rs_c(2, 0)
    back_up(3)
    load("w1", r.w1, r.wa)
    rs_c(2, 1)
    rs_d(2, 0)
    grad_up(3)
    need("w2")
    for n in range(2):
        span = slice(n * half, (n + 1) * half)
        for m in range(2):
            cols = slice(m * 512, (m + 1) * 512)
            acc = nt(r.hs[0, span, :], r.wb[0, cols, :])
            for z in range(1, ts):
                acc = acc + nt(r.hs[z, span, :], r.wb[z, cols, :])
            r.sendbuf[span, cols] = acc.astype(bf16)
        pair(0, n).start()
    rs_b(1, 0)
    rs_a(1, 2)
    rs_c(2, 2)
    rs_d(2, 1)
    need("mid", "b1", "mod", "g")

    def norm_two(n):
        def tile(i, sums):
            span = pl.ds(pl.multiple_of(n * half + i * step, step), step)
            incoming = r.sendbuf[span, :].astype(f32) + r.recvs[0, span, :].astype(f32)
            normal, inverse = normalize(r.mid[span, :].astype(f32))
            e = incoming * (1.0 + mod(4))
            mean_e = jnp.mean(e, axis=-1, keepdims=True)
            mean_en = jnp.mean(e * normal, axis=-1, keepdims=True)
            delta = r.gs[span, :].astype(f32) + (e - mean_e - normal * mean_en) * inverse
            r.hp[0, span, :] = delta[:, :512]
            r.hp[1, span, :] = delta[:, 512:]
            low = (delta * mod(2)).astype(bf16)
            r.dds[span, :] = low
            parts = (incoming, incoming * normal, delta * r.b1[span, :].astype(f32), low.astype(f32))
            return [a + eight(b) for a, b in zip(sums, parts)]

        return tile

    sums = [zeros] * 4
    for n in range(2):
        pair(0, n).wait()
        sums = lax.fori_loop(0, half // step, norm_two(n), sums)
    shift_two, scale_two, gate_one, output_bias = (collapse(v) for v in sums)
    load("x", r.x, r.gs)
    rs_c(2, 3)
    rs_d(2, 2)

    transpose(r.dds)
    need("att", "w1")
    for z in range(0, ts, 2):
        if z == 2:
            rs_b(1, 1)
            rs_a(1, 3)
            rs_d(2, 3)

        def grad_pair(m, carry):
            span = pl.ds(pl.multiple_of(m * 256, 256), 256)
            both = nn(r.xt[span, :], jnp.concatenate([r.atts[z], r.atts[z + 1]], axis=1)).astype(bf16)
            r.d[slot(0, z), span, 384:] = both[:, :128]
            r.d[slot(0, z + 1), span, 384:] = both[:, 128:]
            return carry

        lax.fori_loop(0, features // 256, grad_pair, 0)

        def tile(n, carry):
            span = pl.ds(pl.multiple_of(n * half, half), half)
            weight = jnp.concatenate([r.wa[z, :, 384:], r.wa[z + 1, :, 384:]], axis=1)
            both = nn(r.dds[span, :], weight).astype(bf16)
            r.das[z, span, :] = both[:, :128]
            r.das[z + 1, span, :] = both[:, 128:]
            return carry

        lax.fori_loop(0, 2, tile, 0)
    load("n1t", r.n1t, r.xt)
    need("par", "qh", "kh", "v", "lse", "top", "gate2", "db")
    for z in range(ts):
        need("qp%d" % z, "kp%d" % z)
        attend_back(z, r, own_row(z, 0), own_row(z, 2))
        if z + 2 < ts:
            load_raw(z + 2)
        if z == 0:
            need("n1t")
        grad_into(slot(0, z), slice(0, 384), lambda: r.dqkv[z])
        rs_a(0, z)
        if z == 0:
            rs_c(1, 0)
            rs_b(1, 2)
            rs_c(1, 1)
            rs_d(1, 0)
            rs_b(1, 3)
        if z == 1:
            rs_c(1, 2)
            rs_d(1, 1)
            rs_b(0, 0)
        if z == 2:
            rs_c(1, 3)
            rs_d(1, 2)
            rs_b(0, 1)
        if z == 3:
            rs_c(0, 0)
            rs_d(1, 3)
            rs_b(0, 2)

    for n in range(2):
        span = slice(n * half, (n + 1) * half)
        for m in range(2):
            cols = slice(m * 512, (m + 1) * 512)
            acc = nt(r.dqkv[0, span, :], r.wa[0, cols, :384])
            for z in range(1, ts):
                acc = acc + nt(r.dqkv[z, span, :], r.wa[z, cols, :384])
            r.sendbuf[span, cols] = acc.astype(bf16)
        pair(1, n).start()
    gate_two, down_bias = collapse(r.gates[...]), collapse(r.dbs[...])
    firsts = ((gate_one, shift_two, scale_two), (gate_two, output_bias, down_bias))
    for z in range(ts):
        lanes = slice(z * width, (z + 1) * width)
        for row in range(3):
            r.early[z, row : row + 1, :] = jnp.where(at.k == 0, firsts[0][row][:, lanes], firsts[1][row][:, lanes])
        for row in range(2):
            r.early[z, 3 + row : 4 + row, :128] = r.vec[z, 2 * row : 2 * row + 1, :]
            r.early[z, 3 + row : 4 + row, 128:] = r.vec[z, 2 * row + 1 : 2 * row + 2, :]
            r.early[z, 5 + row : 6 + row, :] = r.ubs[z, :, row * width : (row + 1) * width]
            r.early[z, 7:8, row * 128 : (row + 1) * 128] = r.tops[z, row : row + 1, :]

    def mail_slot(box):
        def slot_of(n):
            f, c, t = at.coords(n)
            return box.at[(f * 2 + c // 2) * ts + t, lax.rem(c, 2)]

        return slot_of

    def toward(box):
        return lambda n: box.at[lax.rem(n, ts)]

    m_start, m_wait = broadcast_messages(
        at, toward(r.early), mail_slot(r.mail_a), r.m_send, r.m_recv, r.loc.at[2]
    )
    l_start, l_wait = broadcast_messages(
        at, toward(r.late), mail_slot(r.mail_b), r.l_send, r.l_recv, r.loc.at[3]
    )
    m_start()
    rs_c(0, 1)
    rs_d(0, 0)
    need("x")

    def norm_one(n):
        def tile(i, sums):
            span = pl.ds(pl.multiple_of(n * half + i * step, step), step)
            incoming = r.sendbuf[span, :].astype(f32) + r.recvs[1, span, :].astype(f32)
            normal, inverse = normalize(r.gs[span, :].astype(f32))
            e = incoming * (1.0 + mod(1))
            mean_e = jnp.mean(e, axis=-1, keepdims=True)
            mean_en = jnp.mean(e * normal, axis=-1, keepdims=True)
            middle_delta = jnp.concatenate([r.hp[0, span, :], r.hp[1, span, :]], axis=1)
            r.dds[span, :] = (middle_delta + (e - mean_e - normal * mean_en) * inverse).astype(bf16)
            return [a + eight(b) for a, b in zip(sums, (incoming, incoming * normal))]

        return tile

    sums = [zeros] * 2
    for n in range(2):
        pair(1, n).wait()
        sums = lax.fori_loop(0, half // step, norm_one(n), sums)
    shift_one, scale_one = (collapse(v) for v in sums)
    for z in range(ts):
        lanes = slice(z * width, (z + 1) * width)
        r.late[z] = jnp.where(at.k == 0, shift_one[:, lanes], scale_one[:, lanes])
    l_start()
    dx_start()
    rs_b(0, 3)
    rs_e(2)
    rs_c(0, 2)
    rs_c(0, 3)
    rs_d(0, 1)
    rs_d(0, 2)
    pair_wait(2)
    rs_e(1)
    rs_d(0, 3)
    m_wait()

    l_wait()
    partial = jnp.zeros(r.silus.shape[1:], f32)
    six = [(r.mail_b, 0, 0), (r.mail_b, 1, 0), (r.mail_a, 0, 0), (r.mail_a, 0, 1), (r.mail_a, 0, 2), (r.mail_a, 1, 0)]
    for j, (box, side, row) in enumerate(six):
        value = box[:, side, row, :]
        for _ in range(3):
            low = value.astype(bf16)
            partial = partial + nt(low, r.wm[j])
            value = value - low.astype(f32)
    r.silus[at.t] = partial

    def silu_copy(s, index):
        return rcopy(r.silus.at[at.t], r.silus.at[index], r.s_send.at[s], r.s_recv.at[s], at.zpeer(s))

    for s in range(1, ts):
        silu_copy(s, at.t).start()
    def over_images(n, carry):
        plain, high, few = carry
        return plain + r.mail_a[n], jnp.maximum(high, r.mail_a[n]), few + r.mail_b[n]

    plain, high, few = lax.fori_loop(1, r.mail_a.shape[0], over_images, (r.mail_a[0], r.mail_a[0], r.mail_b[0]))
    row = lax.broadcasted_iota(jnp.int32, plain.shape, 1)
    r.sum_a[...] = jnp.where(row == 7, high, plain)
    r.sum_b[...] = few
    stores = [
        (r.mail_a, r.maila, 0), (r.mail_b, r.mailb, 1), (r.silus.at[at.t], r.sdel, 2), (r.sum_a, r.suma, 3), (r.sum_b, r.sumb, 4),
    ]
    for src, dst, n in stores[:2] + stores[3:]:
        pltpu.make_async_copy(src, dst, r.out_sem.at[n]).start()
    bo_wait()
    pair_wait(1)
    for s in range(1, ts):
        silu_copy(s, at.zfrom(s)).wait()
    total = r.silus[0]
    for z in range(1, ts):
        total = total + r.silus[z]
    r.silus[at.t] = total
    pltpu.make_async_copy(r.silus.at[at.t], r.sdel, r.out_sem.at[2]).start()
    rs_e(0)
    dx_wait()
    for src, dst, n in stores:
        pltpu.make_async_copy(src, dst, r.out_sem.at[n]).wait()
    pair_wait(0)


def run_backward(fs, cs, ts, sent, padded, per, every, args):
    tokens, features = cs * padded, ts * 256
    f1 = max(fs - 1, 1)
    chunks = 3 * ts
    vm, dma, sds = pltpu.VMEM, pltpu.SemaphoreType.DMA, jax.ShapeDtypeStruct
    rows, cube = (tokens, features), (ts, tokens, 128)
    scratch = dict(
        gs=vm(rows, bf16), hs=vm((ts, tokens, GC), bf16), hp=vm((2, tokens, GC), f32),
        wa=vm((ts, features, GC), bf16), wb=vm((ts, features, GC), bf16),
        mid=vm(rows, bf16), dbs=vm((8, features), f32), b1=vm(rows, bf16), atts=vm(cube, bf16),
        qhs=vm(cube, bf16), khs=vm(cube, bf16), vs=vm(cube, bf16), lses=vm((ts, 2, tokens), f32),
        qp=vm((2, tokens, 128), f32), kp=vm((2, tokens, 128), f32), tops=vm((ts, 2, 128), f32), gates=vm((8, features), f32),
        mods=vm((8, features), f32), psum=vm((ts, 8, 128), f32),
        dds=vm(rows, bf16), xt=vm((features, tokens), bf16), sendbuf=vm(rows, bf16), recvs=vm((2, *rows), bf16),
        das=vm(cube, bf16), dqkv=vm((ts, tokens, 384), bf16), vec=vm((ts, 4, 128), f32), ubs=vm((ts, 1, GC), f32),
        dqa=vm((tokens, 128), f32), dka=vm((2, tokens, HD), f32), dva=vm((2, tokens, HD), f32),
        early=vm((ts, 8, 256), f32), late=vm((ts, 1, 256), f32),
        mail_a=vm((every, 2, 8, 256), f32), mail_b=vm((every, 2, 1, 256), f32),
        silus=vm((ts, every, per), f32),
        d=vm((2 * ts, features, GC), bf16),
        r1=vm((chunks, f1, 2 * per, GC), bf16),
        rx2=vm((chunks, f1, 2 * per, GC), bf16), ry2=vm((chunks, 2 * per, GC), bf16),
        rz=vm((3, 2, 2 * per, GC), bf16), feed=vm((3, 2, 2 * per, GC), bf16), total=vm((2 * per, GC), f32),
        in_sem=dma((48,)), loc=dma((4,)), out_sem=dma((5,)),
        sum_a=vm((2, 8, 256), f32), sum_b=vm((2, 1, 256), f32),
        l_send=dma((fs * cs * ts,)), l_recv=dma((fs * cs * ts,)), s_send=dma((ts,)), s_recv=dma((ts,)),
        bo_send=dma((2 * ts,)), bo_recv=dma((2 * ts,)), dx_send=dma((2 * ts,)), dx_recv=dma((2 * ts,)),
        y1_send=dma((chunks, fs)), y1_recv=dma((chunks, fs)), x1_send=dma((chunks, fs)), x1_recv=dma((chunks, fs)),
        x2_send=dma((chunks, fs)), x2_recv=dma((chunks, fs)), y2_send=dma((chunks,)), y2_recv=dma((chunks,)),
        z_send=dma((chunks,)), z_recv=dma((3, 2)), f_recv=dma((3, 2)), k_send=dma((3,)), k_recv=dma((3,)), k_loc=dma((3,)),
        e_send=dma((2, 2)), e_recv=dma((2, 2)), m_send=dma((fs * cs * ts,)), m_recv=dma((fs * cs * ts,)),
    )
    anywhere, on_chip = pl.BlockSpec(memory_space=pl.ANY), pl.BlockSpec(memory_space=vm)
    share = sds((2, per, GC), f32)
    blocks = sds((2 * ts, sent, 256), bf16)
    results = pl.pallas_call(
        functools.partial(
            backward_kernel, fs, cs, ts, sent, padded, per, BACKWARD_IN + BACKWARD_OUT + tuple(scratch)
        ),
        name="backward",
        out_shape=(
            share, share, share, blocks, blocks, sds((every, 2, 8, 256), f32), sds((every, 2, 1, 256), f32),
            sds((every, per), f32), sds((2, 8, 256), f32), sds((2, 1, 256), f32),
        ),
        in_specs=[anywhere] * (len(BACKWARD_IN) - 3) + [on_chip] * 3,
        out_specs=(anywhere,) * 10,
        scratch_shapes=list(scratch.values()),
        compiler_params=pltpu.CompilerParams(
            collective_id=1, has_side_effects=True, vmem_limit_bytes=63 << 20
        ),
    )(*[args[k] for k in BACKWARD_IN])
    return bundle(BACKWARD_OUT, results)


FINISH_IN = (
    "one", "two", "three", "bo", "dx", "moda", "modb", "cond", "wq", "wk", "columns", "labels", "cdelta",
)
FINISH_OUT = ("block", "dinputs", "dq", "dk", "dv", "dout", "dup", "ddown", "dmod", "cq", "ck", "table")
FINISH_SCRATCH = ("ones", "twos", "threes", "bos", "dxs", "wide", "sem")


def finish_kernel(*values):
    r = bundle(FINISH_IN + FINISH_OUT + FINISH_SCRATCH, values)
    pairs = ((r.bo, r.bos), (r.dx, r.dxs), (r.one, r.ones), (r.two, r.twos), (r.three, r.threes))
    copies = [pltpu.make_async_copy(src, dst, r.sem.at[n]) for n, (src, dst) in enumerate(pairs)]
    for copy in copies:
        copy.start()
    rows, images, _ = r.block.shape
    cond = r.cond[...]
    silu = (cond / (1.0 + jnp.exp(-cond))).astype(bf16).astype(f32)
    left = silu.T.astype(bf16)
    six = [(r.modb, 0, 0), (r.modb, 1, 0), (r.moda, 0, 0), (r.moda, 0, 1), (r.moda, 0, 2), (r.moda, 1, 0)]
    for j, (box, side, row) in enumerate(six):
        value = box[:, side, row, :]
        total = jnp.zeros((left.shape[0], value.shape[1]), f32)
        for _ in range(3):
            low = value.astype(bf16)
            total = total + nn(left, low)
            value = value - low.astype(f32)
        r.dmod[j] = total
    every, classes = r.labels.shape[0], r.table.shape[1]
    chosen = (lax.broadcasted_iota(jnp.int32, (every, classes), 1) == r.labels[...]).astype(f32).astype(bf16)
    value = r.cdelta[...].T
    total = jnp.zeros((value.shape[0], classes), f32)
    for _ in range(3):
        low = value.astype(bf16)
        total = total + nn(low, chosen)
        value = value - low.astype(f32)
    r.table[...] = total
    r.cq[...] = r.wq[...].astype(f32) * r.columns[...]
    r.ck[...] = r.wk[...].astype(f32) * r.columns[...]
    copies[0].wait()
    for i in range(images):
        r.wide[:, i, :] = r.bos[i, :rows, :].astype(f32)
    r.block[...] = r.wide[...].astype(bf16)
    copies[1].wait()
    for i in range(images):
        r.dinputs[:, i, :] = r.dxs[i, :rows, :].astype(f32)
    for copy in copies[2:]:
        copy.wait()
    for h in range(2):
        here = slice(h * 128, (h + 1) * 128)
        r.dq[:, here] = r.ones[h, :, :128]
        r.dk[:, here] = r.ones[h, :, 128:256]
        r.dv[:, here] = r.ones[h, :, 256:384]
        r.dout[here, :] = r.ones[h, :, 384:].T
        half = slice(h * GC, (h + 1) * GC)
        r.dup[:, half] = r.twos[h]
        r.ddown[half, :] = r.threes[h].T


def on_device(
    fs, cs, ts,
    inputs, cotangent, labels, scale_ids, head_flags, class_table, modulate_weight, modulate_bias,
    query_weight, key_weight, value_weight, query_bias, value_bias, query_gain, key_gain,
    output_weight, output_bias, up_weight, up_bias, down_weight, down_bias,
):
    images, rows_here, width = inputs.shape
    if images != 2 * ts or cs != 4 or ts % 2 or width != 256:
        raise ValueError("unsupported mesh")
    length = scale_ids.shape[0]
    every = labels.shape[0]
    count = fs * cs * ts
    sent = -(-rows_here // 16) * 16
    padded = -(-rows_here // 64) * 64
    tokens = cs * padded
    features = ts * width
    per = query_weight.shape[0]
    part_cols = class_table.shape[1]
    f, c, t = (lax.axis_index(n) for n in ("fsdp", "ctx", "tp"))
    core = lax.rem(c, 2)
    block = f * cs + c

    classes = class_table.shape[0]
    onehot = (labels[:, None] == jnp.arange(classes, dtype=jnp.int32)[None, :]).astype(bf16)
    cond_part = jnp.dot(onehot, class_table, preferred_element_type=f32)
    cond_spread = lax.dynamic_update_slice(
        jnp.zeros((every, per), f32), cond_part, (0, t * part_cols)
    )

    lanes = modulate_bias.shape[2]
    small_parts = (
        modulate_bias.reshape(-1, lanes), query_bias, value_bias, query_gain, key_gain,
        output_bias, down_bias, up_bias,
    )
    total_rows, start, small_rows = sum(v.shape[0] for v in small_parts), 0, 0
    for part in small_parts:
        stop = start + part.shape[0]
        small_rows = small_rows + jnp.pad(part, ((start, total_rows - stop), (0, 0)))
        start = stop
    small = lax.dynamic_update_slice(
        jnp.zeros((small_rows.shape[0], HD), bf16), small_rows, (0, block * lanes)
    ).reshape(-1, 2 * HD)
    ids = scale_ids.reshape(cs, rows_here)
    spare = ((0, 0), (0, padded - rows_here))
    ids_query = jnp.pad(ids, spare, constant_values=-1).reshape(1, tokens)
    ids_key = jnp.pad(ids, spare, constant_values=1 << 20).reshape(tokens, 1)
    flat_modulate = modulate_weight.transpose(1, 0, 2)
    k = run_forward(
        fs, cs, ts, sent, padded, per, every,
        dict(
            xb=inputs.transpose(1, 0, 2), gb=cotangent.transpose(1, 0, 2),
            wq=query_weight, wk=key_weight, wv=value_weight, wu=up_weight, wo=output_weight, wd=down_weight,
            sp=small, cond=cond_spread,
            wm=flat_modulate, idq=ids_query, idk=ids_key,
        ),
    )
    m = run_backward(
        fs, cs, ts, sent, padded, per, every,
        {
            key: {"idq": ids_query, "idk": ids_key, "wm": flat_modulate}.get(key, getattr(k, key, None))
            for key in BACKWARD_IN
        },
    )
    heads = modulate_bias.shape[1]
    sum_one, sum_two, sum_three, dx_blocks, bo_blocks = m.o1, m.o2, m.o3, m.dxo, m.boo

    sums = m.suma
    same = jnp.concatenate([m.sumb.reshape(2, width), sums[0, :3], sums[1, :3]])
    halves_sum = sums[:, 3:7]

    def mine(values):
        return lax.dynamic_slice_in_dim(values, block * lanes, lanes, values.ndim - 1)

    same = mine(same.reshape(8, heads, HD))
    modulate_bias_grad, output_bias_grad, down_bias_grad = same[:6], same[6], same[7]
    quarter = mine(halves_sum[:, :2].reshape(2, 4, heads // 2, HD)).transpose(1, 0, 2, 3).reshape(4, heads, lanes)
    query_bias_grad, value_bias_grad, query_gain_grad, key_gain_grad = (quarter[j] for j in range(4))
    up_bias_grad = mine(halves_sum[:, 2:].reshape(-1, HD))
    head_max = sums[:, 7].reshape(heads, 128)[:, 0]

    silu_cols = lax.dynamic_slice_in_dim(m.sdel, t * part_cols, part_cols, 1)
    primal, silu_back = jax.vjp(jax.nn.silu, cond_part)
    cond_delta = silu_back(silu_cols)[0]

    factor = jnp.where(
        head_flags == 1,
        jnp.sqrt(clip_threshold / jnp.maximum(head_max, clip_threshold)),
        jnp.ones_like(head_max),
    )
    columns = jnp.repeat(factor, HD)
    square, flat_rows = (per, width), (rows_here, images, width)
    share = pltpu.VMEM((2, per, GC), f32)
    sent_rows = pltpu.VMEM((images, sent, width), bf16)
    (
        block_out, inputs_grad, query_weight_grad, key_weight_grad, value_weight_grad, output_weight_grad,
        up_weight_grad, down_weight_grad, modulate_weight_grad, clipped_query, clipped_key, class_table_grad,
    ) = pl.pallas_call(
        finish_kernel,
        name="finish",
        out_shape=(
            jax.ShapeDtypeStruct(flat_rows, bf16), jax.ShapeDtypeStruct(flat_rows, f32),
            jax.ShapeDtypeStruct(square, f32), jax.ShapeDtypeStruct(square, f32),
            jax.ShapeDtypeStruct(square, f32), jax.ShapeDtypeStruct((width, per), f32),
            jax.ShapeDtypeStruct(up_weight.shape, f32), jax.ShapeDtypeStruct(down_weight.shape, f32),
            jax.ShapeDtypeStruct((6, per, width), f32),
            jax.ShapeDtypeStruct(square, f32), jax.ShapeDtypeStruct(square, f32),
            jax.ShapeDtypeStruct((part_cols, classes), f32),
        ),
        in_specs=[pl.BlockSpec(memory_space=pl.ANY)] * 5 + [pl.BlockSpec(memory_space=pltpu.VMEM)] * 8,
        scratch_shapes=[
            share, share, share, sent_rows, sent_rows, pltpu.VMEM(flat_rows, f32), pltpu.SemaphoreType.DMA((5,)),
        ],
        compiler_params=pltpu.CompilerParams(vmem_limit_bytes=62 << 20),
    )(
        sum_one, sum_two, sum_three, bo_blocks, dx_blocks, m.maila, m.mailb, k.condr,
        query_weight, key_weight, columns[None, :], labels[:, None], cond_delta,
    )
    class_table_grad = class_table_grad.T
    block_out, inputs_grad = block_out.transpose(1, 0, 2), inputs_grad.transpose(1, 0, 2)
    modulate_weight_grad = modulate_weight_grad.transpose(1, 0, 2)
    clipped_query_bias = query_bias.astype(f32) * factor[:, None]
    return (
        block_out, inputs_grad, class_table_grad, modulate_weight_grad, modulate_bias_grad,
        query_weight_grad, key_weight_grad, value_weight_grad, query_bias_grad, value_bias_grad,
        query_gain_grad, key_gain_grad, output_weight_grad, output_bias_grad,
        up_weight_grad, up_bias_grad, down_weight_grad, down_bias_grad,
        clipped_query, clipped_key, clipped_query_bias,
    )


def solution(mesh):
    rows = P("fsdp", "ctx", "tp")
    table = P(None, ("fsdp", "ctx", "tp"))
    left = P(("fsdp", "ctx"), "tp")
    right = P("tp", ("fsdp", "ctx"))
    modulate = P(("fsdp", "ctx"), None, "tp")
    modulate_small = P(None, "tp", ("fsdp", "ctx"))
    return jax.shard_map(
        functools.partial(on_device, mesh.shape["fsdp"], mesh.shape["ctx"], mesh.shape["tp"]),
        mesh=mesh,
        in_specs=(
            rows, rows, P(), P(), P("tp"), table, modulate, modulate_small,
            left, left, left, right, right, right, right,
            right, right, left, right, right, right,
        ),
        out_specs=(
            rows, rows, table, modulate, modulate_small,
            left, left, left, right, right, right, right,
            right, right, left, right, right, right,
            left, left, right,
        ),
        check_vma=False,
    )
```
